32 devices in a mesh: tile: 8 (over z, x), depth: 4 (over y, core).
Axes of the slice: x: 2, y: 2, z: 4, core: 2. Of those that a mesh axis runs over, the one named last changes fastest.
Arguments:
- density: float32 [64, 128, 128], P('depth', 'tile'), may hold values from 0.5 to 2
- momentum: float32 [3, 64, 128, 128], P(None, 'depth', 'tile'), may hold values from -4 to 4
- magnetic: float32 [3, 64, 128, 128], P(None, 'depth', 'tile'), may hold values from -4 to 4
- energy: float32 [64, 128, 128], P('depth', 'tile'), may hold values from 2 to 4
- shifts: int32 [24], replicated, may hold values from 0 to 55, as said below
- levels: int32 [24], replicated, may hold values from 0 to 63, as said below
Outputs:
- new_state: float32 [8, 64, 128, 128], P(None, 'depth', 'tile')
- intensity: float32 [48, 128, 128], P(None, 'tile', 'depth')
The draws below stay inside these ranges and needn't reach their ends.
Inputs may be any that keep to these rules, and one draw needn't show every extreme that they name: shifts[k] = (1732 (levels[k] - levels[0]) + 1000) // 2000, the nearest whole column to tan(60 degrees) times the depth gap at half a column per level; the last is exactly 55. 24 distinct levels in ascending order, the first 0 and the last 63; each depth slab of 16 consecutive levels holds at most 8 of them, and some slab exactly 8.
All inputs are finite; a program needn't handle non-finite values.
Results may differ from the reference program's by a relative error of at most 0.000054.
Values sent between devices are 32-bit elements; how exact they have to be, the bound alone decides.
A program may use at most 64 MiB of HBM per device.

```python
import math
import jax
import jax.numpy as jnp
from jax import lax

CZ = 16
NY = 128
MOST = 8
W = 48
LEVELS = 64
X = 128
SYN = 24
N_DEPTH = 4


def pick_levels(key):
    total = CZ * N_DEPTH
    first_key, slab_key, second_key = jax.random.split(jax.random.fold_in(key, 7), 3)
    index = jnp.arange(total, dtype=jnp.int32)
    slab = index // CZ
    ends = (index == 0) | (index == total - 1)
    first = jax.random.permutation(first_key, total).astype(jnp.int32)
    first = jnp.where(ends, -1, first).astype(jnp.int32)
    same = slab[:, None] == slab[None, :]
    rank = jnp.sum(same & (first[None, :] < first[:, None]), axis=1)
    chosen = jax.random.randint(slab_key, (), 0, N_DEPTH)
    candidate = rank < MOST
    busy = slab == chosen
    others = candidate & jnp.logical_not(busy)
    second = jax.random.permutation(second_key, total).astype(jnp.int32)
    second = jnp.where(ends, -1, second).astype(jnp.int32)
    other_rank = jnp.sum(others[None, :] & (second[None, :] < second[:, None]), axis=1)
    picked = candidate & busy | others & (other_rank < SYN - MOST)
    return jnp.nonzero(picked, size=SYN)[0].astype(jnp.int32)


def draw_levels(key, part):
    return pick_levels(key)


def draw_shifts(key, part):
    chosen_levels = pick_levels(key)
    gap = chosen_levels - chosen_levels[0]
    return ((1732 * gap + 1000) // 2000).astype(jnp.int32)


def steps_of(own_key, shape, cuts, low, high):
    def one(dim, shards_of):
        draws = jax.random.uniform(jax.random.fold_in(jax.random.fold_in(own_key, 6), dim), (shards_of,), jnp.float32, low / len(cuts), high / len(cuts))
        return jnp.repeat(jnp.exp(draws), shape[dim] // shards_of).reshape((-1,) + (1,) * (len(shape) - dim - 1))

    level = one(*cuts[0])
    for cut in cuts[1:]:
        level = level * one(*cut)
    return level


def bell_draw(key, shape, spread, reach, cuts=(), kind=jnp.bfloat16):
    gain = steps_of(key, shape, cuts, -0.22, 0.18) if cuts else 1.0
    drawn = jax.random.normal(key, shape, jnp.float32) * spread * gain
    return jnp.minimum(jnp.maximum(drawn, -reach), reach).astype(kind)


def setup_inputs(seed: int = 0) -> dict:
    seeds = jax.random.split(jax.random.key(seed), 7)
    return {
        "density": jnp.clip(jnp.exp(math.log(2.0) - 1.3862944 * jax.random.uniform(seeds[0], (LEVELS, X, NY), jnp.float32) ** steps_of(seeds[0], (LEVELS, X, NY), ((0, 4), (1, 8)), -0.2, 0.2)), 0.5, 2.0),
        "momentum": bell_draw(seeds[1], (3, LEVELS, X, NY), 0.5, 4.0, ((1, 4), (2, 8)), jnp.float32),
        "magnetic": bell_draw(seeds[2], (3, LEVELS, X, NY), 0.5, 4.0, ((1, 4), (2, 8)), jnp.float32),
        "energy": jnp.clip(2.0 + 2.0 * jax.random.uniform(seeds[3], (LEVELS, X, NY), jnp.float32) ** steps_of(seeds[3], (LEVELS, X, NY), ((0, 4), (1, 8)), -0.2, 0.2), 2.0, 4.0),
        "shifts": draw_shifts(jax.random.fold_in(seeds[6], 71), 0),
        "levels": draw_levels(jax.random.fold_in(seeds[6], 71), 0),
    }


GAMMA = 5.0 / 3.0
SECTION = 0.02
GRAVITY = 0.5
SIN_VIEW = 0.8660254037844386
COS_VIEW = 0.5
STRENGTH = 4.0
SPACING = 0.25


def derive(padded, axis, count):
    def layer(offset):
        return lax.slice_in_dim(padded, offset, offset + count, axis=axis)
    return (45.0 * (layer(4) - layer(2)) - 9.0 * (layer(5) - layer(1)) + (layer(6) - layer(0))) / 60.0


def flux(state, comp):
    rho = state[0]
    moment = state[1:4]
    field = state[4:7]
    energy = state[7]
    velocity = moment / rho
    field_sq = jnp.sum(field * field, axis=0)
    pressure = (GAMMA - 1.0) * (energy - 0.5 * jnp.sum(moment * velocity, axis=0) - 0.5 * field_sq)
    total = pressure + 0.5 * field_sq
    along = velocity[comp]
    normal = field[comp]
    flux_mom = (moment * along - field * normal).at[comp].add(total)
    flux_mag = along * field - normal * velocity
    flux_energy = (energy + total) * along - normal * jnp.sum(velocity * field, axis=0)
    return jnp.concatenate([moment[comp][None], flux_mom, flux_mag, flux_energy[None]], axis=0)


def tendency(along_x, along_y, along_z, state):
    depth_cells, width_cells, cross_cells = state.shape[1], state.shape[2], state.shape[3]
    rate = -(derive(flux(along_x, 0), 2, width_cells) + derive(flux(along_y, 1), 3, cross_cells) + derive(flux(along_z, 2), 1, depth_cells))
    rate = rate.at[3].add(GRAVITY * state[0])
    rate = rate.at[7].add(GRAVITY * state[3])
    return rate


def line_fields(new_state):
    dens = 0.5 + jax.nn.softplus(new_state[0])
    speed = (COS_VIEW * new_state[3] + SIN_VIEW * new_state[1]) / dens
    field_sq = jnp.sum(new_state[4:7] * new_state[4:7], axis=0)
    source = jax.nn.softplus(new_state[7] - 0.5 * field_sq) / dens
    return jnp.stack([dens, speed, source], axis=1)


def reference(density, momentum, magnetic, energy, shifts, levels):
    state = jnp.concatenate([density[None], momentum, magnetic, energy[None]], axis=0)
    along_x = jnp.pad(state, ((0, 0), (0, 0), (3, 3), (0, 0)), mode="wrap")
    along_y = jnp.pad(state, ((0, 0), (0, 0), (0, 0), (3, 3)), mode="wrap")
    along_z = jnp.pad(state, ((0, 0), (3, 3), (0, 0), (0, 0)), mode="edge")
    new_state = state + SECTION * tendency(along_x, along_y, along_z, state)
    fields = line_fields(new_state)[levels]
    count = levels.shape[0]
    width_cells = fields.shape[2]
    index = (jnp.arange(width_cells, dtype=jnp.int32)[None, :] + shifts[:, None]) % width_cells
    index = jnp.broadcast_to(index[:, None, :, None], fields.shape).astype(jnp.int32)
    sheared = jnp.take_along_axis(fields, index, axis=2)
    dens = sheared[:, 0]
    speed = sheared[:, 1]
    source = sheared[:, 2]

    def emergent(wave):
        offset = (wave.astype(jnp.float32) - 0.5 * (W - 1)) * SPACING
        gap = offset - speed
        dtau = (2.0 / count) * dens * (1.0 + STRENGTH * jnp.exp(-gap * gap))
        running = jnp.cumsum(dtau, axis=0)
        above = jnp.concatenate([jnp.zeros_like(dtau[:1]), running[:-1]], axis=0)
        inner = jnp.sum(source * jnp.exp(-above) * (1.0 - jnp.exp(-dtau)), axis=0)
        return inner + source[count - 1] * jnp.exp(-running[count - 1])

    intensity = lax.map(emergent, jnp.arange(W, dtype=jnp.int32))
    return new_state, intensity
```

```python
import functools
import math

import jax
import jax.numpy as jnp
from jax import lax
from jax.experimental import pallas as pl
from jax.experimental.pallas import tpu as pltpu
from jax.sharding import PartitionSpec as P

W = 48
MOST = 8
GAMMA = 5.0 / 3.0
SECTION = 0.02
GRAVITY = 0.5
SIN_VIEW = 0.8660254037844386
COS_VIEW = 0.5
STRENGTH = 4.0
SPACING = 0.25
LOG2E = 1.4426950408889634
ROOT_LOG2E = math.sqrt(LOG2E)
F32 = jnp.float32
MESH = pl.DeviceIdType.MESH
PAD = 8


def column_shift(level):
    return (1732 * level + 1000) // 2000


def softplus(a):
    return jnp.maximum(a, 0.0) + jnp.log1p(jnp.exp(-jnp.abs(a)))


class Plan:
    def __init__(self, tiles, slabs, depth_cells, width, cross, positions):
        self.tiles, self.slabs = tiles, slabs
        self.depth_cells, self.width, self.cross = depth_cells, width, cross
        self.positions = positions
        self.most = min(MOST, depth_cells)
        self.lanes = cross // slabs
        self.blocks = 128 // self.lanes
        self.items = 3 * self.most
        self.packed = -(-self.items // self.blocks)
        self.low = [column_shift(d * depth_cells) for d in range(slabs)]
        high = [column_shift((d + 1) * depth_cells - 1) for d in range(slabs)]
        self.window = max(h - l for l, h in zip(self.low, high)) + width
        self.rows = -(-self.window // 8) * 8
        self.pieces = []
        for d in range(slabs):
            mine = []
            reach = high[d] - self.low[d] + width
            for o in range(self.low[d] // width, (high[d] + width - 1) // width + 1):
                first = max(0, self.low[d] - width * o)
                last = min(width, self.low[d] + reach - width * o)
                if last > first:
                    mine.append((o, first, last - first, width * o + first - self.low[d]))
            self.pieces.append(mine)
        self.count = max(len(p) for p in self.pieces)


def section_kernel(
    plan, levels, density, momentum, magnetic, energy, state_out, lines_out,
    st, xf, zf, part, ns, pack, recv,
    in_sem, xs_sem, xr_sem, zs_sem, zr_sem, ls_sem, lr_sem, out_sem,
):
    tiles, slabs, cells, width = plan.tiles, plan.slabs, plan.depth_cells, plan.width
    t = lax.axis_index("tile")
    d = lax.axis_index("depth")
    right = lax.rem(t + 1, tiles)
    left = lax.rem(t + tiles - 1, tiles)

    loads = [
        pltpu.make_async_copy(density, st.at[0], in_sem.at[0]),
        pltpu.make_async_copy(momentum, st.at[1:4], in_sem.at[1]),
        pltpu.make_async_copy(magnetic, st.at[4:7], in_sem.at[2]),
        pltpu.make_async_copy(energy, st.at[7], in_sem.at[3]),
    ]
    for load in loads:
        load.start()

    barrier = pltpu.get_barrier_semaphore()

    def greet(tile, depth):
        pl.semaphore_signal(barrier, inc=1, device_id=(tile, depth), device_id_type=MESH)

    greet(right, d)
    greet(left, d)

    @pl.when(d > 0)
    def _():
        greet(t, d - 1)

    @pl.when(d < slabs - 1)
    def _():
        greet(t, d + 1)

    for source in range(slabs):
        for o, _, _, _ in plan.pieces[source]:
            tile = lax.rem(t + o, tiles)
            if o % tiles == 0:

                @pl.when(d != source)
                def _():
                    greet(tile, source)

            else:
                greet(tile, source)

    for load in loads:
        load.wait()

    scale = SECTION / 60.0

    def fluxes(level, carry):
        rho = st[0, level]
        mx, my, mz = st[1, level], st[2, level], st[3, level]
        bx, by, bz = st[4, level], st[5, level], st[6, level]
        en = st[7, level]
        inv = 1.0 / rho
        vx, vy, vz = mx * inv, my * inv, mz * inv
        half_sq = 0.5 * (bx * bx + by * by + bz * bz)
        kinetic = 0.5 * (mx * vx + my * vy + mz * vz)
        total = (GAMMA - 1.0) * (en - kinetic - half_sq) + half_sq
        vb = vx * bx + vy * by + vz * bz
        enthalpy = en + total
        txy = mx * vy - bx * by
        txz = mx * vz - bx * bz
        tyz = my * vz - by * bz
        exy = vx * by - bx * vy
        exz = vx * bz - bx * vz
        eyz = vy * bz - by * vz
        along_x = (
            mx, mx * vx + total - bx * bx, txy, txz, exy, exz, enthalpy * vx - bx * vb
        )
        along_y = (
            my, txy, my * vy + total - by * by, tyz, -exy, eyz, enthalpy * vy - by * vb
        )
        along_z = (
            mz, txz, tyz, mz * vz + total - bz * bz, -exz, -eyz, enthalpy * vz - bz * vb
        )
        for c in range(7):
            xf[c, level, PAD:PAD + width, :] = along_x[c]
            zf[c, level + 3] = along_z[c]

        def cross(f):
            def at(step):
                return pltpu.roll(f, (-step) % plan.cross, 1)

            return (
                45.0 * (at(1) - at(-1)) - 9.0 * (at(2) - at(-2)) + (at(3) - at(-3))
            ) * scale

        base = (
            rho, mx, my, mz + (SECTION * GRAVITY) * rho, bx, by, bz,
            en + (SECTION * GRAVITY) * mz,
        )
        rows_y = (0, 1, 2, 3, 4, 6, 7)
        for c, row in enumerate(rows_y):
            part[row, level] = base[row] - cross(along_y[c])
        part[5, level] = base[5]
        return carry

    lax.fori_loop(0, cells, fluxes, 0)

    targets = 2 + jnp.where(d > 0, 1, 0) + jnp.where(d < slabs - 1, 1, 0)
    for source in range(slabs):
        mine = sum(slabs - (1 if o % tiles == 0 else 0) for o, _, _, _ in plan.pieces[source])
        targets = targets + jnp.where(d == source, mine, 0)
    pl.semaphore_wait(barrier, targets)

    def x_copy(side):
        src = PAD + width - 3 if side == 0 else PAD
        dst = PAD - 3 if side == 0 else PAD + width
        return pltpu.make_async_remote_copy(
            src_ref=xf.at[:, :, pl.ds(src, 3), :],
            dst_ref=xf.at[:, :, pl.ds(dst, 3), :],
            send_sem=xs_sem.at[side],
            recv_sem=xr_sem.at[side],
            device_id=(right if side == 0 else left, d),
            device_id_type=MESH,
        )

    def z_copy(side):
        src = cells if side == 0 else 3
        dst = 0 if side == 0 else cells + 3
        return pltpu.make_async_remote_copy(
            src_ref=zf.at[:, pl.ds(src, 3)],
            dst_ref=zf.at[:, pl.ds(dst, 3)],
            send_sem=zs_sem.at[side],
            recv_sem=zr_sem.at[side],
            device_id=(t, d + 1 if side == 0 else d - 1),
            device_id_type=MESH,
        )

    x_copy(0).start()
    x_copy(1).start()

    @pl.when(d < slabs - 1)
    def _():
        z_copy(0).start()

    @pl.when(d > 0)
    def _():
        z_copy(1).start()

    @pl.when(d == 0)
    def _():
        for c in range(7):
            edge = zf[c, 3]
            for i in range(3):
                zf[c, i] = edge

    @pl.when(d > 0)
    def _():
        z_copy(0).wait_recv()

    @pl.when(d == slabs - 1)
    def _():
        for c in range(7):
            edge = zf[c, cells + 2]
            for i in range(3):
                zf[c, cells + 3 + i] = edge

    @pl.when(d < slabs - 1)
    def _():
        z_copy(1).wait_recv()

    def depth_part(level, carry):
        for c, row in enumerate((0, 1, 2, 3, 4, 5, 7)):
            f = [zf[c, level + i] for i in range(7)]
            part[row, level] = part[row, level] - scale * (
                45.0 * (f[4] - f[2]) - 9.0 * (f[5] - f[1]) + (f[6] - f[0])
            )
        return carry

    lax.fori_loop(0, cells, depth_part, 0)

    x_copy(0).wait_recv()
    x_copy(1).wait_recv()

    def width_part(level, carry):
        for c, row in enumerate((0, 1, 2, 3, 5, 6, 7)):
            f = [xf[c, level, pl.ds(PAD - 3 + i, width), :] for i in range(7)]
            ns[row, level] = part[row, level] - scale * (
                45.0 * (f[4] - f[2]) - 9.0 * (f[5] - f[1]) + (f[6] - f[0])
            )
        ns[4, level] = part[4, level]
        return carry

    lax.fori_loop(0, cells, width_part, 0)

    out_copy = pltpu.make_async_copy(ns, state_out, out_sem.at[0])
    out_copy.start()

    lowest = d * cells
    ahead = jnp.int32(0)
    for k in range(plan.positions):
        ahead = ahead + jnp.where(levels[k] < lowest, 1, 0)
    block_of = lax.broadcasted_iota(jnp.int32, (width, 128), 1) // plan.lanes

    rows = {}
    for slot in range(plan.most):
        held = jnp.clip(
            levels[jnp.minimum(ahead + slot, plan.positions - 1)] - lowest, 0, cells - 1
        )
        dens = 0.5 + softplus(ns[0, held])
        inv = 1.0 / dens
        speed = (COS_VIEW * ns[3, held] + SIN_VIEW * ns[1, held]) * inv
        bx, by, bz = ns[4, held], ns[5, held], ns[6, held]
        source = softplus(ns[7, held] - 0.5 * (bx * bx + by * by + bz * bz)) * inv
        for f, value in enumerate((dens, speed, source)):
            item = 3 * slot + f
            row, block = item // plan.blocks, item % plan.blocks
            for target in range(slabs):
                shift = ((block - target) * plan.lanes) % 128
                moved = pltpu.roll(value, shift, 1) if shift else value
                held_row = rows.get((target, row))
                rows[target, row] = (
                    moved if held_row is None else jnp.where(block_of == block, moved, held_row)
                )
                if block == plan.blocks - 1 or item == plan.items - 1:
                    pack[target, row] = rows.pop((target, row))

    def line_copy(source, n, tile, target):
        _, first, size, at = plan.pieces[source][n]
        return pltpu.make_async_remote_copy(
            src_ref=pack.at[target, :, pl.ds(first, size), :],
            dst_ref=recv.at[source, :, pl.ds(at, size), :],
            send_sem=ls_sem.at[n, target],
            recv_sem=lr_sem.at[source, n],
            device_id=(tile, target),
            device_id_type=MESH,
        )

    def own_copy(source, n):
        _, first, size, at = plan.pieces[source][n]
        return pltpu.make_async_copy(
            pack.at[source, :, pl.ds(first, size), :],
            recv.at[source, :, pl.ds(at, size), :],
            lr_sem.at[source, n],
        )

    for source in range(slabs):

        @pl.when(d == source)
        def _():
            for n, (o, _, _, _) in enumerate(plan.pieces[source]):
                tile = lax.rem(t + tiles - o % tiles, tiles)
                for target in range(slabs):
                    if o % tiles == 0 and target == source:
                        own_copy(source, n).start()
                    else:
                        line_copy(source, n, tile, target).start()

    for source in range(slabs):
        for n, (o, _, _, _) in enumerate(plan.pieces[source]):
            if o % tiles == 0:

                @pl.when(d == source)
                def _():
                    own_copy(source, n).wait()

                @pl.when(d != source)
                def _():
                    line_copy(source, n, left, source).wait_recv()

            else:
                line_copy(source, n, left, source).wait_recv()

    lines_copy = pltpu.make_async_copy(recv, lines_out, out_sem.at[1])
    lines_copy.start()

    x_copy(0).wait_send()
    x_copy(1).wait_send()

    @pl.when(d < slabs - 1)
    def _():
        z_copy(0).wait_send()

    @pl.when(d > 0)
    def _():
        z_copy(1).wait_send()

    for source in range(slabs):

        @pl.when(d == source)
        def _():
            for n, (o, _, _, _) in enumerate(plan.pieces[source]):
                for target in range(slabs):
                    if not (o % tiles == 0 and target == source):
                        line_copy(source, n, left, target).wait_send()

    out_copy.wait()
    lines_copy.wait()


def ray_kernel(
    plan, levels, shifts, lines, state_in, state_out, intensity,
    rows, fields, hold, in_sem, state_sem, out_sem,
):
    slabs, cells, width, blocks = plan.slabs, plan.depth_cells, plan.width, plan.blocks
    lanes, positions = plan.lanes, plan.positions
    lines_copy = pltpu.make_async_copy(lines, rows, in_sem)
    lines_copy.start()
    state_copy = pltpu.make_async_copy(state_in, hold, state_sem)
    state_copy.start()

    slab, slot = [], []
    for k in range(positions):
        level = levels[k]
        slab.append(level // cells)
    run = jnp.int32(0)
    for k in range(positions):
        if k:
            run = jnp.where(slab[k] == slab[k - 1], run + 1, 0)
        slot.append(run)

    lane = lax.broadcasted_iota(jnp.int32, (width, 128), 1)
    within = lax.rem(lane, lanes)
    lines_copy.wait()
    for k in range(positions):
        start = shifts[k] - column_shift(slab[k] * cells)
        got = []
        for f in range(3):
            item = 3 * slot[k] + f
            row, block = item // blocks, lax.rem(item, blocks)
            value = rows[slab[k], row, pl.ds(start, width), :]
            got.append(jnp.take_along_axis(value, within + block * lanes, axis=1))
        dens, speed, source = got
        thin = dens * (-LOG2E * 2.0 / positions)
        fields[0, k] = thin
        fields[1, k] = speed * ROOT_LOG2E
        fields[2, k] = source

    state_copy.wait()
    out_copy = pltpu.make_async_copy(hold, state_out, out_sem)
    out_copy.start()

    groups = W // blocks
    batch = next(b for b in (6, 4, 3, 2, 1) if groups % b == 0)
    which = lax.broadcasted_iota(jnp.int32, (8, 128), 1) // lanes

    for part in range(groups // batch):
        for half in range(width // 8):
            waves = [
                (((part * batch + g) * blocks + which).astype(F32) - 0.5 * (W - 1))
                * (SPACING * ROOT_LOG2E)
                for g in range(batch)
            ]

            def step(k, carry):
                seen, total = carry
                thin = fields[0, k, 8 * half:8 * half + 8, :]
                speed = fields[1, k, 8 * half:8 * half + 8, :]
                source = fields[2, k, 8 * half:8 * half + 8, :]
                strong = STRENGTH * thin
                seen_next, total_next = [], []
                for g in range(batch):
                    gap = waves[g] - speed
                    depth = thin + strong * jnp.exp2(-(gap * gap))
                    after = seen[g] * jnp.exp2(depth)
                    total_next.append(total[g] + source * (seen[g] - after))
                    seen_next.append(after)
                return tuple(seen_next), tuple(total_next)

            ones = tuple(jnp.ones((8, 128), F32) for _ in range(batch))
            zeros = tuple(jnp.zeros((8, 128), F32) for _ in range(batch))
            seen, total = lax.fori_loop(0, positions, step, (ones, zeros), unroll=4)
            last = fields[2, positions - 1, 8 * half:8 * half + 8, :]
            for g in range(batch):
                value = total[g] + last * seen[g]
                for b in range(blocks):
                    intensity[(part * batch + g) * blocks + b, 8 * half:8 * half + 8, :] = value[
                        :, b * lanes:(b + 1) * lanes
                    ]

    out_copy.wait()


def per_device(plan, density, momentum, magnetic, energy, shifts, levels):
    cells, width, cross = density.shape
    slabs = plan.slabs
    any_spec = pl.BlockSpec(memory_space=pl.ANY)
    scalars = pl.BlockSpec(memory_space=pltpu.SMEM)
    state_shape = jax.ShapeDtypeStruct((8, cells, width, cross), F32)
    lines_shape = jax.ShapeDtypeStruct((slabs, plan.packed, plan.rows, 128), F32)
    state, lines = pl.pallas_call(
        functools.partial(section_kernel, plan),
        out_shape=(state_shape, lines_shape),
        in_specs=[scalars] + [any_spec] * 4,
        out_specs=(any_spec, any_spec),
        scratch_shapes=[
            pltpu.VMEM((8, cells, width, cross), F32),
            pltpu.VMEM((7, cells, width + 2 * PAD, cross), F32),
            pltpu.VMEM((7, cells + 6, width, cross), F32),
            pltpu.VMEM((8, cells, width, cross), F32),
            pltpu.VMEM((8, cells, width, cross), F32),
            pltpu.VMEM((slabs, plan.packed, width, 128), F32),
            pltpu.VMEM((slabs, plan.packed, plan.rows, 128), F32),
            pltpu.SemaphoreType.DMA((4,)),
            pltpu.SemaphoreType.DMA((2,)),
            pltpu.SemaphoreType.DMA((2,)),
            pltpu.SemaphoreType.DMA((2,)),
            pltpu.SemaphoreType.DMA((2,)),
            pltpu.SemaphoreType.DMA((plan.count, slabs)),
            pltpu.SemaphoreType.DMA((slabs, plan.count)),
            pltpu.SemaphoreType.DMA((2,)),
        ],
        compiler_params=pltpu.CompilerParams(collective_id=0, has_side_effects=True),
        name="section",
    )(levels, density, momentum, magnetic, energy)
    new_state, intensity = pl.pallas_call(
        functools.partial(ray_kernel, plan),
        out_shape=(state_shape, jax.ShapeDtypeStruct((W, width, plan.lanes), F32)),
        in_specs=[scalars, scalars, any_spec, any_spec],
        out_specs=(any_spec, pl.BlockSpec(memory_space=pltpu.VMEM)),
        scratch_shapes=[
            pltpu.VMEM((slabs, plan.packed, plan.rows, 128), F32),
            pltpu.VMEM((3, plan.positions, width, 128), F32),
            pltpu.VMEM((8, cells, width, cross), F32),
            pltpu.SemaphoreType.DMA,
            pltpu.SemaphoreType.DMA,
            pltpu.SemaphoreType.DMA,
        ],
        name="ray",
    )(levels, shifts, lines, state)
    return new_state, intensity


def solution(mesh):
    tiles, slabs = mesh.shape["tile"], mesh.shape["depth"]

    def body(density, momentum, magnetic, energy, shifts, levels):
        cells, width, cross = density.shape
        plan = Plan(tiles, slabs, cells, width, cross, levels.shape[0])
        return per_device(plan, density, momentum, magnetic, energy, shifts, levels)

    return jax.shard_map(
        body,
        mesh=mesh,
        in_specs=(
            P("depth", "tile", None),
            P(None, "depth", "tile", None),
            P(None, "depth", "tile", None),
            P("depth", "tile", None),
            P(),
            P(),
        ),
        out_specs=(P(None, "depth", "tile", None), P(None, "tile", "depth")),
        check_vma=False,
    )
```

```python
import functools
import math

import jax
import jax.numpy as jnp
from jax import lax
from jax.experimental import pallas as pl
from jax.experimental.pallas import tpu as pltpu
from jax.sharding import PartitionSpec as P

W = 48
MOST = 8
GAMMA = 5.0 / 3.0
SECTION = 0.02
GRAVITY = 0.5
SIN_VIEW = 0.8660254037844386
COS_VIEW = 0.5
STRENGTH = 4.0
SPACING = 0.25
LOG2E = 1.4426950408889634
ROOT_LOG2E = math.sqrt(LOG2E)
F32 = jnp.float32
MESH = pl.DeviceIdType.MESH
PAD = 8


def column_shift(level):
    return (1732 * level + 1000) // 2000


def softplus(a):
    return jnp.maximum(a, 0.0) + jnp.log1p(jnp.exp(-jnp.abs(a)))


class Plan:
    def __init__(self, tiles, slabs, depth_cells, width, cross, positions, parts):
        self.tiles, self.slabs = tiles, slabs
        self.depth_cells, self.width, self.cross = depth_cells, width, cross
        self.positions = positions
        self.most = min(MOST, depth_cells)
        self.lanes = cross // slabs
        self.blocks = 128 // self.lanes
        self.items = 3 * self.most
        self.packed = -(-self.items // self.blocks)
        self.low = [column_shift(d * depth_cells) for d in range(slabs)]
        high = [column_shift((d + 1) * depth_cells - 1) for d in range(slabs)]
        self.rows = -(-(max(h - l for l, h in zip(self.low, high)) + width) // 8) * 8
        parts = min(parts, self.packed)
        cuts = [self.packed * i // parts for i in range(parts + 1)]
        self.pieces = []
        for d in range(slabs):
            mine = []
            for start, stop in zip(cuts[:-1], cuts[1:]):
                slot_low = start * self.blocks // 3
                slot_high = min(self.most - 1, (stop * self.blocks - 1) // 3)
                low = column_shift(d * depth_cells + slot_low)
                high = column_shift(d * depth_cells + depth_cells - self.most + slot_high)
                for o in range(low // width, (high + width - 1) // width + 1):
                    first = max(0, low - width * o)
                    last = min(width, high + width - width * o)
                    if last > first:
                        at = width * o + first - self.low[d]
                        mine.append((o, start, stop - start, first, last - first, at))
            self.pieces.append(mine)
        self.count = max(len(p) for p in self.pieces)
        self.reach = sorted({p[0] for mine in self.pieces for p in mine if p[0] % tiles})


def slab_start(levels, lowest, positions):
    ahead = jnp.int32(0)
    for k in range(positions):
        ahead = ahead + jnp.where(levels[k] < lowest, 1, 0)
    return ahead


def level_order(plan, levels, d, order):
    cells, most, positions = plan.depth_cells, plan.most, plan.positions
    lowest = d * cells
    ahead = slab_start(levels, lowest, positions)
    held = slab_start(levels, lowest + cells, positions) - ahead
    spare = most - held
    used = [
        jnp.where(
            i < held, levels[jnp.minimum(ahead + i, positions - 1)] - lowest, 2 * cells
        )
        for i in range(most)
    ]

    def free(rank):
        level = rank
        for one in used:
            level = level + jnp.where(one <= level, 1, 0)
        return level

    full = jnp.where(spare > 0, free(spare - 1) + 1, 0)
    for j in range(most):
        later = levels[jnp.clip(ahead + j - spare, 0, positions - 1)] - lowest
        order[j] = jnp.clip(jnp.where(j < full, j, later), 0, cells - 1)
    for j in range(cells - most):
        order[most + j] = jnp.clip(free(spare + j), 0, cells - 1)


def primitives(st, level):
    rho = st[0, level]
    mx, my, mz = st[1, level], st[2, level], st[3, level]
    bx, by, bz = st[4, level], st[5, level], st[6, level]
    en = st[7, level]
    inv = 1.0 / rho
    vx, vy, vz = mx * inv, my * inv, mz * inv
    half_sq = 0.5 * (bx * bx + by * by + bz * bz)
    kinetic = 0.5 * (mx * vx + my * vy + mz * vz)
    total = (GAMMA - 1.0) * (en - kinetic - half_sq) + half_sq
    vb = vx * bx + vy * by + vz * bz
    return rho, (mx, my, mz), (bx, by, bz), (vx, vy, vz), en, total, vb


def flux_along(axis, values):
    rho, m, b, v, en, total, vb = values
    out = [m[axis]]
    for i in range(3):
        term = m[i] * v[axis] - b[i] * b[axis]
        out.append(term + total if i == axis else term)
    for i in range(3):
        if i != axis:
            out.append(v[axis] * b[i] - b[axis] * v[i])
    out.append((en + total) * v[axis] - b[axis] * vb)
    return out


ROWS = ((0, 1, 2, 3, 5, 6, 7), (0, 1, 2, 3, 4, 6, 7), (0, 1, 2, 3, 4, 5, 7))
SCALE = SECTION / 60.0


def stencil(f):
    return SCALE * (45.0 * (f[4] - f[2]) - 9.0 * (f[5] - f[1]) + (f[6] - f[0]))


def section_kernel(
    plan, levels, density, momentum, magnetic, energy, state_out, lines_out,
    order, st, xf, zf, part, ns, pack, held, recv,
    in_sem, xs_sem, xr_sem, zs_sem, zr_sem, ds_sem, dr_sem, ls_sem, lr_sem, out_sem,
):
    tiles, slabs, cells, width = plan.tiles, plan.slabs, plan.depth_cells, plan.width
    most = plan.most
    t = lax.axis_index("tile")
    d = lax.axis_index("depth")
    right = lax.rem(t + 1, tiles)
    left = lax.rem(t + tiles - 1, tiles)

    loads = [
        pltpu.make_async_copy(density, st.at[0], in_sem.at[0]),
        pltpu.make_async_copy(momentum, st.at[1:4], in_sem.at[1]),
        pltpu.make_async_copy(magnetic, st.at[4:7], in_sem.at[2]),
        pltpu.make_async_copy(energy, st.at[7], in_sem.at[3]),
    ]
    for load in loads:
        load.start()

    barrier = pltpu.get_barrier_semaphore()

    def greet(tile, depth):
        pl.semaphore_signal(barrier, inc=1, device_id=(tile, depth), device_id_type=MESH)

    greet(right, d)
    greet(left, d)
    for i in range(1, slabs):
        greet(t, lax.rem(d + i, slabs))
    for o in plan.reach:
        greet(lax.rem(t + o, tiles), d)

    level_order(plan, levels, d, order)
    for load in loads:
        load.wait()

    def along_x(slot, carry):
        values = flux_along(0, primitives(st, order[slot]))
        for c in range(7):
            xf[c, slot, PAD:PAD + width, :] = values[c]
        return carry

    def x_copy(side, half):
        src = PAD + width - 3 if side == 0 else PAD
        dst = PAD - 3 if side == 0 else PAD + width
        slots = pl.ds(0, most) if half == 0 else pl.ds(most, cells - most)
        return pltpu.make_async_remote_copy(
            src_ref=xf.at[:, slots, pl.ds(src, 3), :],
            dst_ref=xf.at[:, slots, pl.ds(dst, 3), :],
            send_sem=xs_sem.at[side, half],
            recv_sem=xr_sem.at[side, half],
            device_id=(right if side == 0 else left, d),
            device_id_type=MESH,
        )

    def z_copy(side):
        src = cells if side == 0 else 3
        dst = 0 if side == 0 else cells + 3
        return pltpu.make_async_remote_copy(
            src_ref=zf.at[:, pl.ds(src, 3)],
            dst_ref=zf.at[:, pl.ds(dst, 3)],
            send_sem=zs_sem.at[side],
            recv_sem=zr_sem.at[side],
            device_id=(t, d + 1 if side == 0 else d - 1),
            device_id_type=MESH,
        )

    lax.fori_loop(0, most, along_x, 0)
    pl.semaphore_wait(barrier, 2 + (slabs - 1) + len(plan.reach))
    x_copy(0, 0).start()
    x_copy(1, 0).start()

    def along_z(level):
        values = flux_along(2, primitives(st, level))
        for c in range(7):
            zf[c, level + 3] = values[c]

    def rim(i, carry):
        along_z(i)
        along_z(cells - 3 + i)
        return carry

    lax.fori_loop(0, 3, rim, 0)

    @pl.when(d < slabs - 1)
    def _():
        z_copy(0).start()

    @pl.when(d > 0)
    def _():
        z_copy(1).start()

    halves = 2 if cells > most else 1
    if halves == 2:
        lax.fori_loop(most, cells, along_x, 0)
        x_copy(0, 1).start()
        x_copy(1, 1).start()

    def inner(level, carry):
        along_z(level)
        return carry

    lax.fori_loop(3, cells - 3, inner, 0)

    def cross(f):
        def at(step):
            return pltpu.roll(f, (-step) % plan.cross, 1)

        return stencil([at(i - 3) if i != 3 else f for i in range(7)])

    def along_y(level, carry):
        values = primitives(st, level)
        rho, m, b, _, en, _, _ = values
        base = [
            rho, m[0], m[1], m[2] + (SECTION * GRAVITY) * rho, b[0], b[1], b[2],
            en + (SECTION * GRAVITY) * m[2],
        ]
        flux = flux_along(1, values)
        for c, row in enumerate(ROWS[1]):
            base[row] = base[row] - cross(flux[c])
        for row in range(8):
            part[row, level] = base[row]
        return carry

    lax.fori_loop(0, cells, along_y, 0)

    @pl.when(d == 0)
    def _():
        for c in range(7):
            edge = zf[c, 3]
            for i in range(3):
                zf[c, i] = edge

    @pl.when(d > 0)
    def _():
        z_copy(0).wait_recv()

    @pl.when(d == slabs - 1)
    def _():
        for c in range(7):
            edge = zf[c, cells + 2]
            for i in range(3):
                zf[c, cells + 3 + i] = edge

    @pl.when(d < slabs - 1)
    def _():
        z_copy(1).wait_recv()

    def depth_part(level, carry):
        for c, row in enumerate(ROWS[2]):
            part[row, level] = part[row, level] - stencil([zf[c, level + i] for i in range(7)])
        return carry

    lax.fori_loop(0, cells, depth_part, 0)

    def finish(slot):
        level = order[slot]
        row_of = {row: c for c, row in enumerate(ROWS[0])}
        out = []
        for row in range(8):
            value = part[row, level]
            if row in row_of:
                c = row_of[row]
                value = value - stencil(
                    [xf[c, slot, pl.ds(PAD - 3 + i, width), :] for i in range(7)]
                )
            ns[row, slot] = value
            out.append(value)
        return out

    x_copy(0, 0).wait_recv()
    x_copy(1, 0).wait_recv()

    block_of = lax.broadcasted_iota(jnp.int32, (width, 128), 1) // plan.lanes
    rows = {}
    for slot in range(most):
        new = finish(slot)
        dens = 0.5 + softplus(new[0])
        inv = 1.0 / dens
        speed = (COS_VIEW * new[3] + SIN_VIEW * new[1]) * inv
        bx, by, bz = new[4], new[5], new[6]
        source = softplus(new[7] - 0.5 * (bx * bx + by * by + bz * bz)) * inv
        for f, value in enumerate((dens, speed, source)):
            item = 3 * slot + f
            row, block = item // plan.blocks, item % plan.blocks
            for target in range(slabs):
                shift = ((block - target) * plan.lanes) % 128
                moved = pltpu.roll(value, shift, 1) if shift else value
                earlier = rows.get((target, row))
                rows[target, row] = (
                    moved if earlier is None else jnp.where(block_of == block, moved, earlier)
                )
                if block == plan.blocks - 1 or item == plan.items - 1:
                    pack[target, row] = rows.pop((target, row))

    def depth_copy(step):
        target = lax.rem(d + step, slabs)
        return pltpu.make_async_remote_copy(
            src_ref=pack.at[target],
            dst_ref=held.at[d],
            send_sem=ds_sem.at[step],
            recv_sem=dr_sem.at[step],
            device_id=(t, target),
            device_id_type=MESH,
        )

    own = pltpu.make_async_copy(pack.at[d], held.at[d], dr_sem.at[0])
    own.start()
    for step in range(1, slabs):
        depth_copy(step).start()

    def line_copy(source, n):
        o, row, count, first, size, at = plan.pieces[source][n]
        src = held.at[source, pl.ds(row, count), pl.ds(first, size), :]
        dst = recv.at[source, pl.ds(row, count), pl.ds(at, size), :]
        if o % tiles == 0:
            return pltpu.make_async_copy(src, dst, lr_sem.at[source, n]), False
        return pltpu.make_async_remote_copy(
            src_ref=src,
            dst_ref=dst,
            send_sem=ls_sem.at[source, n],
            recv_sem=lr_sem.at[source, n],
            device_id=(lax.rem(t + tiles - o % tiles, tiles), d),
            device_id_type=MESH,
        ), True

    def forward(slab):
        for source in range(slabs):

            @pl.when(slab == source)
            def _():
                for n in range(len(plan.pieces[source])):
                    line_copy(source, n)[0].start()

    own.wait()
    forward(d)
    for step in range(1, slabs):
        depth_copy(step).wait_recv()
        forward(lax.rem(d + slabs - step, slabs))

    if halves == 2:
        x_copy(0, 1).wait_recv()
        x_copy(1, 1).wait_recv()

        def rest(slot, carry):
            finish(slot)
            return carry

        lax.fori_loop(most, cells, rest, 0)

    out_copy = pltpu.make_async_copy(ns, state_out, out_sem.at[0])
    out_copy.start()

    for source in range(slabs):
        for n in range(len(plan.pieces[source])):
            copy, remote = line_copy(source, n)
            if remote:
                copy.wait_recv()
            else:
                copy.wait()

    lines_copy = pltpu.make_async_copy(recv, lines_out, out_sem.at[1])
    lines_copy.start()

    for half in range(halves):
        x_copy(0, half).wait_send()
        x_copy(1, half).wait_send()

    @pl.when(d < slabs - 1)
    def _():
        z_copy(0).wait_send()

    @pl.when(d > 0)
    def _():
        z_copy(1).wait_send()

    for step in range(1, slabs):
        depth_copy(step).wait_send()
    for source in range(slabs):
        for n in range(len(plan.pieces[source])):
            copy, remote = line_copy(source, n)
            if remote:
                copy.wait_send()

    out_copy.wait()
    lines_copy.wait()


def ray_kernel(
    plan, levels, shifts, lines, state_in, state_out, intensity,
    order, rows, fields, hold, in_sem, state_sem, out_sem,
):
    slabs, cells, width, blocks = plan.slabs, plan.depth_cells, plan.width, plan.blocks
    lanes, positions, most = plan.lanes, plan.positions, plan.most
    lines_copy = pltpu.make_async_copy(lines, rows, in_sem)
    lines_copy.start()
    state_copy = pltpu.make_async_copy(state_in, hold, state_sem)
    state_copy.start()
    d = lax.axis_index("depth")
    level_order(plan, levels, d, order)

    slab = [levels[k] // cells for k in range(positions)]
    before = [jnp.int32(0)]
    for k in range(1, positions):
        before.append(jnp.where(slab[k] == slab[k - 1], before[-1] + 1, 0))
    held = [before[-1] + 1]
    for k in range(positions - 2, -1, -1):
        held.insert(0, jnp.where(slab[k] == slab[k + 1], held[0], before[k] + 1))
    slot = [
        before[k]
        + jnp.minimum(most - held[k], levels[k] - slab[k] * cells - before[k])
        for k in range(positions)
    ]

    lane = lax.broadcasted_iota(jnp.int32, (width, 128), 1)
    within = lax.rem(lane, lanes)
    wanted = lane // lanes == lax.rem(
        lax.broadcasted_iota(jnp.int32, (width, 128), 0), blocks
    )
    lines_copy.wait()
    for k in range(positions):
        start = shifts[k] - (1732 * (slab[k] * cells) + 1000) // 2000
        for f in range(3):
            item = 3 * slot[k] + f
            row, block = item // blocks, lax.rem(item, blocks)
            value = rows[slab[k], row, pl.ds(start, width), :]
            value = jnp.take_along_axis(value, within + block * lanes, axis=1)
            value = jnp.where(wanted, value, 0.0)
            step = 1
            while step < blocks:
                value = value + pltpu.roll(value, width - step, 0)
                step *= 2
            if f == 0:
                value = value * (-LOG2E * 2.0 / positions)
            elif f == 1:
                value = value * ROOT_LOG2E
            fields[f, k] = value

    state_copy.wait()
    out_copies = [
        pltpu.make_async_copy(hold.at[:, j], state_out.at[:, order[j]], out_sem.at[j])
        for j in range(cells)
    ]
    for copy in out_copies:
        copy.start()

    groups = W // 8
    for part in range(width // blocks):
        waves = [
            (
                (8 * g + lax.broadcasted_iota(jnp.int32, (8, 128), 0)).astype(F32)
                - 0.5 * (W - 1)
            )
            * (SPACING * ROOT_LOG2E)
            for g in range(groups)
        ]

        def field(f, k):
            return jnp.broadcast_to(fields[f, k, part * blocks:part * blocks + 1, :], (8, 128))

        def step(k, carry):
            seen, total = carry
            thin, speed, source = field(0, k), field(1, k), field(2, k)
            strong = STRENGTH * thin
            seen_next, total_next = [], []
            for g in range(groups):
                gap = waves[g] - speed
                depth = thin + strong * jnp.exp2(-(gap * gap))
                after = seen[g] * jnp.exp2(depth)
                total_next.append(total[g] + source * (seen[g] - after))
                seen_next.append(after)
            return tuple(seen_next), tuple(total_next)

        ones = tuple(jnp.ones((8, 128), F32) for _ in range(groups))
        zeros = tuple(jnp.zeros((8, 128), F32) for _ in range(groups))
        seen, total = lax.fori_loop(0, positions, step, (ones, zeros), unroll=4)
        last = field(2, positions - 1)
        value = jnp.concatenate([total[g] + last * seen[g] for g in range(groups)], axis=0)
        intensity[part * 128:(part + 1) * 128, :] = value.T

    for copy in out_copies:
        copy.wait()


def per_device(plan, density, momentum, magnetic, energy, shifts, levels):
    cells, width, cross = density.shape
    slabs = plan.slabs
    any_spec = pl.BlockSpec(memory_space=pl.ANY)
    scalars = pl.BlockSpec(memory_space=pltpu.SMEM)
    state_shape = jax.ShapeDtypeStruct((8, cells, width, cross), F32)
    lines_shape = jax.ShapeDtypeStruct((slabs, plan.packed, plan.rows, 128), F32)
    state, lines = pl.pallas_call(
        functools.partial(section_kernel, plan),
        out_shape=(state_shape, lines_shape),
        in_specs=[scalars] + [any_spec] * 4,
        out_specs=(any_spec, any_spec),
        scratch_shapes=[
            pltpu.SMEM((cells,), jnp.int32),
            pltpu.VMEM((8, cells, width, cross), F32),
            pltpu.VMEM((7, cells, width + 2 * PAD, cross), F32),
            pltpu.VMEM((7, cells + 6, width, cross), F32),
            pltpu.VMEM((8, cells, width, cross), F32),
            pltpu.VMEM((8, cells, width, cross), F32),
            pltpu.VMEM((slabs, plan.packed, width, 128), F32),
            pltpu.VMEM((slabs, plan.packed, width, 128), F32),
            pltpu.VMEM((slabs, plan.packed, plan.rows, 128), F32),
            pltpu.SemaphoreType.DMA((4,)),
            pltpu.SemaphoreType.DMA((2, 2)),
            pltpu.SemaphoreType.DMA((2, 2)),
            pltpu.SemaphoreType.DMA((2,)),
            pltpu.SemaphoreType.DMA((2,)),
            pltpu.SemaphoreType.DMA((slabs,)),
            pltpu.SemaphoreType.DMA((slabs,)),
            pltpu.SemaphoreType.DMA((slabs, plan.count)),
            pltpu.SemaphoreType.DMA((slabs, plan.count)),
            pltpu.SemaphoreType.DMA((2,)),
        ],
        compiler_params=pltpu.CompilerParams(collective_id=0, has_side_effects=True),
        name="section",
    )(levels, density, momentum, magnetic, energy)
    new_state, intensity = pl.pallas_call(
        functools.partial(ray_kernel, plan),
        out_shape=(state_shape, jax.ShapeDtypeStruct((width * plan.lanes, W), F32)),
        in_specs=[scalars, scalars, any_spec, any_spec],
        out_specs=(any_spec, pl.BlockSpec(memory_space=pltpu.VMEM)),
        scratch_shapes=[
            pltpu.SMEM((cells,), jnp.int32),
            pltpu.VMEM((slabs, plan.packed, plan.rows, 128), F32),
            pltpu.VMEM((3, plan.positions, width, 128), F32),
            pltpu.VMEM((8, cells, width, cross), F32),
            pltpu.SemaphoreType.DMA,
            pltpu.SemaphoreType.DMA,
            pltpu.SemaphoreType.DMA((cells,)),
        ],
        name="ray",
    )(levels, shifts, lines, state)
    intensity = intensity.reshape(width, plan.lanes, W)
    return new_state, jnp.transpose(intensity, (2, 0, 1))


def solution(mesh):
    tiles, slabs = mesh.shape["tile"], mesh.shape["depth"]

    def body(density, momentum, magnetic, energy, shifts, levels):
        cells, width, cross = density.shape
        plan = Plan(tiles, slabs, cells, width, cross, levels.shape[0], 2)
        return per_device(plan, density, momentum, magnetic, energy, shifts, levels)

    return jax.shard_map(
        body,
        mesh=mesh,
        in_specs=(
            P("depth", "tile", None),
            P(None, "depth", "tile", None),
            P(None, "depth", "tile", None),
            P("depth", "tile", None),
            P(),
            P(),
        ),
        out_specs=(P(None, "depth", "tile", None), P(None, "tile", "depth")),
        check_vma=False,
    )
```

```python
import functools
import math

import jax
import jax.numpy as jnp
from jax import lax
from jax.experimental import pallas as pl
from jax.experimental.pallas import tpu as pltpu
from jax.sharding import PartitionSpec as P

W = 48
MOST = 8
GAMMA = 5.0 / 3.0
SECTION = 0.02
GRAVITY = 0.5
SIN_VIEW = 0.8660254037844386
COS_VIEW = 0.5
STRENGTH = 4.0
SPACING = 0.25
LOG2E = 1.4426950408889634
ROOT_LOG2E = math.sqrt(LOG2E)
F32 = jnp.float32
MESH = pl.DeviceIdType.MESH
PAD = 8


def column_shift(level):
    return (1732 * level + 1000) // 2000


def softplus(a):
    return jnp.maximum(a, 0.0) + jnp.log1p(jnp.exp(-jnp.abs(a)))


class Plan:
    def __init__(self, tiles, slabs, depth_cells, width, cross, positions, parts):
        self.tiles, self.slabs = tiles, slabs
        self.depth_cells, self.width, self.cross = depth_cells, width, cross
        self.positions = positions
        self.most = min(MOST, depth_cells)
        self.lanes = cross // slabs
        self.blocks = 128 // self.lanes
        self.items = 3 * self.most
        self.packed = -(-self.items // self.blocks)
        self.low = [column_shift(d * depth_cells) for d in range(slabs)]
        high = [column_shift((d + 1) * depth_cells - 1) for d in range(slabs)]
        self.rows = -(-(max(h - l for l, h in zip(self.low, high)) + width) // 8) * 8
        parts = min(parts, self.packed)
        cuts = [self.packed * i // parts for i in range(parts + 1)]
        self.groups = list(zip(cuts[:-1], cuts[1:]))
        ends = [min(self.most, -(-stop * self.blocks // 3)) for _, stop in self.groups]
        ends.append(depth_cells)
        self.spans = list(zip([0] + ends[:-1], ends))
        if self.spans[-1][0] == self.spans[-1][1]:
            self.spans.pop()
        self.pieces = []
        for d in range(slabs):
            mine = []
            for group, (start, stop) in enumerate(self.groups):
                slot_low = start * self.blocks // 3
                slot_high = min(self.most - 1, (stop * self.blocks - 1) // 3)
                low = column_shift(d * depth_cells + slot_low)
                high = column_shift(d * depth_cells + depth_cells - self.most + slot_high)
                for o in range(low // width, (high + width - 1) // width + 1):
                    first = max(0, low - width * o)
                    last = min(width, high + width - width * o)
                    if last > first:
                        at = width * o + first - self.low[d]
                        mine.append((o, group, first, last - first, at))
            self.pieces.append(mine)
        self.count = max(len(p) for p in self.pieces)
        self.reach = sorted({p[0] for mine in self.pieces for p in mine if p[0] % tiles})


def slab_start(levels, lowest, positions):
    ahead = jnp.int32(0)
    for k in range(positions):
        ahead = ahead + jnp.where(levels[k] < lowest, 1, 0)
    return ahead


def level_order(plan, levels, d, order):
    cells, most, positions = plan.depth_cells, plan.most, plan.positions
    lowest = d * cells
    ahead = slab_start(levels, lowest, positions)
    held = slab_start(levels, lowest + cells, positions) - ahead
    spare = most - held
    used = [
        jnp.where(
            i < held, levels[jnp.minimum(ahead + i, positions - 1)] - lowest, 2 * cells
        )
        for i in range(most)
    ]

    def free(rank):
        level = rank
        for one in used:
            level = level + jnp.where(one <= level, 1, 0)
        return level

    full = jnp.where(spare > 0, free(spare - 1) + 1, 0)
    for j in range(most):
        later = levels[jnp.clip(ahead + j - spare, 0, positions - 1)] - lowest
        order[j] = jnp.clip(jnp.where(j < full, j, later), 0, cells - 1)
    for j in range(cells - most):
        order[most + j] = jnp.clip(free(spare + j), 0, cells - 1)


def ray_order(plan, levels, shifts, order):
    cells, most, positions = plan.depth_cells, plan.most, plan.positions
    slab = [levels[k] // cells for k in range(positions)]
    before = [jnp.int32(0)]
    for k in range(1, positions):
        before.append(jnp.where(slab[k] == slab[k - 1], before[-1] + 1, 0))
    held = [before[-1] + 1]
    for k in range(positions - 2, -1, -1):
        held.insert(0, jnp.where(slab[k] == slab[k + 1], held[0], before[k] + 1))
    for k in range(positions):
        spare = jnp.minimum(most - held[k], levels[k] - slab[k] * cells - before[k])
        at = cells + 3 * k
        order[at] = slab[k]
        order[at + 1] = before[k] + spare
        order[at + 2] = shifts[k] - (1732 * (slab[k] * cells) + 1000) // 2000


def primitives(st, level):
    rho = st[0, level]
    mx, my, mz = st[1, level], st[2, level], st[3, level]
    bx, by, bz = st[4, level], st[5, level], st[6, level]
    en = st[7, level]
    inv = 1.0 / rho
    vx, vy, vz = mx * inv, my * inv, mz * inv
    half_sq = 0.5 * (bx * bx + by * by + bz * bz)
    kinetic = 0.5 * (mx * vx + my * vy + mz * vz)
    total = (GAMMA - 1.0) * (en - kinetic - half_sq) + half_sq
    vb = vx * bx + vy * by + vz * bz
    return rho, (mx, my, mz), (bx, by, bz), (vx, vy, vz), en, total, vb


def flux_along(axis, values):
    rho, m, b, v, en, total, vb = values
    out = [m[axis]]
    for i in range(3):
        term = m[i] * v[axis] - b[i] * b[axis]
        out.append(term + total if i == axis else term)
    for i in range(3):
        if i != axis:
            out.append(v[axis] * b[i] - b[axis] * v[i])
    out.append((en + total) * v[axis] - b[axis] * vb)
    return out


ROWS = ((0, 1, 2, 3, 5, 6, 7), (0, 1, 2, 3, 4, 6, 7), (0, 1, 2, 3, 4, 5, 7))
SCALE = SECTION / 60.0


def stencil(f):
    return SCALE * (45.0 * (f[4] - f[2]) - 9.0 * (f[5] - f[1]) + (f[6] - f[0]))


def section_kernel(
    plan, levels_in, shifts_in, density, momentum, magnetic, energy, ns, recv, order,
    levels, shifts, st, xf, zf, part, pack, held,
    in_sem, xs_sem, xr_sem, zs_sem, zr_sem, ds_sem, dr_sem, ls_sem, lr_sem,
):
    tiles, slabs, cells, width = plan.tiles, plan.slabs, plan.depth_cells, plan.width
    most = plan.most
    t = lax.axis_index("tile")
    d = lax.axis_index("depth")
    right = lax.rem(t + 1, tiles)
    left = lax.rem(t + tiles - 1, tiles)

    loads = [
        pltpu.make_async_copy(density, st.at[0], in_sem.at[0]),
        pltpu.make_async_copy(momentum, st.at[1:4], in_sem.at[1]),
        pltpu.make_async_copy(magnetic, st.at[4:7], in_sem.at[2]),
        pltpu.make_async_copy(energy, st.at[7], in_sem.at[3]),
    ]
    index_loads = [
        pltpu.make_async_copy(levels_in, levels, in_sem.at[4]),
        pltpu.make_async_copy(shifts_in, shifts, in_sem.at[5]),
    ]
    for load in index_loads + loads:
        load.start()

    barrier = pltpu.get_barrier_semaphore()

    def greet(tile, depth):
        pl.semaphore_signal(barrier, inc=1, device_id=(tile, depth), device_id_type=MESH)

    greet(right, d)
    greet(left, d)
    for i in range(1, slabs):
        greet(t, lax.rem(d + i, slabs))
    for o in plan.reach:
        greet(lax.rem(t + o, tiles), d)

    for load in index_loads:
        load.wait()
    level_order(plan, levels, d, order)
    for load in loads:
        load.wait()

    def along_x(slot, carry):
        values = flux_along(0, primitives(st, order[slot]))
        for c in range(7):
            xf[c, slot, PAD:PAD + width, :] = values[c]
        return carry

    def x_copy(side, span):
        src = PAD + width - 3 if side == 0 else PAD
        dst = PAD - 3 if side == 0 else PAD + width
        start, stop = plan.spans[span]
        slots = pl.ds(start, stop - start)
        return pltpu.make_async_remote_copy(
            src_ref=xf.at[:, slots, pl.ds(src, 3), :],
            dst_ref=xf.at[:, slots, pl.ds(dst, 3), :],
            send_sem=xs_sem.at[side, span],
            recv_sem=xr_sem.at[side, span],
            device_id=(right if side == 0 else left, d),
            device_id_type=MESH,
        )

    def z_copy(side):
        src = cells if side == 0 else 3
        dst = 0 if side == 0 else cells + 3
        return pltpu.make_async_remote_copy(
            src_ref=zf.at[:, pl.ds(src, 3)],
            dst_ref=zf.at[:, pl.ds(dst, 3)],
            send_sem=zs_sem.at[side],
            recv_sem=zr_sem.at[side],
            device_id=(t, d + 1 if side == 0 else d - 1),
            device_id_type=MESH,
        )

    spans, groups = len(plan.spans), len(plan.groups)
    lax.fori_loop(0, plan.spans[0][1], along_x, 0)
    pl.semaphore_wait(barrier, 2 + (slabs - 1) + len(plan.reach))
    x_copy(0, 0).start()
    x_copy(1, 0).start()
    for span in range(1, groups):
        lax.fori_loop(plan.spans[span][0], plan.spans[span][1], along_x, 0)
        x_copy(0, span).start()
        x_copy(1, span).start()

    def along_z(level):
        values = flux_along(2, primitives(st, level))
        for c in range(7):
            zf[c, level + 3] = values[c]

    def rim(i, carry):
        along_z(i)
        along_z(cells - 3 + i)
        return carry

    lax.fori_loop(0, 3, rim, 0)

    @pl.when(d < slabs - 1)
    def _():
        z_copy(0).start()

    @pl.when(d > 0)
    def _():
        z_copy(1).start()

    for span in range(groups, spans):
        lax.fori_loop(plan.spans[span][0], plan.spans[span][1], along_x, 0)
        x_copy(0, span).start()
        x_copy(1, span).start()

    def inner(level, carry):
        along_z(level)
        return carry

    lax.fori_loop(3, cells - 3, inner, 0)

    def cross(f):
        def at(step):
            return pltpu.roll(f, (-step) % plan.cross, 1)

        return stencil([at(i - 3) if i != 3 else f for i in range(7)])

    def along_y(level, carry):
        values = primitives(st, level)
        rho, m, b, _, en, _, _ = values
        base = [
            rho, m[0], m[1], m[2] + (SECTION * GRAVITY) * rho, b[0], b[1], b[2],
            en + (SECTION * GRAVITY) * m[2],
        ]
        flux = flux_along(1, values)
        for c, row in enumerate(ROWS[1]):
            base[row] = base[row] - cross(flux[c])
        for row in range(8):
            part[row, level] = base[row]
        return carry

    lax.fori_loop(0, cells, along_y, 0)

    @pl.when(d == 0)
    def _():
        for c in range(7):
            edge = zf[c, 3]
            for i in range(3):
                zf[c, i] = edge

    @pl.when(d > 0)
    def _():
        z_copy(0).wait_recv()

    @pl.when(d == slabs - 1)
    def _():
        for c in range(7):
            edge = zf[c, cells + 2]
            for i in range(3):
                zf[c, cells + 3 + i] = edge

    @pl.when(d < slabs - 1)
    def _():
        z_copy(1).wait_recv()

    def depth_part(level, carry):
        for c, row in enumerate(ROWS[2]):
            part[row, level] = part[row, level] - stencil([zf[c, level + i] for i in range(7)])
        return carry

    lax.fori_loop(0, cells, depth_part, 0)
    ray_order(plan, levels, shifts, order)

    def finish(slot):
        level = order[slot]
        row_of = {row: c for c, row in enumerate(ROWS[0])}
        out = []
        for row in range(8):
            value = part[row, level]
            if row in row_of:
                c = row_of[row]
                value = value - stencil(
                    [xf[c, slot, pl.ds(PAD - 3 + i, width), :] for i in range(7)]
                )
            ns[row, slot] = value
            out.append(value)
        return out

    block_of = lax.broadcasted_iota(jnp.int32, (width, 128), 1) // plan.lanes
    rows = {}

    def emit(slot):
        new = finish(slot)
        dens = 0.5 + softplus(new[0])
        inv = 1.0 / dens
        speed = (COS_VIEW * new[3] + SIN_VIEW * new[1]) * inv
        bx, by, bz = new[4], new[5], new[6]
        source = softplus(new[7] - 0.5 * (bx * bx + by * by + bz * bz)) * inv
        for f, value in enumerate((dens, speed, source)):
            item = 3 * slot + f
            row, block = item // plan.blocks, item % plan.blocks
            for target in range(slabs):
                shift = ((block - target) * plan.lanes) % 128
                moved = pltpu.roll(value, shift, 1) if shift else value
                earlier = rows.get((target, row))
                rows[target, row] = (
                    moved if earlier is None else jnp.where(block_of == block, moved, earlier)
                )
                if block == plan.blocks - 1 or item == plan.items - 1:
                    pack[target, row] = rows.pop((target, row))

    def depth_copy(step, group):
        target = lax.rem(d + step, slabs)
        start, stop = plan.groups[group]
        part_rows = pl.ds(start, stop - start)
        if step == 0:
            return pltpu.make_async_copy(
                pack.at[d, part_rows], held.at[d, part_rows], dr_sem.at[0, group]
            )
        return pltpu.make_async_remote_copy(
            src_ref=pack.at[target, part_rows],
            dst_ref=held.at[d, part_rows],
            send_sem=ds_sem.at[step, group],
            recv_sem=dr_sem.at[step, group],
            device_id=(t, target),
            device_id_type=MESH,
        )

    def line_copy(source, n):
        o, group, first, size, at = plan.pieces[source][n]
        start, stop = plan.groups[group]
        src = held.at[source, pl.ds(start, stop - start), pl.ds(first, size), :]
        dst = recv.at[source, pl.ds(start, stop - start), pl.ds(at, size), :]
        if o % tiles == 0:
            return pltpu.make_async_copy(src, dst, lr_sem.at[source, n]), False
        return pltpu.make_async_remote_copy(
            src_ref=src,
            dst_ref=dst,
            send_sem=ls_sem.at[source, n],
            recv_sem=lr_sem.at[source, n],
            device_id=(lax.rem(t + tiles - o % tiles, tiles), d),
            device_id_type=MESH,
        ), True

    def forward(slab, group):
        for source in range(slabs):

            @pl.when(slab == source)
            def _():
                for n, piece in enumerate(plan.pieces[source]):
                    if piece[1] == group:
                        line_copy(source, n)[0].start()

    for group in range(groups):
        x_copy(0, group).wait_recv()
        x_copy(1, group).wait_recv()
        for slot in range(*plan.spans[group]):
            emit(slot)
        for step in range(slabs):
            depth_copy(step, group).start()
        depth_copy(0, group).wait()
        forward(d, group)

    for group in range(groups):
        for step in range(1, slabs):
            depth_copy(step, group).wait_recv()
            forward(lax.rem(d + slabs - step, slabs), group)

    def rest(slot, carry):
        finish(slot)
        return carry

    for span in range(groups, spans):
        x_copy(0, span).wait_recv()
        x_copy(1, span).wait_recv()
        lax.fori_loop(plan.spans[span][0], plan.spans[span][1], rest, 0)

    for source in range(slabs):
        for n in range(len(plan.pieces[source])):
            copy, remote = line_copy(source, n)
            if remote:
                copy.wait_recv()
            else:
                copy.wait()

    for span in range(spans):
        x_copy(0, span).wait_send()
        x_copy(1, span).wait_send()

    @pl.when(d < slabs - 1)
    def _():
        z_copy(0).wait_send()

    @pl.when(d > 0)
    def _():
        z_copy(1).wait_send()

    for group in range(groups):
        for step in range(1, slabs):
            depth_copy(step, group).wait_send()
    for source in range(slabs):
        for n in range(len(plan.pieces[source])):
            copy, remote = line_copy(source, n)
            if remote:
                copy.wait_send()


def ray_kernel(plan, order, rows, hold, state_out, intensity, fields, out_sem):
    cells, width, blocks = plan.depth_cells, plan.width, plan.blocks
    lanes, positions = plan.lanes, plan.positions
    out_copies = [
        pltpu.make_async_copy(hold.at[:, j], state_out.at[:, order[j]], out_sem.at[j])
        for j in range(cells)
    ]
    for copy in out_copies:
        copy.start()

    lane = lax.broadcasted_iota(jnp.int32, (width, 128), 1)
    within = lax.rem(lane, lanes)
    wanted = lane // lanes == lax.rem(
        lax.broadcasted_iota(jnp.int32, (width, 128), 0), blocks
    )
    for k in range(positions):
        at = cells + 3 * k
        slab, slot, start = order[at], order[at + 1], order[at + 2]
        for f in range(3):
            item = 3 * slot + f
            row, block = item // blocks, lax.rem(item, blocks)
            value = rows[slab, row, pl.ds(start, width), :]
            value = jnp.take_along_axis(value, within + block * lanes, axis=1)
            value = jnp.where(wanted, value, 0.0)
            step = 1
            while step < blocks:
                value = value + pltpu.roll(value, width - step, 0)
                step *= 2
            if f == 0:
                value = value * (-LOG2E * 2.0 / positions)
            elif f == 1:
                value = value * ROOT_LOG2E
            fields[f, k] = value

    groups = W // 8
    for part in range(width // blocks):
        waves = [
            (
                (8 * g + lax.broadcasted_iota(jnp.int32, (8, 128), 0)).astype(F32)
                - 0.5 * (W - 1)
            )
            * (SPACING * ROOT_LOG2E)
            for g in range(groups)
        ]

        def field(f, k):
            return jnp.broadcast_to(fields[f, k, part * blocks:part * blocks + 1, :], (8, 128))

        def step(k, carry):
            seen, total = carry
            thin, speed, source = field(0, k), field(1, k), field(2, k)
            strong = STRENGTH * thin
            seen_next, total_next = [], []
            for g in range(groups):
                gap = waves[g] - speed
                depth = thin + strong * jnp.exp2(-(gap * gap))
                after = seen[g] * jnp.exp2(depth)
                total_next.append(total[g] + source * (seen[g] - after))
                seen_next.append(after)
            return tuple(seen_next), tuple(total_next)

        ones = tuple(jnp.ones((8, 128), F32) for _ in range(groups))
        zeros = tuple(jnp.zeros((8, 128), F32) for _ in range(groups))
        seen, total = lax.fori_loop(0, positions, step, (ones, zeros), unroll=8)
        last = field(2, positions - 1)
        value = jnp.concatenate([total[g] + last * seen[g] for g in range(groups)], axis=0)
        intensity[part * 128:(part + 1) * 128, :] = value.T

    for copy in out_copies:
        copy.wait()


def per_device(plan, density, momentum, magnetic, energy, shifts, levels):
    cells, width, cross = density.shape
    slabs = plan.slabs
    any_spec = pl.BlockSpec(memory_space=pl.ANY)
    scalars = pl.BlockSpec(memory_space=pltpu.SMEM)
    vmem = pl.BlockSpec(memory_space=pltpu.VMEM)
    state_shape = (8, cells, width, cross)
    lines_shape = (slabs, plan.packed, plan.rows, 128)
    parts, spans = len(plan.groups), len(plan.spans)
    state, lines, order = pl.pallas_call(
        functools.partial(section_kernel, plan),
        out_shape=(
            pltpu.VMEM(state_shape, F32),
            pltpu.VMEM(lines_shape, F32),
            jax.ShapeDtypeStruct((cells + 3 * plan.positions,), jnp.int32),
        ),
        in_specs=[pl.BlockSpec(memory_space=pltpu.HBM)] * 6,
        out_specs=(vmem, vmem, scalars),
        scratch_shapes=[
            pltpu.SMEM((plan.positions,), jnp.int32),
            pltpu.SMEM((plan.positions,), jnp.int32),
            pltpu.VMEM(state_shape, F32),
            pltpu.VMEM((7, cells, width + 2 * PAD, cross), F32),
            pltpu.VMEM((7, cells + 6, width, cross), F32),
            pltpu.VMEM(state_shape, F32),
            pltpu.VMEM((slabs, plan.packed, width, 128), F32),
            pltpu.VMEM((slabs, plan.packed, width, 128), F32),
            pltpu.SemaphoreType.DMA((6,)),
            pltpu.SemaphoreType.DMA((2, spans)),
            pltpu.SemaphoreType.DMA((2, spans)),
            pltpu.SemaphoreType.DMA((2,)),
            pltpu.SemaphoreType.DMA((2,)),
            pltpu.SemaphoreType.DMA((slabs, parts)),
            pltpu.SemaphoreType.DMA((slabs, parts)),
            pltpu.SemaphoreType.DMA((slabs, plan.count)),
            pltpu.SemaphoreType.DMA((slabs, plan.count)),
        ],
        compiler_params=pltpu.CompilerParams(
            collective_id=0, has_side_effects=True, vmem_limit_bytes=16 << 20
        ),
        name="section",
    )(*(
        pltpu.with_memory_space_constraint(x, pltpu.HBM)
        for x in (levels, shifts, density, momentum, magnetic, energy)
    ))
    lines = pltpu.with_memory_space_constraint(lines, pltpu.VMEM)
    state = pltpu.with_memory_space_constraint(state, pltpu.VMEM)
    new_state, intensity = pl.pallas_call(
        functools.partial(ray_kernel, plan),
        out_shape=(
            jax.ShapeDtypeStruct(state_shape, F32),
            jax.ShapeDtypeStruct((width * plan.lanes, W), F32),
        ),
        in_specs=[scalars, vmem, vmem],
        out_specs=(any_spec, vmem),
        scratch_shapes=[
            pltpu.VMEM((3, plan.positions, width, 128), F32),
            pltpu.SemaphoreType.DMA((cells,)),
        ],
        compiler_params=pltpu.CompilerParams(vmem_limit_bytes=16 << 20),
        name="ray",
    )(order, lines, state)
    intensity = intensity.reshape(width, plan.lanes, W)
    return new_state, jnp.transpose(intensity, (2, 0, 1))


def solution(mesh):
    tiles, slabs = mesh.shape["tile"], mesh.shape["depth"]

    def body(density, momentum, magnetic, energy, shifts, levels):
        cells, width, cross = density.shape
        plan = Plan(tiles, slabs, cells, width, cross, levels.shape[0], 2)
        return per_device(plan, density, momentum, magnetic, energy, shifts, levels)

    return jax.shard_map(
        body,
        mesh=mesh,
        in_specs=(
            P("depth", "tile", None),
            P(None, "depth", "tile", None),
            P(None, "depth", "tile", None),
            P("depth", "tile", None),
            P(),
            P(),
        ),
        out_specs=(P(None, "depth", "tile", None), P(None, "tile", "depth")),
        check_vma=False,
    )
```

```python
import functools
import math

import jax
import jax.numpy as jnp
from jax import lax
from jax.experimental import pallas as pl
from jax.experimental.pallas import tpu as pltpu
from jax.sharding import PartitionSpec as P

W = 48
MOST = 8
GAMMA = 5.0 / 3.0
SECTION = 0.02
GRAVITY = 0.5
SIN_VIEW = 0.8660254037844386
COS_VIEW = 0.5
STRENGTH = 4.0
SPACING = 0.25
LOG2E = 1.4426950408889634
ROOT_LOG2E = math.sqrt(LOG2E)
F32 = jnp.float32
MESH = pl.DeviceIdType.MESH
PAD = 8


def column_shift(level):
    return (1732 * level + 1000) // 2000


def softplus(a):
    return jnp.maximum(a, 0.0) + jnp.log1p(jnp.exp(-jnp.abs(a)))


class Plan:
    def __init__(self, tiles, slabs, depth_cells, width, cross, positions, parts):
        self.tiles, self.slabs = tiles, slabs
        self.depth_cells, self.width, self.cross = depth_cells, width, cross
        self.positions = positions
        self.most = min(MOST, depth_cells)
        self.lanes = cross // slabs
        self.blocks = 128 // self.lanes
        self.items = 3 * self.most
        self.packed = -(-self.items // self.blocks)
        self.low = [column_shift(d * depth_cells) for d in range(slabs)]
        high = [column_shift((d + 1) * depth_cells - 1) for d in range(slabs)]
        self.rows = -(-(max(h - l for l, h in zip(self.low, high)) + width) // 8) * 8
        parts = min(parts, self.packed)
        cuts = [self.packed * i // parts for i in range(parts + 1)]
        self.groups = list(zip(cuts[:-1], cuts[1:]))
        self.spans = [(0, self.most)]
        if depth_cells > self.most:
            self.spans.append((self.most, depth_cells))
        self.core = width - 6
        self.pieces = []
        for d in range(slabs):
            mine = []
            for group, (start, stop) in enumerate(self.groups):
                slot_low = start * self.blocks // 3
                slot_high = min(self.most - 1, (stop * self.blocks - 1) // 3)
                low = column_shift(d * depth_cells + slot_low)
                high = column_shift(d * depth_cells + depth_cells - self.most + slot_high)
                for o in range(low // width, (high + width - 1) // width + 1):
                    for kind, left, right in ((0, 3, width - 3), (1, 0, 3), (1, width - 3, width)):
                        first = max(left, low - width * o)
                        last = min(right, high + width - width * o)
                        if last > first:
                            at = width * o + first - self.low[d]
                            row = first - (3 if kind == 0 else left and width - 8)
                            mine.append((o, group, row, last - first, at, kind))
            self.pieces.append(mine)
        self.count = max(len(p) for p in self.pieces)
        self.reach = sorted({p[0] for mine in self.pieces for p in mine if p[0] % tiles})


def slab_start(levels, lowest, positions):
    ahead = jnp.int32(0)
    for k in range(positions):
        ahead = ahead + jnp.where(levels[k] < lowest, 1, 0)
    return ahead


def level_order(plan, levels, d, order):
    cells, most, positions = plan.depth_cells, plan.most, plan.positions
    lowest = d * cells
    ahead = slab_start(levels, lowest, positions)
    held = slab_start(levels, lowest + cells, positions) - ahead
    spare = most - held
    used = [
        jnp.where(
            i < held, levels[jnp.minimum(ahead + i, positions - 1)] - lowest, 2 * cells
        )
        for i in range(most)
    ]

    def free(rank):
        level = rank
        for one in used:
            level = level + jnp.where(one <= level, 1, 0)
        return level

    full = jnp.where(spare > 0, free(spare - 1) + 1, 0)
    for j in range(most):
        later = levels[jnp.clip(ahead + j - spare, 0, positions - 1)] - lowest
        order[j] = jnp.clip(jnp.where(j < full, j, later), 0, cells - 1)
    for j in range(cells - most):
        order[most + j] = jnp.clip(free(spare + j), 0, cells - 1)


def ray_order(plan, levels, shifts, order):
    cells, most, positions = plan.depth_cells, plan.most, plan.positions
    slab = [levels[k] // cells for k in range(positions)]
    before = [jnp.int32(0)]
    for k in range(1, positions):
        before.append(jnp.where(slab[k] == slab[k - 1], before[-1] + 1, 0))
    held = [before[-1] + 1]
    for k in range(positions - 2, -1, -1):
        held.insert(0, jnp.where(slab[k] == slab[k + 1], held[0], before[k] + 1))
    for k in range(positions):
        spare = jnp.minimum(most - held[k], levels[k] - slab[k] * cells - before[k])
        at = cells + 3 * k
        order[at] = slab[k]
        order[at + 1] = before[k] + spare
        order[at + 2] = shifts[k] - (1732 * (slab[k] * cells) + 1000) // 2000


def primitives(st, level):
    rho = st[0, level]
    mx, my, mz = st[1, level], st[2, level], st[3, level]
    bx, by, bz = st[4, level], st[5, level], st[6, level]
    en = st[7, level]
    inv = 1.0 / rho
    vx, vy, vz = mx * inv, my * inv, mz * inv
    half_sq = 0.5 * (bx * bx + by * by + bz * bz)
    kinetic = 0.5 * (mx * vx + my * vy + mz * vz)
    total = (GAMMA - 1.0) * (en - kinetic - half_sq) + half_sq
    vb = vx * bx + vy * by + vz * bz
    return rho, (mx, my, mz), (bx, by, bz), (vx, vy, vz), en, total, vb


def flux_along(axis, values):
    rho, m, b, v, en, total, vb = values
    out = [m[axis]]
    for i in range(3):
        term = m[i] * v[axis] - b[i] * b[axis]
        out.append(term + total if i == axis else term)
    for i in range(3):
        if i != axis:
            out.append(v[axis] * b[i] - b[axis] * v[i])
    out.append((en + total) * v[axis] - b[axis] * vb)
    return out


ROWS = ((0, 1, 2, 3, 5, 6, 7), (0, 1, 2, 3, 4, 6, 7), (0, 1, 2, 3, 4, 5, 7))
SCALE = SECTION / 60.0


def stencil(f):
    return SCALE * (45.0 * (f[4] - f[2]) - 9.0 * (f[5] - f[1]) + (f[6] - f[0]))


def section_kernel(
    plan, levels_in, shifts_in, density, momentum, magnetic, energy, ns, recv, order,
    levels, shifts, st, xf, zf, part, pack, rim_pack, held, rim_held,
    in_sem, xs_sem, xr_sem, zs_sem, zr_sem, ds_sem, dr_sem, ls_sem, lr_sem,
):
    tiles, slabs, cells, width = plan.tiles, plan.slabs, plan.depth_cells, plan.width
    most = plan.most
    t = lax.axis_index("tile")
    d = lax.axis_index("depth")
    right = lax.rem(t + 1, tiles)
    left = lax.rem(t + tiles - 1, tiles)

    loads = [
        pltpu.make_async_copy(density, st.at[0], in_sem.at[0]),
        pltpu.make_async_copy(momentum, st.at[1:4], in_sem.at[1]),
        pltpu.make_async_copy(magnetic, st.at[4:7], in_sem.at[2]),
        pltpu.make_async_copy(energy, st.at[7], in_sem.at[3]),
    ]
    index_loads = [
        pltpu.make_async_copy(levels_in, levels, in_sem.at[4]),
        pltpu.make_async_copy(shifts_in, shifts, in_sem.at[5]),
    ]
    for load in index_loads + loads:
        load.start()

    barrier = pltpu.get_barrier_semaphore()

    def greet(tile, depth):
        pl.semaphore_signal(barrier, inc=1, device_id=(tile, depth), device_id_type=MESH)

    greet(right, d)
    greet(left, d)
    for i in range(1, slabs):
        greet(t, lax.rem(d + i, slabs))
    for o in plan.reach:
        greet(lax.rem(t + o, tiles), d)

    for load in index_loads:
        load.wait()
    level_order(plan, levels, d, order)
    for load in loads:
        load.wait()

    def along_x(slot, carry):
        values = flux_along(0, primitives(st, order[slot]))
        for c in range(7):
            xf[c, slot, PAD:PAD + width, :] = values[c]
        return carry

    def x_copy(side, span):
        src = PAD + width - 3 if side == 0 else PAD
        dst = PAD - 3 if side == 0 else PAD + width
        start, stop = plan.spans[span]
        slots = pl.ds(start, stop - start)
        return pltpu.make_async_remote_copy(
            src_ref=xf.at[:, slots, pl.ds(src, 3), :],
            dst_ref=xf.at[:, slots, pl.ds(dst, 3), :],
            send_sem=xs_sem.at[side, span],
            recv_sem=xr_sem.at[side, span],
            device_id=(right if side == 0 else left, d),
            device_id_type=MESH,
        )

    def z_copy(side):
        src = cells if side == 0 else 3
        dst = 0 if side == 0 else cells + 3
        return pltpu.make_async_remote_copy(
            src_ref=zf.at[:, pl.ds(src, 3)],
            dst_ref=zf.at[:, pl.ds(dst, 3)],
            send_sem=zs_sem.at[side],
            recv_sem=zr_sem.at[side],
            device_id=(t, d + 1 if side == 0 else d - 1),
            device_id_type=MESH,
        )

    spans = len(plan.spans)

    def along_z(level):
        values = flux_along(2, primitives(st, level))
        for c in range(7):
            zf[c, level + 3] = values[c]

    def rim(i, carry):
        along_z(i)
        along_z(cells - 3 + i)
        return carry

    lax.fori_loop(0, 3, rim, 0)
    lax.fori_loop(*plan.spans[0], along_x, 0)
    pl.semaphore_wait(barrier, 2 + (slabs - 1) + len(plan.reach))

    @pl.when(d < slabs - 1)
    def _():
        z_copy(0).start()

    @pl.when(d > 0)
    def _():
        z_copy(1).start()

    x_copy(0, 0).start()
    x_copy(1, 0).start()
    for span in range(1, spans):
        lax.fori_loop(*plan.spans[span], along_x, 0)
        x_copy(0, span).start()
        x_copy(1, span).start()

    def inner(level, carry):
        along_z(level)
        return carry

    lax.fori_loop(3, cells - 3, inner, 0)

    def cross(f):
        def at(step):
            return pltpu.roll(f, (-step) % plan.cross, 1)

        return stencil([at(i - 3) if i != 3 else f for i in range(7)])

    def along_y(level, carry):
        values = primitives(st, level)
        rho, m, b, _, en, _, _ = values
        base = [
            rho, m[0], m[1], m[2] + (SECTION * GRAVITY) * rho, b[0], b[1], b[2],
            en + (SECTION * GRAVITY) * m[2],
        ]
        flux = flux_along(1, values)
        for c, row in enumerate(ROWS[1]):
            base[row] = base[row] - cross(flux[c])
        for row in range(8):
            part[row, level] = base[row]
        return carry

    lax.fori_loop(0, cells, along_y, 0)

    @pl.when(d == 0)
    def _():
        for c in range(7):
            edge = zf[c, 3]
            for i in range(3):
                zf[c, i] = edge

    @pl.when(d > 0)
    def _():
        z_copy(0).wait_recv()

    @pl.when(d == slabs - 1)
    def _():
        for c in range(7):
            edge = zf[c, cells + 2]
            for i in range(3):
                zf[c, cells + 3 + i] = edge

    @pl.when(d < slabs - 1)
    def _():
        z_copy(1).wait_recv()

    def depth_part(level, carry):
        for c, row in enumerate(ROWS[2]):
            part[row, level] = part[row, level] - stencil([zf[c, level + i] for i in range(7)])
        return carry

    lax.fori_loop(0, cells, depth_part, 0)
    ray_order(plan, levels, shifts, order)

    def finish(slot):
        level = order[slot]
        row_of = {row: c for c, row in enumerate(ROWS[0])}
        out = []
        for row in range(8):
            value = part[row, level]
            if row in row_of:
                c = row_of[row]
                value = value - stencil(
                    [xf[c, slot, pl.ds(PAD - 3 + i, width), :] for i in range(7)]
                )
            ns[row, slot] = value
            out.append(value)
        return out

    def emit(new, out, height):
        block_of = lax.broadcasted_iota(jnp.int32, (height, 128), 1) // plan.lanes
        for slot in range(most):
            rho, mx, mz, bx, by, bz, en = new(slot)
            dens = 0.5 + softplus(rho)
            inv = 1.0 / dens
            speed = (COS_VIEW * mz + SIN_VIEW * mx) * inv
            source = softplus(en - 0.5 * (bx * bx + by * by + bz * bz)) * inv
            for f, value in enumerate((dens, speed, source)):
                item = 3 * slot + f
                row, block = item // plan.blocks, item % plan.blocks
                for target in range(slabs):
                    shift = ((block - target) * plan.lanes) % 128
                    moved = pltpu.roll(value, shift, 1) if shift else value
                    if block:
                        moved = jnp.where(block_of == block, moved, rows[target, row])
                    rows[target, row] = moved
                    if block == plan.blocks - 1 or item == plan.items - 1:
                        out[target, row] = rows.pop((target, row))

    rows = {}
    cores = 2 if slabs % 2 == 0 else 1

    def peer(step, sign):
        chip, core = d // cores, lax.rem(d, cores)
        far, flip = step // cores, step % cores
        chips = slabs // cores
        return lax.rem(chip + chips + sign * far, chips) * cores + (1 - core if flip else core)

    def depth_copy(step, kind):
        source, target = (rim_pack, rim_held) if kind else (pack, held)
        if step == 0:
            return pltpu.make_async_copy(source.at[d], target.at[d], dr_sem.at[0, kind])
        to = peer(step, 1)
        return pltpu.make_async_remote_copy(
            src_ref=source.at[to],
            dst_ref=target.at[d],
            send_sem=ds_sem.at[step, kind],
            recv_sem=dr_sem.at[step, kind],
            device_id=(t, to),
            device_id_type=MESH,
        )

    def line_copy(source, n):
        o, group, first, size, at, kind = plan.pieces[source][n]
        start, stop = plan.groups[group]
        origin = rim_held if kind else held
        src = origin.at[source, pl.ds(start, stop - start), pl.ds(first, size), :]
        dst = recv.at[source, pl.ds(start, stop - start), pl.ds(at, size), :]
        if o % tiles == 0:
            return pltpu.make_async_copy(src, dst, lr_sem.at[source, n]), False
        return pltpu.make_async_remote_copy(
            src_ref=src,
            dst_ref=dst,
            send_sem=ls_sem.at[source, n],
            recv_sem=lr_sem.at[source, n],
            device_id=(lax.rem(t + tiles - o % tiles, tiles), d),
            device_id_type=MESH,
        ), True

    def forward(slab, kind):
        for source in range(slabs):

            @pl.when(slab == source)
            def _():
                for n, piece in enumerate(plan.pieces[source]):
                    if piece[5] == kind:
                        line_copy(source, n)[0].start()

    line_rows = (0, 1, 3, 4, 5, 6, 7)
    x_row = {row: c for c, row in enumerate(ROWS[0])}

    def core_state(slot):
        level = order[slot]
        out = []
        for row in line_rows:
            value = part[row, level, 3:width - 3, :]
            if row in x_row:
                value = value - stencil(
                    [xf[x_row[row], slot, pl.ds(PAD + i, plan.core), :] for i in range(7)]
                )
            out.append(value)
        return out

    emit(core_state, pack, plan.core)
    for step in range(slabs):
        depth_copy(step, 0).start()
    for step in range(slabs):
        if step:
            depth_copy(step, 0).wait_recv()
        else:
            depth_copy(step, 0).wait()
        forward(peer(step, -1), 0)

    x_copy(0, 0).wait_recv()
    x_copy(1, 0).wait_recv()
    low_rows = lax.broadcasted_iota(jnp.int32, (8, 128), 0) < 3

    def rim_state(slot):
        new = finish(slot)
        return [
            jnp.where(low_rows, new[row][:8], new[row][width - 8:]) for row in line_rows
        ]

    emit(rim_state, rim_pack, 8)
    for step in range(slabs):
        depth_copy(step, 1).start()
    for step in range(slabs):
        if step:
            depth_copy(step, 1).wait_recv()
        else:
            depth_copy(step, 1).wait()
        forward(peer(step, -1), 1)

    def rest(slot, carry):
        finish(slot)
        return carry

    for span in range(1, spans):
        x_copy(0, span).wait_recv()
        x_copy(1, span).wait_recv()
        lax.fori_loop(*plan.spans[span], rest, 0)

    for source in range(slabs):
        for n in range(len(plan.pieces[source])):
            copy, remote = line_copy(source, n)
            if remote:
                copy.wait_recv()
            else:
                copy.wait()

    for span in range(spans):
        x_copy(0, span).wait_send()
        x_copy(1, span).wait_send()

    @pl.when(d < slabs - 1)
    def _():
        z_copy(0).wait_send()

    @pl.when(d > 0)
    def _():
        z_copy(1).wait_send()

    for kind in range(2):
        for step in range(1, slabs):
            depth_copy(step, kind).wait_send()
    for source in range(slabs):
        for n in range(len(plan.pieces[source])):
            copy, remote = line_copy(source, n)
            if remote:
                copy.wait_send()


def ray_kernel(plan, order, rows, hold, state_out, intensity, fields, out_sem):
    cells, width, blocks = plan.depth_cells, plan.width, plan.blocks
    lanes, positions = plan.lanes, plan.positions
    out_copies = [
        pltpu.make_async_copy(hold.at[:, j], state_out.at[:, order[j]], out_sem.at[j])
        for j in range(cells)
    ]
    for copy in out_copies:
        copy.start()

    lane = lax.broadcasted_iota(jnp.int32, (width, 128), 1)
    within = lax.rem(lane, lanes)
    wanted = lane // lanes == lax.rem(
        lax.broadcasted_iota(jnp.int32, (width, 128), 0), blocks
    )
    for k in range(positions):
        at = cells + 3 * k
        slab, slot, start = order[at], order[at + 1], order[at + 2]
        for f in range(3):
            item = 3 * slot + f
            row, block = item // blocks, lax.rem(item, blocks)
            value = rows[slab, row, pl.ds(start, width), :]
            value = jnp.take_along_axis(value, within + block * lanes, axis=1)
            value = jnp.where(wanted, value, 0.0)
            step = 1
            while step < blocks:
                value = value + pltpu.roll(value, width - step, 0)
                step *= 2
            if f == 0:
                value = value * (-LOG2E * 2.0 / positions)
            elif f == 1:
                value = value * ROOT_LOG2E
            fields[f, k] = value

    groups = W // 8
    for part in range(width // blocks):
        waves = [
            (
                (8 * g + lax.broadcasted_iota(jnp.int32, (8, 128), 0)).astype(F32)
                - 0.5 * (W - 1)
            )
            * (SPACING * ROOT_LOG2E)
            for g in range(groups)
        ]

        def field(f, k):
            return jnp.broadcast_to(fields[f, k, part * blocks:part * blocks + 1, :], (8, 128))

        def step(k, carry):
            seen, total = carry
            thin, speed, source = field(0, k), field(1, k), field(2, k)
            strong = STRENGTH * thin
            seen_next, total_next = [], []
            for g in range(groups):
                gap = waves[g] - speed
                depth = thin + strong * jnp.exp2(-(gap * gap))
                after = seen[g] * jnp.exp2(depth)
                total_next.append(total[g] + source * (seen[g] - after))
                seen_next.append(after)
            return tuple(seen_next), tuple(total_next)

        ones = tuple(jnp.ones((8, 128), F32) for _ in range(groups))
        zeros = tuple(jnp.zeros((8, 128), F32) for _ in range(groups))
        seen, total = lax.fori_loop(0, positions, step, (ones, zeros), unroll=8)
        last = field(2, positions - 1)
        value = jnp.concatenate([total[g] + last * seen[g] for g in range(groups)], axis=0)
        intensity[part * 128:(part + 1) * 128, :] = value.T

    for copy in out_copies:
        copy.wait()


def per_device(plan, density, momentum, magnetic, energy, shifts, levels):
    cells, width, cross = density.shape
    slabs = plan.slabs
    any_spec = pl.BlockSpec(memory_space=pl.ANY)
    scalars = pl.BlockSpec(memory_space=pltpu.SMEM)
    vmem = pl.BlockSpec(memory_space=pltpu.VMEM)
    state_shape = (8, cells, width, cross)
    lines_shape = (slabs, plan.packed, plan.rows, 128)
    spans = len(plan.spans)
    state, lines, order = pl.pallas_call(
        functools.partial(section_kernel, plan),
        out_shape=(
            pltpu.VMEM(state_shape, F32),
            pltpu.VMEM(lines_shape, F32),
            jax.ShapeDtypeStruct((cells + 3 * plan.positions,), jnp.int32),
        ),
        in_specs=[pl.BlockSpec(memory_space=pltpu.HBM)] * 6,
        out_specs=(vmem, vmem, scalars),
        scratch_shapes=[
            pltpu.SMEM((plan.positions,), jnp.int32),
            pltpu.SMEM((plan.positions,), jnp.int32),
            pltpu.VMEM(state_shape, F32),
            pltpu.VMEM((7, cells, width + 2 * PAD, cross), F32),
            pltpu.VMEM((7, cells + 6, width, cross), F32),
            pltpu.VMEM(state_shape, F32),
            pltpu.VMEM((slabs, plan.packed, plan.core, 128), F32),
            pltpu.VMEM((slabs, plan.packed, 8, 128), F32),
            pltpu.VMEM((slabs, plan.packed, plan.core, 128), F32),
            pltpu.VMEM((slabs, plan.packed, 8, 128), F32),
            pltpu.SemaphoreType.DMA((6,)),
            pltpu.SemaphoreType.DMA((2, spans)),
            pltpu.SemaphoreType.DMA((2, spans)),
            pltpu.SemaphoreType.DMA((2,)),
            pltpu.SemaphoreType.DMA((2,)),
            pltpu.SemaphoreType.DMA((slabs, 2)),
            pltpu.SemaphoreType.DMA((slabs, 2)),
            pltpu.SemaphoreType.DMA((slabs, plan.count)),
            pltpu.SemaphoreType.DMA((slabs, plan.count)),
        ],
        compiler_params=pltpu.CompilerParams(
            collective_id=0, has_side_effects=True, vmem_limit_bytes=16 << 20
        ),
        name="section",
    )(*(
        pltpu.with_memory_space_constraint(x, pltpu.HBM)
        for x in (levels, shifts, density, momentum, magnetic, energy)
    ))
    lines = pltpu.with_memory_space_constraint(lines, pltpu.VMEM)
    state = pltpu.with_memory_space_constraint(state, pltpu.VMEM)
    new_state, intensity = pl.pallas_call(
        functools.partial(ray_kernel, plan),
        out_shape=(
            jax.ShapeDtypeStruct(state_shape, F32),
            jax.ShapeDtypeStruct((width * plan.lanes, W), F32),
        ),
        in_specs=[scalars, vmem, vmem],
        out_specs=(any_spec, vmem),
        scratch_shapes=[
            pltpu.VMEM((3, plan.positions, width, 128), F32),
            pltpu.SemaphoreType.DMA((cells,)),
        ],
        compiler_params=pltpu.CompilerParams(vmem_limit_bytes=16 << 20),
        name="ray",
    )(order, lines, state)
    intensity = intensity.reshape(width, plan.lanes, W)
    return new_state, jnp.transpose(intensity, (2, 0, 1))


def solution(mesh):
    tiles, slabs = mesh.shape["tile"], mesh.shape["depth"]

    def body(density, momentum, magnetic, energy, shifts, levels):
        cells, width, cross = density.shape
        plan = Plan(tiles, slabs, cells, width, cross, levels.shape[0], 1)
        return per_device(plan, density, momentum, magnetic, energy, shifts, levels)

    return jax.shard_map(
        body,
        mesh=mesh,
        in_specs=(
            P("depth", "tile", None),
            P(None, "depth", "tile", None),
            P(None, "depth", "tile", None),
            P("depth", "tile", None),
            P(),
            P(),
        ),
        out_specs=(P(None, "depth", "tile", None), P(None, "tile", "depth")),
        check_vma=False,
    )
```

```python
import functools
import math

import jax
import jax.numpy as jnp
from jax import lax
from jax.experimental import pallas as pl
from jax.experimental.pallas import tpu as pltpu
from jax.sharding import PartitionSpec as P

W = 48
MOST = 8
GAMMA = 5.0 / 3.0
SECTION = 0.02
GRAVITY = 0.5
SIN_VIEW = 0.8660254037844386
COS_VIEW = 0.5
STRENGTH = 4.0
SPACING = 0.25
LOG2E = 1.4426950408889634
ROOT_LOG2E = math.sqrt(LOG2E)
F32 = jnp.float32
MESH = pl.DeviceIdType.MESH
PAD = 8


def column_shift(level):
    return (1732 * level + 1000) // 2000


def softplus(a):
    return jnp.maximum(a, 0.0) + jnp.log1p(jnp.exp(-jnp.abs(a)))


class Plan:
    def __init__(self, tiles, slabs, depth_cells, width, cross, positions, parts):
        self.tiles, self.slabs = tiles, slabs
        self.depth_cells, self.width, self.cross = depth_cells, width, cross
        self.positions = positions
        self.most = min(MOST, depth_cells)
        self.lanes = cross // slabs
        self.blocks = 128 // self.lanes
        self.items = 3 * self.most
        self.packed = -(-self.items // self.blocks)
        self.low = [column_shift(d * depth_cells) for d in range(slabs)]
        high = [column_shift((d + 1) * depth_cells - 1) for d in range(slabs)]
        self.rows = -(-(max(h - l for l, h in zip(self.low, high)) + width) // 8) * 8
        parts = min(parts, self.packed)
        cuts = [self.packed * i // parts for i in range(parts + 1)]
        self.groups = list(zip(cuts[:-1], cuts[1:]))
        self.spans = [(0, self.most)]
        if depth_cells > self.most:
            self.spans.append((self.most, depth_cells))
        self.core = width - 6
        self.pieces = []
        for d in range(slabs):
            mine = []
            for group, (start, stop) in enumerate(self.groups):
                slot_low = start * self.blocks // 3
                slot_high = min(self.most - 1, (stop * self.blocks - 1) // 3)
                low = column_shift(d * depth_cells + slot_low)
                high = column_shift(d * depth_cells + depth_cells - self.most + slot_high)
                for o in range(low // width, (high + width - 1) // width + 1):
                    for kind, left, right in ((0, 3, width - 3), (1, 0, 3), (1, width - 3, width)):
                        first = max(left, low - width * o)
                        last = min(right, high + width - width * o)
                        if last > first:
                            at = width * o + first - self.low[d]
                            row = first - (3 if kind == 0 else left and width - 8)
                            mine.append((o, group, row, last - first, at, kind))
            self.pieces.append(mine)
        self.count = max(len(p) for p in self.pieces)
        self.reach = sorted({p[0] for mine in self.pieces for p in mine if p[0] % tiles})


def slab_start(levels, lowest, positions):
    ahead = jnp.int32(0)
    for k in range(positions):
        ahead = ahead + jnp.where(levels[k] < lowest, 1, 0)
    return ahead


def level_order(plan, levels, d, order):
    cells, most, positions = plan.depth_cells, plan.most, plan.positions
    lowest = d * cells
    ahead = slab_start(levels, lowest, positions)
    held = slab_start(levels, lowest + cells, positions) - ahead
    spare = most - held
    used = [
        jnp.where(
            i < held, levels[jnp.minimum(ahead + i, positions - 1)] - lowest, 2 * cells
        )
        for i in range(most)
    ]

    def free(rank):
        level = rank
        for one in used:
            level = level + jnp.where(one <= level, 1, 0)
        return level

    full = jnp.where(spare > 0, free(spare - 1) + 1, 0)
    for j in range(most):
        later = levels[jnp.clip(ahead + j - spare, 0, positions - 1)] - lowest
        order[j] = jnp.clip(jnp.where(j < full, j, later), 0, cells - 1)
    for j in range(cells - most):
        order[most + j] = jnp.clip(free(spare + j), 0, cells - 1)


def ray_order(plan, levels, shifts, order):
    cells, most, positions = plan.depth_cells, plan.most, plan.positions
    slab = [levels[k] // cells for k in range(positions)]
    before = [jnp.int32(0)]
    for k in range(1, positions):
        before.append(jnp.where(slab[k] == slab[k - 1], before[-1] + 1, 0))
    held = [before[-1] + 1]
    for k in range(positions - 2, -1, -1):
        held.insert(0, jnp.where(slab[k] == slab[k + 1], held[0], before[k] + 1))
    for k in range(positions):
        spare = jnp.minimum(most - held[k], levels[k] - slab[k] * cells - before[k])
        at = cells + 3 * k
        order[at] = slab[k]
        order[at + 1] = before[k] + spare
        order[at + 2] = shifts[k] - (1732 * (slab[k] * cells) + 1000) // 2000


def primitives(st, level):
    rho = st[0, level]
    mx, my, mz = st[1, level], st[2, level], st[3, level]
    bx, by, bz = st[4, level], st[5, level], st[6, level]
    en = st[7, level]
    inv = 1.0 / rho
    vx, vy, vz = mx * inv, my * inv, mz * inv
    half_sq = 0.5 * (bx * bx + by * by + bz * bz)
    kinetic = 0.5 * (mx * vx + my * vy + mz * vz)
    total = (GAMMA - 1.0) * (en - kinetic - half_sq) + half_sq
    vb = vx * bx + vy * by + vz * bz
    return rho, (mx, my, mz), (bx, by, bz), (vx, vy, vz), en, total, vb


def flux_along(axis, values):
    rho, m, b, v, en, total, vb = values
    out = [m[axis]]
    for i in range(3):
        term = m[i] * v[axis] - b[i] * b[axis]
        out.append(term + total if i == axis else term)
    for i in range(3):
        if i != axis:
            out.append(v[axis] * b[i] - b[axis] * v[i])
    out.append((en + total) * v[axis] - b[axis] * vb)
    return out


ROWS = ((0, 1, 2, 3, 5, 6, 7), (0, 1, 2, 3, 4, 6, 7), (0, 1, 2, 3, 4, 5, 7))
SCALE = SECTION / 60.0


def stencil(f):
    return SCALE * (45.0 * (f[4] - f[2]) - 9.0 * (f[5] - f[1]) + (f[6] - f[0]))


def section_kernel(
    plan, levels_in, shifts_in, density, momentum, magnetic, energy, ns, recv, order,
    levels, shifts, st, xf, yf, zf, part, pack, rim_pack, held, rim_held,
    in_sem, xs_sem, xr_sem, zs_sem, zr_sem, ds_sem, dr_sem, ls_sem, lr_sem,
    rs_sem,
):
    tiles, slabs, cells, width = plan.tiles, plan.slabs, plan.depth_cells, plan.width
    most = plan.most
    t = lax.axis_index("tile")
    d = lax.axis_index("depth")
    right = lax.rem(t + 1, tiles)
    left = lax.rem(t + tiles - 1, tiles)

    loads = [
        pltpu.make_async_copy(density, st.at[0], in_sem.at[0]),
        pltpu.make_async_copy(momentum, st.at[1:4], in_sem.at[1]),
        pltpu.make_async_copy(magnetic, st.at[4:7], in_sem.at[2]),
        pltpu.make_async_copy(energy, st.at[7], in_sem.at[3]),
    ]
    index_loads = [
        pltpu.make_async_copy(levels_in, levels, in_sem.at[4]),
        pltpu.make_async_copy(shifts_in, shifts, in_sem.at[5]),
    ]
    for load in index_loads + loads:
        load.start()

    barrier = pltpu.get_barrier_semaphore()

    def greet(tile, depth):
        pl.semaphore_signal(barrier, inc=1, device_id=(tile, depth), device_id_type=MESH)

    greet(right, d)
    greet(left, d)
    for i in range(1, slabs):
        greet(t, lax.rem(d + i, slabs))
    for o in plan.reach:
        greet(lax.rem(t + o, tiles), d)

    for load in index_loads:
        load.wait()
    level_order(plan, levels, d, order)
    for load in loads:
        load.wait()

    def along_x(slot, carry):
        values = flux_along(0, primitives(st, order[slot]))
        for c in range(7):
            xf[c, slot, PAD:PAD + width, :] = values[c]
        return carry

    def x_copy(side, span):
        src = PAD + width - 3 if side == 0 else PAD
        dst = PAD - 3 if side == 0 else PAD + width
        start, stop = plan.spans[span]
        slots = pl.ds(start, stop - start)
        return pltpu.make_async_remote_copy(
            src_ref=xf.at[:, slots, pl.ds(src, 3), :],
            dst_ref=xf.at[:, slots, pl.ds(dst, 3), :],
            send_sem=xs_sem.at[side, span],
            recv_sem=xr_sem.at[side, span],
            device_id=(right if side == 0 else left, d),
            device_id_type=MESH,
        )

    def z_copy(side):
        src = cells if side == 0 else 3
        dst = 0 if side == 0 else cells + 3
        return pltpu.make_async_remote_copy(
            src_ref=zf.at[:, pl.ds(src, 3)],
            dst_ref=zf.at[:, pl.ds(dst, 3)],
            send_sem=zs_sem.at[side],
            recv_sem=zr_sem.at[side],
            device_id=(t, d + 1 if side == 0 else d - 1),
            device_id_type=MESH,
        )

    spans = len(plan.spans)

    def along_y(level, carry):
        values = primitives(st, level)
        rho, m, b, _, en, _, _ = values
        base = [
            rho, m[0], m[1], m[2] + (SECTION * GRAVITY) * rho, b[0], b[1], b[2],
            en + (SECTION * GRAVITY) * m[2],
        ]
        for row in range(8):
            part[row, level] = base[row]
        for c, f in enumerate(flux_along(1, values)):
            high = f.astype(jnp.bfloat16)
            yf[c, level, :, :plan.cross] = high
            yf[c, level, :, plan.cross:] = (f - high.astype(F32)).astype(jnp.bfloat16)
        return carry

    def cross():
        shape = (2 * plan.cross, plan.cross)
        ahead = lax.broadcasted_iota(jnp.int32, shape, 0) - lax.broadcasted_iota(
            jnp.int32, shape, 1
        )
        ahead = lax.rem(ahead + plan.cross, plan.cross)
        band = jnp.zeros(shape, F32)
        for i, weight in ((1, 45.0), (2, -9.0), (3, 1.0)):
            band = jnp.where(ahead == i, weight, band)
            band = jnp.where(ahead == plan.cross - i, -weight, band)
        band = band.astype(jnp.bfloat16)
        for c, row in enumerate(ROWS[1]):
            flat = yf[c].reshape(cells * width, 2 * plan.cross)
            slope = jnp.dot(flat, band, preferred_element_type=F32)
            part[row] = part[row] - SCALE * slope.reshape(cells, width, plan.cross)

    def all_y():
        lax.fori_loop(0, cells, along_y, 0)
        cross()

    def early(work):
        pass

    def late(work):
        work()

    def along_z(level):
        values = flux_along(2, primitives(st, level))
        for c in range(7):
            zf[c, level + 3] = values[c]

    def rim(i, carry):
        along_z(i)
        along_z(cells - 3 + i)
        return carry

    lax.fori_loop(0, 3, rim, 0)
    lax.fori_loop(*plan.spans[0], along_x, 0)
    early(all_y)
    pl.semaphore_wait(barrier, 2 + (slabs - 1) + len(plan.reach))

    @pl.when(d < slabs - 1)
    def _():
        z_copy(0).start()

    @pl.when(d > 0)
    def _():
        z_copy(1).start()

    x_copy(0, 0).start()
    x_copy(1, 0).start()
    for span in range(1, spans):
        lax.fori_loop(*plan.spans[span], along_x, 0)
        x_copy(0, span).start()
        x_copy(1, span).start()

    def inner(level, carry):
        along_z(level)
        return carry

    lax.fori_loop(3, cells - 3, inner, 0)

    late(all_y)

    @pl.when(d == 0)
    def _():
        for c in range(7):
            edge = zf[c, 3]
            for i in range(3):
                zf[c, i] = edge

    @pl.when(d > 0)
    def _():
        z_copy(0).wait_recv()

    @pl.when(d == slabs - 1)
    def _():
        for c in range(7):
            edge = zf[c, cells + 2]
            for i in range(3):
                zf[c, cells + 3 + i] = edge

    @pl.when(d < slabs - 1)
    def _():
        z_copy(1).wait_recv()

    def depth_part(level, carry):
        for c, row in enumerate(ROWS[2]):
            part[row, level] = part[row, level] - stencil([zf[c, level + i] for i in range(7)])
        return carry

    lax.fori_loop(0, cells, depth_part, 0)
    ray_order(plan, levels, shifts, order)

    def finish(slot):
        level = order[slot]
        row_of = {row: c for c, row in enumerate(ROWS[0])}
        out = []
        for row in range(8):
            value = part[row, level]
            if row in row_of:
                c = row_of[row]
                value = value - stencil(
                    [xf[c, slot, pl.ds(PAD - 3 + i, width), :] for i in range(7)]
                )
            ns[row, slot] = value
            out.append(value)
        return out

    def emit(new, out, height):
        block_of = lax.broadcasted_iota(jnp.int32, (height, 128), 1) // plan.lanes
        for slot in range(most):
            rho, mx, mz, bx, by, bz, en = new(slot)
            dens = 0.5 + softplus(rho)
            inv = 1.0 / dens
            speed = (COS_VIEW * mz + SIN_VIEW * mx) * inv
            source = softplus(en - 0.5 * (bx * bx + by * by + bz * bz)) * inv
            for f, value in enumerate((dens, speed, source)):
                item = 3 * slot + f
                row, block = item // plan.blocks, item % plan.blocks
                for target in range(slabs):
                    shift = ((block - target) * plan.lanes) % 128
                    moved = pltpu.roll(value, shift, 1) if shift else value
                    if block:
                        moved = jnp.where(block_of == block, moved, rows[target, row])
                    rows[target, row] = moved
                    if block == plan.blocks - 1 or item == plan.items - 1:
                        out[target, row] = rows.pop((target, row))

    rows = {}
    cores = 2 if slabs % 2 == 0 else 1

    def peer(step, sign):
        chip, core = d // cores, lax.rem(d, cores)
        far, flip = step // cores, step % cores
        chips = slabs // cores
        return lax.rem(chip + chips + sign * far, chips) * cores + (1 - core if flip else core)

    def depth_copy(step, kind):
        source, target = (rim_pack, rim_held) if kind else (pack, held)
        to = peer(step, 1)
        return pltpu.make_async_remote_copy(
            src_ref=source.at[to],
            dst_ref=target.at[d],
            send_sem=ds_sem.at[step, kind],
            recv_sem=dr_sem.at[step, kind],
            device_id=(t, to),
            device_id_type=MESH,
        )

    def line_copy(source, n, own=False):
        o, group, first, size, at, kind = plan.pieces[source][n]
        start, stop = plan.groups[group]
        if own:
            origin = rim_pack if kind else pack
        else:
            origin = rim_held if kind else held
        return pltpu.make_async_remote_copy(
            src_ref=origin.at[source, pl.ds(start, stop - start), pl.ds(first, size), :],
            dst_ref=recv.at[source, pl.ds(start, stop - start), pl.ds(at, size), :],
            send_sem=ls_sem.at[source, n],
            recv_sem=lr_sem.at[source, n],
            device_id=(lax.rem(t + tiles - o % tiles, tiles), d),
            device_id_type=MESH,
        )

    def rim_copy(source, n, target):
        o, group, first, size, at, _ = plan.pieces[source][n]
        start, stop = plan.groups[group]
        return pltpu.make_async_remote_copy(
            src_ref=rim_pack.at[target, pl.ds(start, stop - start), pl.ds(first, size), :],
            dst_ref=recv.at[source, pl.ds(start, stop - start), pl.ds(at, size), :],
            send_sem=rs_sem.at[n, target],
            recv_sem=lr_sem.at[source, n],
            device_id=(lax.rem(t + tiles - o % tiles, tiles), target),
            device_id_type=MESH,
        )

    def keep(source, n, own):
        _, group, first, size, at, kind = plan.pieces[source][n]
        start, stop = plan.groups[group]
        if own:
            origin = rim_pack if kind else pack
        else:
            origin = rim_held if kind else held
        for row in range(start, stop):
            recv[source, row, at:at + size, :] = origin[source, row, first:first + size, :]

    def forward(slab, kind, own=False):
        for source in range(slabs):

            @pl.when(slab == source)
            def _():
                for stays in (False, True):
                    for n, piece in enumerate(plan.pieces[source]):
                        if piece[5] == kind and (piece[0] % tiles == 0) == stays:
                            if stays:
                                keep(source, n, own)
                            else:
                                line_copy(source, n, own).start()

    line_rows = (0, 1, 3, 4, 5, 6, 7)
    x_row = {row: c for c, row in enumerate(ROWS[0])}

    def core_state(slot):
        level = order[slot]
        out = []
        for row in line_rows:
            value = part[row, level, 3:width - 3, :]
            if row in x_row:
                value = value - stencil(
                    [xf[x_row[row], slot, pl.ds(PAD + i, plan.core), :] for i in range(7)]
                )
            out.append(value)
        return out

    emit(core_state, pack, plan.core)
    for step in range(1, slabs):
        depth_copy(step, 0).start()
    forward(d, 0, own=True)
    for step in range(1, slabs):
        depth_copy(step, 0).wait_recv()
        forward(peer(step, -1), 0)

    x_copy(0, 0).wait_recv()
    x_copy(1, 0).wait_recv()
    low_rows = lax.broadcasted_iota(jnp.int32, (8, 128), 0) < 3

    def rim_state(slot):
        new = finish(slot)
        return [
            jnp.where(low_rows, new[row][:8], new[row][width - 8:]) for row in line_rows
        ]

    emit(rim_state, rim_pack, 8)
    rims = [
        (source, n)
        for source in range(slabs)
        for n, piece in enumerate(plan.pieces[source])
        if piece[5] == 1
    ]
    for source in range(slabs):

        @pl.when(d == source)
        def _():
            for one, n in rims:
                if one == source:
                    for target in range(slabs):
                        if target == source and plan.pieces[source][n][0] % tiles == 0:
                            keep(source, n, True)
                        else:
                            rim_copy(source, n, target).start()


    def rest(slot, carry):
        finish(slot)
        return carry

    for span in range(1, spans):
        x_copy(0, span).wait_recv()
        x_copy(1, span).wait_recv()
        lax.fori_loop(*plan.spans[span], rest, 0)

    for source in range(slabs):
        for n in range(len(plan.pieces[source])):
            here = plan.pieces[source][n][0] % tiles == 0
            if plan.pieces[source][n][5] == 1 and here:
                pl.when(d != source)(rim_copy(source, n, source).wait_recv)
            elif plan.pieces[source][n][5] == 1:
                rim_copy(source, n, source).wait_recv()
            elif not here:
                line_copy(source, n).wait_recv()

    for span in range(spans):
        x_copy(0, span).wait_send()
        x_copy(1, span).wait_send()

    @pl.when(d < slabs - 1)
    def _():
        z_copy(0).wait_send()

    @pl.when(d > 0)
    def _():
        z_copy(1).wait_send()

    for step in range(1, slabs):
        depth_copy(step, 0).wait_send()
    for source in range(slabs):
        for n in range(len(plan.pieces[source])):
            if plan.pieces[source][n][0] % tiles and plan.pieces[source][n][5] == 0:
                line_copy(source, n).wait_send()

        @pl.when(d == source)
        def _():
            for one, n in rims:
                if one == source:
                    for target in range(slabs):
                        if not (target == source and plan.pieces[source][n][0] % tiles == 0):
                            rim_copy(source, n, target).wait_send()


def ray_kernel(plan, order, rows, hold, state_out, intensity, fields, out_sem):
    cells, width, blocks = plan.depth_cells, plan.width, plan.blocks
    lanes, positions = plan.lanes, plan.positions
    out_copies = [
        pltpu.make_async_copy(hold.at[:, j], state_out.at[:, order[j]], out_sem.at[j])
        for j in range(cells)
    ]
    for copy in out_copies:
        copy.start()

    lane = lax.broadcasted_iota(jnp.int32, (width, 128), 1)
    within = lax.rem(lane, lanes)
    wanted = lane // lanes == lax.rem(
        lax.broadcasted_iota(jnp.int32, (width, 128), 0), blocks
    )
    for k in range(positions):
        at = cells + 3 * k
        slab, slot, start = order[at], order[at + 1], order[at + 2]
        for f in range(3):
            item = 3 * slot + f
            row, block = item // blocks, lax.rem(item, blocks)
            value = rows[slab, row, pl.ds(start, width), :]
            value = jnp.take_along_axis(value, within + block * lanes, axis=1)
            value = jnp.where(wanted, value, 0.0)
            step = 1
            while step < blocks:
                value = value + pltpu.roll(value, width - step, 0)
                step *= 2
            if f == 0:
                value = value * (-LOG2E * 2.0 / positions)
            elif f == 1:
                value = value * ROOT_LOG2E
            fields[f, k] = value

    groups = W // 8
    for part in range(width // blocks):
        waves = [
            (
                (8 * g + lax.broadcasted_iota(jnp.int32, (8, 128), 0)).astype(F32)
                - 0.5 * (W - 1)
            )
            * (SPACING * ROOT_LOG2E)
            for g in range(groups)
        ]

        def field(f, k):
            return jnp.broadcast_to(fields[f, k, part * blocks:part * blocks + 1, :], (8, 128))

        def step(k, carry):
            seen, total = carry
            thin, speed, source = field(0, k), field(1, k), field(2, k)
            strong = STRENGTH * thin
            seen_next, total_next = [], []
            for g in range(groups):
                gap = waves[g] - speed
                depth = thin + strong * jnp.exp2(-(gap * gap))
                after = seen[g] * jnp.exp2(depth)
                total_next.append(total[g] + source * (seen[g] - after))
                seen_next.append(after)
            return tuple(seen_next), tuple(total_next)

        ones = tuple(jnp.ones((8, 128), F32) for _ in range(groups))
        zeros = tuple(jnp.zeros((8, 128), F32) for _ in range(groups))
        seen, total = lax.fori_loop(0, positions, step, (ones, zeros), unroll=8)
        last = field(2, positions - 1)
        value = jnp.concatenate([total[g] + last * seen[g] for g in range(groups)], axis=0)
        intensity[part * 128:(part + 1) * 128, :] = value.T

    for copy in out_copies:
        copy.wait()


def per_device(plan, density, momentum, magnetic, energy, shifts, levels):
    cells, width, cross = density.shape
    slabs = plan.slabs
    any_spec = pl.BlockSpec(memory_space=pl.ANY)
    scalars = pl.BlockSpec(memory_space=pltpu.SMEM)
    vmem = pl.BlockSpec(memory_space=pltpu.VMEM)
    state_shape = (8, cells, width, cross)
    lines_shape = (slabs, plan.packed, plan.rows, 128)
    spans = len(plan.spans)
    state, lines, order = pl.pallas_call(
        functools.partial(section_kernel, plan),
        out_shape=(
            pltpu.VMEM(state_shape, F32),
            pltpu.VMEM(lines_shape, F32),
            jax.ShapeDtypeStruct((cells + 3 * plan.positions,), jnp.int32),
        ),
        in_specs=[pl.BlockSpec(memory_space=pltpu.HBM)] * 6,
        out_specs=(vmem, vmem, scalars),
        scratch_shapes=[
            pltpu.SMEM((plan.positions,), jnp.int32),
            pltpu.SMEM((plan.positions,), jnp.int32),
            pltpu.VMEM(state_shape, F32),
            pltpu.VMEM((7, cells, width + 2 * PAD, cross), F32),
            pltpu.VMEM((7, cells, width, 2 * cross), jnp.bfloat16),
            pltpu.VMEM((7, cells + 6, width, cross), F32),
            pltpu.VMEM(state_shape, F32),
            pltpu.VMEM((slabs, plan.packed, plan.core, 128), F32),
            pltpu.VMEM((slabs, plan.packed, 8, 128), F32),
            pltpu.VMEM((slabs, plan.packed, plan.core, 128), F32),
            pltpu.VMEM((slabs, plan.packed, 8, 128), F32),
            pltpu.SemaphoreType.DMA((6,)),
            pltpu.SemaphoreType.DMA((2, spans)),
            pltpu.SemaphoreType.DMA((2, spans)),
            pltpu.SemaphoreType.DMA((2,)),
            pltpu.SemaphoreType.DMA((2,)),
            pltpu.SemaphoreType.DMA((slabs, 2)),
            pltpu.SemaphoreType.DMA((slabs, 2)),
            pltpu.SemaphoreType.DMA((slabs, plan.count)),
            pltpu.SemaphoreType.DMA((slabs, plan.count)),
            pltpu.SemaphoreType.DMA((plan.count, slabs)),
        ],
        compiler_params=pltpu.CompilerParams(
            collective_id=0, has_side_effects=True, vmem_limit_bytes=16 << 20
        ),
        name="section",
    )(*(
        pltpu.with_memory_space_constraint(x, pltpu.HBM)
        for x in (levels, shifts, density, momentum, magnetic, energy)
    ))
    lines = pltpu.with_memory_space_constraint(lines, pltpu.VMEM)
    state = pltpu.with_memory_space_constraint(state, pltpu.VMEM)
    new_state, intensity = pl.pallas_call(
        functools.partial(ray_kernel, plan),
        out_shape=(
            jax.ShapeDtypeStruct(state_shape, F32),
            jax.ShapeDtypeStruct((width * plan.lanes, W), F32),
        ),
        in_specs=[scalars, vmem, vmem],
        out_specs=(any_spec, vmem),
        scratch_shapes=[
            pltpu.VMEM((3, plan.positions, width, 128), F32),
            pltpu.SemaphoreType.DMA((cells,)),
        ],
        compiler_params=pltpu.CompilerParams(vmem_limit_bytes=16 << 20),
        name="ray",
    )(order, lines, state)
    intensity = intensity.reshape(width, plan.lanes, W)
    return new_state, jnp.transpose(intensity, (2, 0, 1))


def solution(mesh):
    tiles, slabs = mesh.shape["tile"], mesh.shape["depth"]

    def body(density, momentum, magnetic, energy, shifts, levels):
        cells, width, cross = density.shape
        plan = Plan(tiles, slabs, cells, width, cross, levels.shape[0], 1)
        return per_device(plan, density, momentum, magnetic, energy, shifts, levels)

    return jax.shard_map(
        body,
        mesh=mesh,
        in_specs=(
            P("depth", "tile", None),
            P(None, "depth", "tile", None),
            P(None, "depth", "tile", None),
            P("depth", "tile", None),
            P(),
            P(),
        ),
        out_specs=(P(None, "depth", "tile", None), P(None, "tile", "depth")),
        check_vma=False,
    )
```

```python
import functools
import math

import jax
import jax.numpy as jnp
from jax import lax
from jax.experimental import pallas as pl
from jax.experimental.pallas import tpu as pltpu
from jax.sharding import PartitionSpec as P

W = 48
MOST = 8
GAMMA = 5.0 / 3.0
SECTION = 0.02
GRAVITY = 0.5
SIN_VIEW = 0.8660254037844386
COS_VIEW = 0.5
STRENGTH = 4.0
SPACING = 0.25
LOG2E = 1.4426950408889634
ROOT_LOG2E = math.sqrt(LOG2E)
F32 = jnp.float32
MESH = pl.DeviceIdType.MESH
PAD = 8


def column_shift(level):
    return (1732 * level + 1000) // 2000


def softplus(a):
    return jnp.maximum(a, 0.0) + jnp.log1p(jnp.exp(-jnp.abs(a)))


class Plan:
    def __init__(self, tiles, slabs, depth_cells, width, cross, positions, parts):
        self.tiles, self.slabs = tiles, slabs
        self.depth_cells, self.width, self.cross = depth_cells, width, cross
        self.positions = positions
        self.most = min(MOST, depth_cells)
        self.lanes = cross // slabs
        self.blocks = 128 // self.lanes
        self.items = 3 * self.most
        self.packed = -(-self.items // self.blocks)
        self.low = [column_shift(d * depth_cells) for d in range(slabs)]
        high = [column_shift((d + 1) * depth_cells - 1) for d in range(slabs)]
        self.rows = -(-(max(h - l for l, h in zip(self.low, high)) + width) // 8) * 8
        parts = min(parts, self.packed)
        cuts = [self.packed * i // parts for i in range(parts + 1)]
        self.groups = list(zip(cuts[:-1], cuts[1:]))
        self.spans = [(0, self.most)]
        if depth_cells > self.most:
            self.spans.append((self.most, depth_cells))
        self.core = width - 6
        self.pieces = []
        for d in range(slabs):
            mine = []
            for group, (start, stop) in enumerate(self.groups):
                slot_low = start * self.blocks // 3
                slot_high = min(self.most - 1, (stop * self.blocks - 1) // 3)
                low = column_shift(d * depth_cells + slot_low)
                high = column_shift(d * depth_cells + depth_cells - self.most + slot_high)
                for o in range(low // width, (high + width - 1) // width + 1):
                    for kind, left, right in ((0, 3, width - 3), (1, 0, 3), (1, width - 3, width)):
                        first = max(left, low - width * o)
                        last = min(right, high + width - width * o)
                        if last > first:
                            at = width * o + first - self.low[d]
                            row = first - (3 if kind == 0 else left and width - 8)
                            mine.append((o, group, row, last - first, at, kind))
            self.pieces.append(mine)
        self.count = max(len(p) for p in self.pieces)
        self.reach = sorted({p[0] for mine in self.pieces for p in mine if p[0] % tiles})


def slab_start(levels, lowest, positions):
    ahead = jnp.int32(0)
    for k in range(positions):
        ahead = ahead + jnp.where(levels[k] < lowest, 1, 0)
    return ahead


def level_order(plan, levels, d, order):
    cells, most, positions = plan.depth_cells, plan.most, plan.positions
    lowest = d * cells
    ahead = slab_start(levels, lowest, positions)
    held = slab_start(levels, lowest + cells, positions) - ahead
    spare = most - held
    used = [
        jnp.where(
            i < held, levels[jnp.minimum(ahead + i, positions - 1)] - lowest, 2 * cells
        )
        for i in range(most)
    ]

    def free(rank):
        level = rank
        for one in used:
            level = level + jnp.where(one <= level, 1, 0)
        return level

    full = jnp.where(spare > 0, free(spare - 1) + 1, 0)
    for j in range(most):
        later = levels[jnp.clip(ahead + j - spare, 0, positions - 1)] - lowest
        order[j] = jnp.clip(jnp.where(j < full, j, later), 0, cells - 1)
    for j in range(cells - most):
        order[most + j] = jnp.clip(free(spare + j), 0, cells - 1)
    first = [order[j] for j in range(most)]
    for level in range(cells):
        below, here = jnp.int32(0), jnp.int32(0)
        for one in first:
            below = below + jnp.where(one < level, 1, 0)
            here = here + jnp.where(one == level, 1, 0)
        slot = jnp.where(here > 0, below, most + level - below)
        order[cells + 3 * positions + level] = jnp.clip(slot, 0, cells - 1)


def ray_order(plan, levels, shifts, order):
    cells, most, positions = plan.depth_cells, plan.most, plan.positions
    slab = [levels[k] // cells for k in range(positions)]
    before = [jnp.int32(0)]
    for k in range(1, positions):
        before.append(jnp.where(slab[k] == slab[k - 1], before[-1] + 1, 0))
    held = [before[-1] + 1]
    for k in range(positions - 2, -1, -1):
        held.insert(0, jnp.where(slab[k] == slab[k + 1], held[0], before[k] + 1))
    for k in range(positions):
        spare = jnp.minimum(most - held[k], levels[k] - slab[k] * cells - before[k])
        at = cells + 3 * k
        start = shifts[k] - (1732 * (slab[k] * cells) + 1000) // 2000
        order[at] = jnp.clip(slab[k], 0, plan.slabs - 1)
        order[at + 1] = jnp.clip(before[k] + spare, 0, most - 1)
        order[at + 2] = jnp.clip(start, 0, plan.rows - plan.width)


def primitives(st, level):
    rho = st[0, level]
    mx, my, mz = st[1, level], st[2, level], st[3, level]
    bx, by, bz = st[4, level], st[5, level], st[6, level]
    en = st[7, level]
    inv = 1.0 / rho
    vx, vy, vz = mx * inv, my * inv, mz * inv
    half_sq = 0.5 * (bx * bx + by * by + bz * bz)
    kinetic = 0.5 * (mx * vx + my * vy + mz * vz)
    total = (GAMMA - 1.0) * (en - kinetic - half_sq) + half_sq
    vb = vx * bx + vy * by + vz * bz
    return rho, (mx, my, mz), (bx, by, bz), (vx, vy, vz), en, total, vb


def flux_along(axis, values):
    rho, m, b, v, en, total, vb = values
    out = [m[axis]]
    for i in range(3):
        term = m[i] * v[axis] - b[i] * b[axis]
        out.append(term + total if i == axis else term)
    for i in range(3):
        if i != axis:
            out.append(v[axis] * b[i] - b[axis] * v[i])
    out.append((en + total) * v[axis] - b[axis] * vb)
    return out


ROWS = ((0, 1, 2, 3, 5, 6, 7), (0, 1, 2, 3, 4, 6, 7), (0, 1, 2, 3, 4, 5, 7))
SCALE = SECTION / 60.0


def stencil(f):
    return SCALE * (45.0 * (f[4] - f[2]) - 9.0 * (f[5] - f[1]) + (f[6] - f[0]))


def section_kernel(
    plan, levels_in, shifts_in, density, momentum, magnetic, energy, ns, fields,
    order, recv, levels, shifts, st, xf, yf, zf, part, pack, rim_pack, held, rim_held,
    in_sem, xs_sem, xr_sem, zs_sem, zr_sem, ds_sem, dr_sem, ls_sem, lr_sem,
    rs_sem,
):
    tiles, slabs, cells, width = plan.tiles, plan.slabs, plan.depth_cells, plan.width
    most = plan.most
    t = lax.axis_index("tile")
    d = lax.axis_index("depth")
    right = lax.rem(t + 1, tiles)
    left = lax.rem(t + tiles - 1, tiles)

    loads = [
        pltpu.make_async_copy(density, st.at[0], in_sem.at[0]),
        pltpu.make_async_copy(momentum, st.at[1:4], in_sem.at[1]),
        pltpu.make_async_copy(magnetic, st.at[4:7], in_sem.at[2]),
        pltpu.make_async_copy(energy, st.at[7], in_sem.at[3]),
    ]
    index_loads = [
        pltpu.make_async_copy(levels_in, levels, in_sem.at[4]),
        pltpu.make_async_copy(shifts_in, shifts, in_sem.at[5]),
    ]
    for load in index_loads + loads:
        load.start()

    barrier = pltpu.get_barrier_semaphore()

    def greet(tile, depth):
        pl.semaphore_signal(barrier, inc=1, device_id=(tile, depth), device_id_type=MESH)

    greet(right, d)
    greet(left, d)
    for i in range(1, slabs):
        greet(t, lax.rem(d + i, slabs))
    for o in plan.reach:
        greet(lax.rem(t + o, tiles), d)

    for load in index_loads:
        load.wait()
    level_order(plan, levels, d, order)
    for load in loads:
        load.wait()

    def along_x(slot, carry):
        values = flux_along(0, primitives(st, order[slot]))
        for c in range(7):
            xf[c, slot, PAD:PAD + width, :] = values[c]
        return carry

    def x_copy(side, span):
        src = PAD + width - 3 if side == 0 else PAD
        dst = PAD - 3 if side == 0 else PAD + width
        start, stop = plan.spans[span]
        slots = pl.ds(start, stop - start)
        return pltpu.make_async_remote_copy(
            src_ref=xf.at[:, slots, pl.ds(src, 3), :],
            dst_ref=xf.at[:, slots, pl.ds(dst, 3), :],
            send_sem=xs_sem.at[side, span],
            recv_sem=xr_sem.at[side, span],
            device_id=(right if side == 0 else left, d),
            device_id_type=MESH,
        )

    def z_copy(side):
        src = cells if side == 0 else 3
        dst = 0 if side == 0 else cells + 3
        return pltpu.make_async_remote_copy(
            src_ref=zf.at[:, pl.ds(src, 3)],
            dst_ref=zf.at[:, pl.ds(dst, 3)],
            send_sem=zs_sem.at[side],
            recv_sem=zr_sem.at[side],
            device_id=(t, d + 1 if side == 0 else d - 1),
            device_id_type=MESH,
        )

    spans = len(plan.spans)

    def along_y(level, carry):
        values = primitives(st, level)
        rho, m, b, _, en, _, _ = values
        base = [
            rho, m[0], m[1], m[2] + (SECTION * GRAVITY) * rho, b[0], b[1], b[2],
            en + (SECTION * GRAVITY) * m[2],
        ]
        for row in range(8):
            part[row, level] = base[row]
        for c, f in enumerate(flux_along(1, values)):
            high = f.astype(jnp.bfloat16)
            yf[c, level, :, :plan.cross] = high
            yf[c, level, :, plan.cross:] = (f - high.astype(F32)).astype(jnp.bfloat16)
        return carry

    def cross():
        shape = (2 * plan.cross, plan.cross)
        ahead = lax.broadcasted_iota(jnp.int32, shape, 0) - lax.broadcasted_iota(
            jnp.int32, shape, 1
        )
        ahead = lax.rem(ahead + plan.cross, plan.cross)
        band = jnp.zeros(shape, F32)
        for i, weight in ((1, 45.0), (2, -9.0), (3, 1.0)):
            band = jnp.where(ahead == i, weight, band)
            band = jnp.where(ahead == plan.cross - i, -weight, band)
        band = band.astype(jnp.bfloat16)
        for c, row in enumerate(ROWS[1]):
            flat = yf[c].reshape(cells * width, 2 * plan.cross)
            slope = jnp.dot(flat, band, preferred_element_type=F32)
            part[row] = part[row] - SCALE * slope.reshape(cells, width, plan.cross)

    def all_y():
        lax.fori_loop(0, cells, along_y, 0)
        cross()

    def early(work):
        pass

    def late(work):
        work()

    def along_z(level):
        values = flux_along(2, primitives(st, level))
        for c in range(7):
            zf[c, level + 3] = values[c]

    def rim(i, carry):
        along_z(i)
        along_z(cells - 3 + i)
        return carry

    lax.fori_loop(0, 3, rim, 0)
    lax.fori_loop(*plan.spans[0], along_x, 0)
    early(all_y)
    pl.semaphore_wait(barrier, 2 + (slabs - 1) + len(plan.reach))

    @pl.when(d < slabs - 1)
    def _():
        z_copy(0).start()

    @pl.when(d > 0)
    def _():
        z_copy(1).start()

    x_copy(0, 0).start()
    x_copy(1, 0).start()
    for span in range(1, spans):
        lax.fori_loop(*plan.spans[span], along_x, 0)
        x_copy(0, span).start()
        x_copy(1, span).start()

    def inner(level, carry):
        along_z(level)
        return carry

    lax.fori_loop(3, cells - 3, inner, 0)

    late(all_y)

    @pl.when(d == 0)
    def _():
        for c in range(7):
            edge = zf[c, 3]
            for i in range(3):
                zf[c, i] = edge

    @pl.when(d > 0)
    def _():
        z_copy(0).wait_recv()

    @pl.when(d == slabs - 1)
    def _():
        for c in range(7):
            edge = zf[c, cells + 2]
            for i in range(3):
                zf[c, cells + 3 + i] = edge

    @pl.when(d < slabs - 1)
    def _():
        z_copy(1).wait_recv()

    def depth_part(level, carry):
        for c, row in enumerate(ROWS[2]):
            part[row, level] = part[row, level] - stencil([zf[c, level + i] for i in range(7)])
        return carry

    lax.fori_loop(0, cells, depth_part, 0)
    ray_order(plan, levels, shifts, order)

    x_row = {row: c for c, row in enumerate(ROWS[0])}

    def advance(row, level, slot):
        value = part[row, level]
        if row in x_row:
            value = value - stencil(
                [xf[x_row[row], slot, pl.ds(PAD - 3 + i, width), :] for i in range(7)]
            )
        return value

    def emit(new, out, height):
        block_of = lax.broadcasted_iota(jnp.int32, (height, 128), 1) // plan.lanes
        for slot in range(most):
            rho, mx, mz, bx, by, bz, en = new(slot)
            dens = 0.5 + softplus(rho)
            inv = 1.0 / dens
            speed = (COS_VIEW * mz + SIN_VIEW * mx) * inv
            source = softplus(en - 0.5 * (bx * bx + by * by + bz * bz)) * inv
            for f, value in enumerate((dens, speed, source)):
                item = 3 * slot + f
                row, block = item // plan.blocks, item % plan.blocks
                for target in range(slabs):
                    shift = ((block - target) * plan.lanes) % 128
                    moved = pltpu.roll(value, shift, 1) if shift else value
                    if block:
                        moved = jnp.where(block_of == block, moved, rows[target, row])
                    rows[target, row] = moved
                    if block == plan.blocks - 1 or item == plan.items - 1:
                        out[target, row] = rows.pop((target, row))

    rows = {}
    cores = 2 if slabs % 2 == 0 else 1

    def peer(step, sign):
        chip, core = d // cores, lax.rem(d, cores)
        far, flip = step // cores, step % cores
        chips = slabs // cores
        return lax.rem(chip + chips + sign * far, chips) * cores + (1 - core if flip else core)

    def depth_copy(step, kind):
        source, target = (rim_pack, rim_held) if kind else (pack, held)
        to = peer(step, 1)
        return pltpu.make_async_remote_copy(
            src_ref=source.at[to],
            dst_ref=target.at[d],
            send_sem=ds_sem.at[step, kind],
            recv_sem=dr_sem.at[step, kind],
            device_id=(t, to),
            device_id_type=MESH,
        )

    def line_copy(source, n, own=False):
        o, group, first, size, at, kind = plan.pieces[source][n]
        start, stop = plan.groups[group]
        if own:
            origin = rim_pack if kind else pack
        else:
            origin = rim_held if kind else held
        return pltpu.make_async_remote_copy(
            src_ref=origin.at[source, pl.ds(start, stop - start), pl.ds(first, size), :],
            dst_ref=recv.at[source, pl.ds(start, stop - start), pl.ds(at, size), :],
            send_sem=ls_sem.at[source, n],
            recv_sem=lr_sem.at[source, n],
            device_id=(lax.rem(t + tiles - o % tiles, tiles), d),
            device_id_type=MESH,
        )

    def rim_copy(source, n, target):
        o, group, first, size, at, _ = plan.pieces[source][n]
        start, stop = plan.groups[group]
        return pltpu.make_async_remote_copy(
            src_ref=rim_pack.at[target, pl.ds(start, stop - start), pl.ds(first, size), :],
            dst_ref=recv.at[source, pl.ds(start, stop - start), pl.ds(at, size), :],
            send_sem=rs_sem.at[n, target],
            recv_sem=lr_sem.at[source, n],
            device_id=(lax.rem(t + tiles - o % tiles, tiles), target),
            device_id_type=MESH,
        )

    def keep(source, n, own):
        _, group, first, size, at, kind = plan.pieces[source][n]
        start, stop = plan.groups[group]
        if own:
            origin = rim_pack if kind else pack
        else:
            origin = rim_held if kind else held
        for row in range(start, stop):
            recv[source, row, at:at + size, :] = origin[source, row, first:first + size, :]

    def forward(slab, kind, own=False):
        for source in range(slabs):

            @pl.when(slab == source)
            def _():
                for stays in (False, True):
                    for n, piece in enumerate(plan.pieces[source]):
                        if piece[5] == kind and (piece[0] % tiles == 0) == stays:
                            if stays:
                                keep(source, n, own)
                            else:
                                line_copy(source, n, own).start()

    line_rows = (0, 1, 3, 4, 5, 6, 7)

    def core_state(slot):
        level = order[slot]
        out = []
        for row in line_rows:
            value = part[row, level, 3:width - 3, :]
            if row in x_row:
                value = value - stencil(
                    [xf[x_row[row], slot, pl.ds(PAD + i, plan.core), :] for i in range(7)]
                )
            out.append(value)
        return out

    emit(core_state, pack, plan.core)
    for step in range(1, slabs):
        depth_copy(step, 0).start()
    forward(d, 0, own=True)
    for step in range(1, slabs):
        depth_copy(step, 0).wait_recv()
        forward(peer(step, -1), 0)

    x_copy(0, 0).wait_recv()
    x_copy(1, 0).wait_recv()
    low_rows = lax.broadcasted_iota(jnp.int32, (8, 128), 0) < 3

    def rim_state(slot):
        new = [advance(row, order[slot], slot) for row in line_rows]
        return [jnp.where(low_rows, one[:8], one[width - 8:]) for one in new]

    emit(rim_state, rim_pack, 8)
    rims = [
        (source, n)
        for source in range(slabs)
        for n, piece in enumerate(plan.pieces[source])
        if piece[5] == 1
    ]
    for source in range(slabs):

        @pl.when(d == source)
        def _():
            for one, n in rims:
                if one == source:
                    for target in range(slabs):
                        if target == source and plan.pieces[source][n][0] % tiles == 0:
                            keep(source, n, True)
                        else:
                            rim_copy(source, n, target).start()


    def rest(level, carry):
        slot = order[cells + 3 * plan.positions + level]
        for row in range(8):
            ns[row, level] = advance(row, level, slot)
        return carry

    for span in range(1, spans):
        x_copy(0, span).wait_recv()
        x_copy(1, span).wait_recv()
    lax.fori_loop(0, cells, rest, 0)

    for source in range(slabs):
        for n in range(len(plan.pieces[source])):
            here = plan.pieces[source][n][0] % tiles == 0
            if plan.pieces[source][n][5] == 1 and here:
                pl.when(d != source)(rim_copy(source, n, source).wait_recv)
            elif plan.pieces[source][n][5] == 1:
                rim_copy(source, n, source).wait_recv()
            elif not here:
                line_copy(source, n).wait_recv()

    lane = lax.broadcasted_iota(jnp.int32, (width, 128), 1)
    within = lax.rem(lane, plan.lanes)
    wanted = lane // plan.lanes == lax.rem(
        lax.broadcasted_iota(jnp.int32, (width, 128), 0), plan.blocks
    )
    for k in range(plan.positions):
        at = cells + 3 * k
        slab, slot, start = order[at], order[at + 1], order[at + 2]
        for f in range(3):
            item = 3 * slot + f
            row, block = item // plan.blocks, lax.rem(item, plan.blocks)
            value = recv[slab, row, pl.ds(start, width), :]
            value = jnp.take_along_axis(value, within + block * plan.lanes, axis=1)
            value = jnp.where(wanted, value, 0.0)
            step = 1
            while step < plan.blocks:
                value = value + pltpu.roll(value, width - step, 0)
                step *= 2
            if f == 0:
                value = value * (-LOG2E * 2.0 / plan.positions)
            elif f == 1:
                value = value * ROOT_LOG2E
            fields[f, k] = value

    for span in range(spans):
        x_copy(0, span).wait_send()
        x_copy(1, span).wait_send()

    @pl.when(d < slabs - 1)
    def _():
        z_copy(0).wait_send()

    @pl.when(d > 0)
    def _():
        z_copy(1).wait_send()

    for step in range(1, slabs):
        depth_copy(step, 0).wait_send()
    for source in range(slabs):
        for n in range(len(plan.pieces[source])):
            if plan.pieces[source][n][0] % tiles and plan.pieces[source][n][5] == 0:
                line_copy(source, n).wait_send()

        @pl.when(d == source)
        def _():
            for one, n in rims:
                if one == source:
                    for target in range(slabs):
                        if not (target == source and plan.pieces[source][n][0] % tiles == 0):
                            rim_copy(source, n, target).wait_send()


def ray_kernel(plan, fields, hold, state_out, intensity, out_sem):
    width, blocks, positions = plan.width, plan.blocks, plan.positions
    out_copy = pltpu.make_async_copy(hold, state_out, out_sem)
    out_copy.start()

    groups = W // 8
    for part in range(width // blocks):
        waves = [
            (
                (8 * g + lax.broadcasted_iota(jnp.int32, (8, 128), 0)).astype(F32)
                - 0.5 * (W - 1)
            )
            * (SPACING * ROOT_LOG2E)
            for g in range(groups)
        ]

        def field(f, k):
            return jnp.broadcast_to(fields[f, k, part * blocks:part * blocks + 1, :], (8, 128))

        def step(k, carry):
            seen, total = carry
            thin, speed, source = field(0, k), field(1, k), field(2, k)
            strong = STRENGTH * thin
            seen_next, total_next = [], []
            for g in range(groups):
                gap = waves[g] - speed
                depth = thin + strong * jnp.exp2(-(gap * gap))
                after = seen[g] * jnp.exp2(depth)
                total_next.append(total[g] + source * (seen[g] - after))
                seen_next.append(after)
            return tuple(seen_next), tuple(total_next)

        ones = tuple(jnp.ones((8, 128), F32) for _ in range(groups))
        zeros = tuple(jnp.zeros((8, 128), F32) for _ in range(groups))
        seen, total = lax.fori_loop(0, positions, step, (ones, zeros), unroll=24)
        last = field(2, positions - 1)
        value = jnp.concatenate([total[g] + last * seen[g] for g in range(groups)], axis=0)
        intensity[part * 128:(part + 1) * 128, :] = value.T

    out_copy.wait()


def per_device(plan, density, momentum, magnetic, energy, shifts, levels):
    cells, width, cross = density.shape
    slabs = plan.slabs
    any_spec = pl.BlockSpec(memory_space=pl.ANY)
    vmem = pl.BlockSpec(memory_space=pltpu.VMEM)
    state_shape = (8, cells, width, cross)
    lines_shape = (slabs, plan.packed, plan.rows, 128)
    fields_shape = (3, plan.positions, width, 128)
    spans = len(plan.spans)
    state, fields = pl.pallas_call(
        functools.partial(section_kernel, plan),
        out_shape=(
            pltpu.VMEM(state_shape, F32),
            pltpu.VMEM(fields_shape, F32),
        ),
        in_specs=[pl.BlockSpec(memory_space=pltpu.HBM)] * 6,
        out_specs=(vmem, vmem),
        scratch_shapes=[
            pltpu.SMEM((2 * cells + 3 * plan.positions,), jnp.int32),
            pltpu.VMEM(lines_shape, F32),
            pltpu.SMEM((plan.positions,), jnp.int32),
            pltpu.SMEM((plan.positions,), jnp.int32),
            pltpu.VMEM(state_shape, F32),
            pltpu.VMEM((7, cells, width + 2 * PAD, cross), F32),
            pltpu.VMEM((7, cells, width, 2 * cross), jnp.bfloat16),
            pltpu.VMEM((7, cells + 6, width, cross), F32),
            pltpu.VMEM(state_shape, F32),
            pltpu.VMEM((slabs, plan.packed, plan.core, 128), F32),
            pltpu.VMEM((slabs, plan.packed, 8, 128), F32),
            pltpu.VMEM((slabs, plan.packed, plan.core, 128), F32),
            pltpu.VMEM((slabs, plan.packed, 8, 128), F32),
            pltpu.SemaphoreType.DMA((6,)),
            pltpu.SemaphoreType.DMA((2, spans)),
            pltpu.SemaphoreType.DMA((2, spans)),
            pltpu.SemaphoreType.DMA((2,)),
            pltpu.SemaphoreType.DMA((2,)),
            pltpu.SemaphoreType.DMA((slabs, 2)),
            pltpu.SemaphoreType.DMA((slabs, 2)),
            pltpu.SemaphoreType.DMA((slabs, plan.count)),
            pltpu.SemaphoreType.DMA((slabs, plan.count)),
            pltpu.SemaphoreType.DMA((plan.count, slabs)),
        ],
        compiler_params=pltpu.CompilerParams(
            collective_id=0, has_side_effects=True, vmem_limit_bytes=16 << 20
        ),
        name="section",
    )(*(
        pltpu.with_memory_space_constraint(x, pltpu.HBM)
        for x in (levels, shifts, density, momentum, magnetic, energy)
    ))
    fields = pltpu.with_memory_space_constraint(fields, pltpu.VMEM)
    state = pltpu.with_memory_space_constraint(state, pltpu.VMEM)
    new_state, intensity = pl.pallas_call(
        functools.partial(ray_kernel, plan),
        out_shape=(
            jax.ShapeDtypeStruct(state_shape, F32),
            jax.ShapeDtypeStruct((width * plan.lanes, W), F32),
        ),
        in_specs=[vmem, vmem],
        out_specs=(any_spec, vmem),
        scratch_shapes=[
            pltpu.SemaphoreType.DMA,
        ],
        compiler_params=pltpu.CompilerParams(vmem_limit_bytes=16 << 20),
        name="ray",
    )(fields, state)
    intensity = intensity.reshape(width, plan.lanes, W)
    return new_state, jnp.transpose(intensity, (2, 0, 1))


def solution(mesh):
    tiles, slabs = mesh.shape["tile"], mesh.shape["depth"]

    def body(density, momentum, magnetic, energy, shifts, levels):
        cells, width, cross = density.shape
        plan = Plan(tiles, slabs, cells, width, cross, levels.shape[0], 1)
        return per_device(plan, density, momentum, magnetic, energy, shifts, levels)

    return jax.shard_map(
        body,
        mesh=mesh,
        in_specs=(
            P("depth", "tile", None),
            P(None, "depth", "tile", None),
            P(None, "depth", "tile", None),
            P("depth", "tile", None),
            P(),
            P(),
        ),
        out_specs=(P(None, "depth", "tile", None), P(None, "tile", "depth")),
        check_vma=False,
    )
```

```python
import functools
import math

import jax
import jax.numpy as jnp
from jax import lax
from jax.experimental import pallas as pl
from jax.experimental.pallas import tpu as pltpu
from jax.sharding import PartitionSpec as P

W = 48
MOST = 8
GAMMA = 5.0 / 3.0
SECTION = 0.02
GRAVITY = 0.5
SIN_VIEW = 0.8660254037844386
COS_VIEW = 0.5
STRENGTH = 4.0
SPACING = 0.25
LOG2E = 1.4426950408889634
ROOT_LOG2E = math.sqrt(LOG2E)
F32 = jnp.float32
MESH = pl.DeviceIdType.MESH
PAD = 8


def column_shift(level):
    return (1732 * level + 1000) // 2000


def softplus(a):
    return jnp.maximum(a, 0.0) + jnp.log1p(jnp.exp(-jnp.abs(a)))


class Plan:
    def __init__(self, tiles, slabs, depth_cells, width, cross, positions, parts):
        self.tiles, self.slabs = tiles, slabs
        self.depth_cells, self.width, self.cross = depth_cells, width, cross
        self.positions = positions
        self.most = min(MOST, depth_cells)
        self.lanes = cross // slabs
        self.blocks = 128 // self.lanes
        self.items = 3 * self.most
        self.packed = -(-self.items // self.blocks)
        self.low = [column_shift(d * depth_cells) for d in range(slabs)]
        high = [column_shift((d + 1) * depth_cells - 1) for d in range(slabs)]
        self.rows = -(-(max(h - l for l, h in zip(self.low, high)) + width) // 8) * 8
        parts = min(parts, self.packed)
        cuts = [self.packed * i // parts for i in range(parts + 1)]
        self.groups = list(zip(cuts[:-1], cuts[1:]))
        self.spans = [(0, self.most)]
        if depth_cells > self.most:
            self.spans.append((self.most, depth_cells))
        self.core = width - 6
        self.pieces = []
        for d in range(slabs):
            mine = []
            for group, (start, stop) in enumerate(self.groups):
                slot_low = start * self.blocks // 3
                slot_high = min(self.most - 1, (stop * self.blocks - 1) // 3)
                low = column_shift(d * depth_cells + slot_low)
                high = column_shift(d * depth_cells + depth_cells - self.most + slot_high)
                for o in range(low // width, (high + width - 1) // width + 1):
                    for kind, left, right in ((0, 3, width - 3), (1, 0, 3), (1, width - 3, width)):
                        first = max(left, low - width * o)
                        last = min(right, high + width - width * o)
                        if last > first:
                            at = width * o + first - self.low[d]
                            row = first - (3 if kind == 0 else left and width - 8)
                            mine.append((o, group, row, last - first, at, kind))
            self.pieces.append(mine)
        self.count = max(len(p) for p in self.pieces)
        self.reach = sorted({p[0] for mine in self.pieces for p in mine if p[0] % tiles})


def slab_start(levels, lowest, positions):
    ahead = jnp.int32(0)
    for k in range(positions):
        ahead = ahead + jnp.where(levels[k] < lowest, 1, 0)
    return ahead


def level_order(plan, levels, d, order):
    cells, most, positions = plan.depth_cells, plan.most, plan.positions
    lowest = d * cells
    ahead = slab_start(levels, lowest, positions)
    held = slab_start(levels, lowest + cells, positions) - ahead
    spare = most - held
    used = [
        jnp.where(
            i < held, levels[jnp.minimum(ahead + i, positions - 1)] - lowest, 2 * cells
        )
        for i in range(most)
    ]

    def free(rank):
        level = rank
        for one in used:
            level = level + jnp.where(one <= level, 1, 0)
        return level

    full = jnp.where(spare > 0, free(spare - 1) + 1, 0)
    for j in range(most):
        later = levels[jnp.clip(ahead + j - spare, 0, positions - 1)] - lowest
        order[j] = jnp.clip(jnp.where(j < full, j, later), 0, cells - 1)
    for j in range(cells - most):
        order[most + j] = jnp.clip(free(spare + j), 0, cells - 1)
    first = [order[j] for j in range(most)]
    for level in range(cells):
        below, here = jnp.int32(0), jnp.int32(0)
        for one in first:
            below = below + jnp.where(one < level, 1, 0)
            here = here + jnp.where(one == level, 1, 0)
        slot = jnp.where(here > 0, below, most + level - below)
        order[cells + 3 * positions + level] = jnp.clip(slot, 0, cells - 1)


def ray_order(plan, levels, shifts, order):
    cells, most, positions = plan.depth_cells, plan.most, plan.positions
    slab = [levels[k] // cells for k in range(positions)]
    before = [jnp.int32(0)]
    for k in range(1, positions):
        before.append(jnp.where(slab[k] == slab[k - 1], before[-1] + 1, 0))
    held = [before[-1] + 1]
    for k in range(positions - 2, -1, -1):
        held.insert(0, jnp.where(slab[k] == slab[k + 1], held[0], before[k] + 1))
    for k in range(positions):
        spare = jnp.minimum(most - held[k], levels[k] - slab[k] * cells - before[k])
        at = cells + 3 * k
        start = shifts[k] - (1732 * (slab[k] * cells) + 1000) // 2000
        order[at] = jnp.clip(slab[k], 0, plan.slabs - 1)
        order[at + 1] = jnp.clip(before[k] + spare, 0, most - 1)
        order[at + 2] = jnp.clip(start, 0, plan.rows - plan.width)


def primitives(st, level):
    rho = st[0, level]
    mx, my, mz = st[1, level], st[2, level], st[3, level]
    bx, by, bz = st[4, level], st[5, level], st[6, level]
    en = st[7, level]
    inv = 1.0 / rho
    vx, vy, vz = mx * inv, my * inv, mz * inv
    half_sq = 0.5 * (bx * bx + by * by + bz * bz)
    kinetic = 0.5 * (mx * vx + my * vy + mz * vz)
    total = (GAMMA - 1.0) * (en - kinetic - half_sq) + half_sq
    vb = vx * bx + vy * by + vz * bz
    return rho, (mx, my, mz), (bx, by, bz), (vx, vy, vz), en, total, vb


def flux_along(axis, values):
    rho, m, b, v, en, total, vb = values
    out = [m[axis]]
    for i in range(3):
        term = m[i] * v[axis] - b[i] * b[axis]
        out.append(term + total if i == axis else term)
    for i in range(3):
        if i != axis:
            out.append(v[axis] * b[i] - b[axis] * v[i])
    out.append((en + total) * v[axis] - b[axis] * vb)
    return out


ROWS = ((0, 1, 2, 3, 5, 6, 7), (0, 1, 2, 3, 4, 6, 7), (0, 1, 2, 3, 4, 5, 7))
SCALE = SECTION / 60.0


def stencil(f):
    return SCALE * (45.0 * (f[4] - f[2]) - 9.0 * (f[5] - f[1]) + (f[6] - f[0]))


def section_kernel(
    plan, levels_in, shifts_in, density, momentum, magnetic, energy, ns, fields,
    order, recv, levels, shifts, st, xf, yf, zf, part, pack, rim_pack, held, rim_held,
    in_sem, xs_sem, xr_sem, zs_sem, zr_sem, ds_sem, dr_sem, ls_sem, lr_sem,
    rs_sem,
):
    tiles, slabs, cells, width = plan.tiles, plan.slabs, plan.depth_cells, plan.width
    most = plan.most
    t = lax.axis_index("tile")
    d = lax.axis_index("depth")
    right = lax.rem(t + 1, tiles)
    left = lax.rem(t + tiles - 1, tiles)

    loads = [
        pltpu.make_async_copy(density, st.at[0], in_sem.at[0]),
        pltpu.make_async_copy(momentum, st.at[1:4], in_sem.at[1]),
        pltpu.make_async_copy(magnetic, st.at[4:7], in_sem.at[2]),
        pltpu.make_async_copy(energy, st.at[7], in_sem.at[3]),
    ]
    index_loads = [
        pltpu.make_async_copy(levels_in, levels, in_sem.at[4]),
        pltpu.make_async_copy(shifts_in, shifts, in_sem.at[5]),
    ]
    for load in index_loads + loads:
        load.start()

    barrier = pltpu.get_barrier_semaphore()

    def greet(tile, depth):
        pl.semaphore_signal(barrier, inc=1, device_id=(tile, depth), device_id_type=MESH)

    greet(right, d)
    greet(left, d)
    for i in range(1, slabs):
        greet(t, lax.rem(d + i, slabs))
    for o in plan.reach:
        greet(lax.rem(t + o, tiles), d)

    for load in index_loads:
        load.wait()
    level_order(plan, levels, d, order)
    for load in loads:
        load.wait()

    def along_x(slot, carry):
        values = flux_along(0, primitives(st, order[slot]))
        for c in range(7):
            xf[c, slot, PAD:PAD + width, :] = values[c]
        return carry

    def x_copy(side, span):
        src = PAD + width - 3 if side == 0 else PAD
        dst = PAD - 3 if side == 0 else PAD + width
        start, stop = plan.spans[span]
        slots = pl.ds(start, stop - start)
        return pltpu.make_async_remote_copy(
            src_ref=xf.at[:, slots, pl.ds(src, 3), :],
            dst_ref=xf.at[:, slots, pl.ds(dst, 3), :],
            send_sem=xs_sem.at[side, span],
            recv_sem=xr_sem.at[side, span],
            device_id=(right if side == 0 else left, d),
            device_id_type=MESH,
        )

    def z_copy(side):
        src = cells if side == 0 else 3
        dst = 0 if side == 0 else cells + 3
        return pltpu.make_async_remote_copy(
            src_ref=zf.at[:, pl.ds(src, 3)],
            dst_ref=zf.at[:, pl.ds(dst, 3)],
            send_sem=zs_sem.at[side],
            recv_sem=zr_sem.at[side],
            device_id=(t, d + 1 if side == 0 else d - 1),
            device_id_type=MESH,
        )

    spans = len(plan.spans)

    def along_y(level, carry):
        values = primitives(st, level)
        rho, m, b, _, en, _, _ = values
        base = [
            rho, m[0], m[1], m[2] + (SECTION * GRAVITY) * rho, b[0], b[1], b[2],
            en + (SECTION * GRAVITY) * m[2],
        ]
        for row in range(8):
            part[row, level] = base[row]
        for c, f in enumerate(flux_along(1, values)):
            high = f.astype(jnp.bfloat16)
            yf[c, level, :, :plan.cross] = high
            yf[c, level, :, plan.cross:] = (f - high.astype(F32)).astype(jnp.bfloat16)
        return carry

    def cross():
        shape = (2 * plan.cross, plan.cross)
        ahead = lax.broadcasted_iota(jnp.int32, shape, 0) - lax.broadcasted_iota(
            jnp.int32, shape, 1
        )
        ahead = lax.rem(ahead + plan.cross, plan.cross)
        band = jnp.zeros(shape, F32)
        for i, weight in ((1, 45.0), (2, -9.0), (3, 1.0)):
            band = jnp.where(ahead == i, weight, band)
            band = jnp.where(ahead == plan.cross - i, -weight, band)
        band = band.astype(jnp.bfloat16)
        for c, row in enumerate(ROWS[1]):
            flat = yf[c].reshape(cells * width, 2 * plan.cross)
            slope = jnp.dot(flat, band, preferred_element_type=F32)
            part[row] = part[row] - SCALE * slope.reshape(cells, width, plan.cross)

    def all_y():
        lax.fori_loop(0, cells, along_y, 0)
        cross()

    def along_z(level):
        values = flux_along(2, primitives(st, level))
        for c in range(7):
            zf[c, level + 3] = values[c]

    def rim(i, carry):
        along_z(i)
        along_z(cells - 3 + i)
        return carry

    lax.fori_loop(0, 3, rim, 0)
    lax.fori_loop(*plan.spans[0], along_x, 0)
    pl.semaphore_wait(barrier, 2 + (slabs - 1) + len(plan.reach))

    @pl.when(d < slabs - 1)
    def _():
        z_copy(0).start()

    @pl.when(d > 0)
    def _():
        z_copy(1).start()

    x_copy(0, 0).start()
    x_copy(1, 0).start()
    for span in range(1, spans):
        lax.fori_loop(*plan.spans[span], along_x, 0)
        x_copy(0, span).start()
        x_copy(1, span).start()

    def inner(level, carry):
        along_z(level)
        return carry

    lax.fori_loop(3, cells - 3, inner, 0)

    all_y()

    @pl.when(d == 0)
    def _():
        for c in range(7):
            edge = zf[c, 3]
            for i in range(3):
                zf[c, i] = edge

    @pl.when(d > 0)
    def _():
        z_copy(0).wait_recv()

    @pl.when(d == slabs - 1)
    def _():
        for c in range(7):
            edge = zf[c, cells + 2]
            for i in range(3):
                zf[c, cells + 3 + i] = edge

    @pl.when(d < slabs - 1)
    def _():
        z_copy(1).wait_recv()

    def depth_part(level, carry):
        for c, row in enumerate(ROWS[2]):
            part[row, level] = part[row, level] - stencil([zf[c, level + i] for i in range(7)])
        return carry

    lax.fori_loop(0, cells, depth_part, 0)
    ray_order(plan, levels, shifts, order)

    x_row = {row: c for c, row in enumerate(ROWS[0])}

    def advance(row, level, slot):
        value = part[row, level]
        if row in x_row:
            value = value - stencil(
                [xf[x_row[row], slot, pl.ds(PAD - 3 + i, width), :] for i in range(7)]
            )
        return value

    def emit(new, out, height):
        block_of = lax.broadcasted_iota(jnp.int32, (height, 128), 1) // plan.lanes
        for slot in range(most):
            rho, mx, mz, bx, by, bz, en = new(slot)
            dens = 0.5 + softplus(rho)
            inv = 1.0 / dens
            speed = (COS_VIEW * mz + SIN_VIEW * mx) * inv
            source = softplus(en - 0.5 * (bx * bx + by * by + bz * bz)) * inv
            for f, value in enumerate((dens, speed, source)):
                item = 3 * slot + f
                row, block = item // plan.blocks, item % plan.blocks
                for target in range(slabs):
                    shift = ((block - target) * plan.lanes) % 128
                    moved = pltpu.roll(value, shift, 1) if shift else value
                    if block:
                        moved = jnp.where(block_of == block, moved, rows[target, row])
                    rows[target, row] = moved
                    if block == plan.blocks - 1 or item == plan.items - 1:
                        out[target, row] = rows.pop((target, row))

    rows = {}
    cores = 2 if slabs % 2 == 0 else 1

    def peer(step, sign):
        chip, core = d // cores, lax.rem(d, cores)
        far, flip = step // cores, step % cores
        chips = slabs // cores
        return lax.rem(chip + chips + sign * far, chips) * cores + (1 - core if flip else core)

    def depth_copy(step, kind):
        source, target = (rim_pack, rim_held) if kind else (pack, held)
        to = peer(step, 1)
        return pltpu.make_async_remote_copy(
            src_ref=source.at[to],
            dst_ref=target.at[d],
            send_sem=ds_sem.at[step, kind],
            recv_sem=dr_sem.at[step, kind],
            device_id=(t, to),
            device_id_type=MESH,
        )

    def line_copy(source, n, own=False):
        o, group, first, size, at, kind = plan.pieces[source][n]
        start, stop = plan.groups[group]
        if own:
            origin = rim_pack if kind else pack
        else:
            origin = rim_held if kind else held
        return pltpu.make_async_remote_copy(
            src_ref=origin.at[source, pl.ds(start, stop - start), pl.ds(first, size), :],
            dst_ref=recv.at[source, pl.ds(start, stop - start), pl.ds(at, size), :],
            send_sem=ls_sem.at[source, n],
            recv_sem=lr_sem.at[source, n],
            device_id=(lax.rem(t + tiles - o % tiles, tiles), d),
            device_id_type=MESH,
        )

    def rim_copy(source, n, target):
        o, group, first, size, at, _ = plan.pieces[source][n]
        start, stop = plan.groups[group]
        return pltpu.make_async_remote_copy(
            src_ref=rim_pack.at[target, pl.ds(start, stop - start), pl.ds(first, size), :],
            dst_ref=recv.at[source, pl.ds(start, stop - start), pl.ds(at, size), :],
            send_sem=rs_sem.at[n, target],
            recv_sem=lr_sem.at[source, n],
            device_id=(lax.rem(t + tiles - o % tiles, tiles), target),
            device_id_type=MESH,
        )

    def keep(source, n, own):
        _, group, first, size, at, kind = plan.pieces[source][n]
        start, stop = plan.groups[group]
        if own:
            origin = rim_pack if kind else pack
        else:
            origin = rim_held if kind else held
        for row in range(start, stop):
            recv[source, row, at:at + size, :] = origin[source, row, first:first + size, :]

    def forward(slab, kind, own=False):
        for source in range(slabs):

            @pl.when(slab == source)
            def _():
                for stays in (False, True):
                    for n, piece in reversed(list(enumerate(plan.pieces[source]))):
                        if piece[5] == kind and (piece[0] % tiles == 0) == stays:
                            if stays:
                                keep(source, n, own)
                            else:
                                line_copy(source, n, own).start()

    line_rows = (0, 1, 3, 4, 5, 6, 7)

    def core_state(slot):
        level = order[slot]
        out = []
        for row in line_rows:
            value = part[row, level, 3:width - 3, :]
            if row in x_row:
                value = value - stencil(
                    [xf[x_row[row], slot, pl.ds(PAD + i, plan.core), :] for i in range(7)]
                )
            out.append(value)
        return out

    emit(core_state, pack, plan.core)
    for step in range(1, slabs):
        depth_copy(step, 0).start()
    forward(d, 0, own=True)
    for step in range(1, slabs):
        depth_copy(step, 0).wait_recv()
        forward(peer(step, -1), 0)

    x_copy(0, 0).wait_recv()
    x_copy(1, 0).wait_recv()
    low_rows = lax.broadcasted_iota(jnp.int32, (8, 128), 0) < 3

    def rim_state(slot):
        new = [advance(row, order[slot], slot) for row in line_rows]
        return [jnp.where(low_rows, one[:8], one[width - 8:]) for one in new]

    emit(rim_state, rim_pack, 8)
    rims = [
        (source, n)
        for source in range(slabs)
        for n, piece in enumerate(plan.pieces[source])
        if piece[5] == 1
    ]
    for source in range(slabs):

        @pl.when(d == source)
        def _():
            for one, n in reversed(rims):
                if one == source:
                    for target in range(slabs):
                        if target == source and plan.pieces[source][n][0] % tiles == 0:
                            keep(source, n, True)
                        else:
                            rim_copy(source, n, target).start()


    def rest(level, carry):
        slot = order[cells + 3 * plan.positions + level]
        for row in range(8):
            ns[row, level] = advance(row, level, slot)
        return carry

    for span in range(1, spans):
        x_copy(0, span).wait_recv()
        x_copy(1, span).wait_recv()
    lax.fori_loop(0, cells, rest, 0)

    for span in range(spans):
        x_copy(0, span).wait_send()
        x_copy(1, span).wait_send()

    @pl.when(d < slabs - 1)
    def _():
        z_copy(0).wait_send()

    @pl.when(d > 0)
    def _():
        z_copy(1).wait_send()

    for step in range(1, slabs):
        depth_copy(step, 0).wait_send()
    for source in range(slabs):
        for n in range(len(plan.pieces[source])):
            if plan.pieces[source][n][0] % tiles and plan.pieces[source][n][5] == 0:
                line_copy(source, n).wait_send()

        @pl.when(d == source)
        def _():
            for one, n in rims:
                if one == source:
                    for target in range(slabs):
                        if not (target == source and plan.pieces[source][n][0] % tiles == 0):
                            rim_copy(source, n, target).wait_send()

    for source in range(slabs):
        for n in range(len(plan.pieces[source])):
            here = plan.pieces[source][n][0] % tiles == 0
            if plan.pieces[source][n][5] == 1 and here:
                pl.when(d != source)(rim_copy(source, n, source).wait_recv)
            elif plan.pieces[source][n][5] == 1:
                rim_copy(source, n, source).wait_recv()
            elif not here:
                line_copy(source, n).wait_recv()

    lane = lax.broadcasted_iota(jnp.int32, (width, 128), 1)
    within = lax.rem(lane, plan.lanes)
    wanted = lane // plan.lanes == lax.rem(
        lax.broadcasted_iota(jnp.int32, (width, 128), 0), plan.blocks
    )
    for k in range(plan.positions):
        at = cells + 3 * k
        slab, slot, start = order[at], order[at + 1], order[at + 2]
        for f in range(3):
            item = 3 * slot + f
            row, block = item // plan.blocks, lax.rem(item, plan.blocks)
            value = recv[slab, row, pl.ds(start, width), :]
            value = jnp.take_along_axis(value, within + block * plan.lanes, axis=1)
            value = jnp.where(wanted, value, 0.0)
            step = 1
            while step < plan.blocks:
                value = value + pltpu.roll(value, width - step, 0)
                step *= 2
            if f == 0:
                value = value * (-LOG2E * 2.0 / plan.positions)
            elif f == 1:
                value = value * ROOT_LOG2E
            fields[f, k] = value


def ray_kernel(plan, fields, hold, state_out, intensity, out_sem):
    width, blocks, positions = plan.width, plan.blocks, plan.positions
    out_copy = pltpu.make_async_copy(hold, state_out, out_sem)
    out_copy.start()

    groups = W // 8
    for part in range(width // blocks):
        waves = [
            (
                (8 * g + lax.broadcasted_iota(jnp.int32, (8, 128), 0)).astype(F32)
                - 0.5 * (W - 1)
            )
            * (SPACING * ROOT_LOG2E)
            for g in range(groups)
        ]

        def field(f, k):
            return jnp.broadcast_to(fields[f, k, part * blocks:part * blocks + 1, :], (8, 128))

        def step(k, carry):
            seen, total = carry
            thin, speed, source = field(0, k), field(1, k), field(2, k)
            strong = STRENGTH * thin
            seen_next, total_next = [], []
            for g in range(groups):
                gap = waves[g] - speed
                depth = thin + strong * jnp.exp2(-(gap * gap))
                after = seen[g] * jnp.exp2(depth)
                total_next.append(total[g] + source * (seen[g] - after))
                seen_next.append(after)
            return tuple(seen_next), tuple(total_next)

        ones = tuple(jnp.ones((8, 128), F32) for _ in range(groups))
        zeros = tuple(jnp.zeros((8, 128), F32) for _ in range(groups))
        seen, total = lax.fori_loop(0, positions, step, (ones, zeros), unroll=24)
        last = field(2, positions - 1)
        value = jnp.concatenate([total[g] + last * seen[g] for g in range(groups)], axis=0)
        intensity[part * 128:(part + 1) * 128, :] = value.T

    out_copy.wait()


def per_device(plan, density, momentum, magnetic, energy, shifts, levels):
    cells, width, cross = density.shape
    slabs = plan.slabs
    any_spec = pl.BlockSpec(memory_space=pl.ANY)
    vmem = pl.BlockSpec(memory_space=pltpu.VMEM)
    state_shape = (8, cells, width, cross)
    lines_shape = (slabs, plan.packed, plan.rows, 128)
    fields_shape = (3, plan.positions, width, 128)
    spans = len(plan.spans)
    state, fields = pl.pallas_call(
        functools.partial(section_kernel, plan),
        out_shape=(
            pltpu.VMEM(state_shape, F32),
            pltpu.VMEM(fields_shape, F32),
        ),
        in_specs=[pl.BlockSpec(memory_space=pltpu.HBM)] * 6,
        out_specs=(vmem, vmem),
        scratch_shapes=[
            pltpu.SMEM((2 * cells + 3 * plan.positions,), jnp.int32),
            pltpu.VMEM(lines_shape, F32),
            pltpu.SMEM((plan.positions,), jnp.int32),
            pltpu.SMEM((plan.positions,), jnp.int32),
            pltpu.VMEM(state_shape, F32),
            pltpu.VMEM((7, cells, width + 2 * PAD, cross), F32),
            pltpu.VMEM((7, cells, width, 2 * cross), jnp.bfloat16),
            pltpu.VMEM((7, cells + 6, width, cross), F32),
            pltpu.VMEM(state_shape, F32),
            pltpu.VMEM((slabs, plan.packed, plan.core, 128), F32),
            pltpu.VMEM((slabs, plan.packed, 8, 128), F32),
            pltpu.VMEM((slabs, plan.packed, plan.core, 128), F32),
            pltpu.VMEM((slabs, plan.packed, 8, 128), F32),
            pltpu.SemaphoreType.DMA((6,)),
            pltpu.SemaphoreType.DMA((2, spans)),
            pltpu.SemaphoreType.DMA((2, spans)),
            pltpu.SemaphoreType.DMA((2,)),
            pltpu.SemaphoreType.DMA((2,)),
            pltpu.SemaphoreType.DMA((slabs, 2)),
            pltpu.SemaphoreType.DMA((slabs, 2)),
            pltpu.SemaphoreType.DMA((slabs, plan.count)),
            pltpu.SemaphoreType.DMA((slabs, plan.count)),
            pltpu.SemaphoreType.DMA((plan.count, slabs)),
        ],
        compiler_params=pltpu.CompilerParams(
            collective_id=0, has_side_effects=True, vmem_limit_bytes=16 << 20
        ),
        name="section",
    )(*(
        pltpu.with_memory_space_constraint(x, pltpu.HBM)
        for x in (levels, shifts, density, momentum, magnetic, energy)
    ))
    fields = pltpu.with_memory_space_constraint(fields, pltpu.VMEM)
    state = pltpu.with_memory_space_constraint(state, pltpu.VMEM)
    new_state, intensity = pl.pallas_call(
        functools.partial(ray_kernel, plan),
        out_shape=(
            jax.ShapeDtypeStruct(state_shape, F32),
            jax.ShapeDtypeStruct((width * plan.lanes, W), F32),
        ),
        in_specs=[vmem, vmem],
        out_specs=(any_spec, vmem),
        scratch_shapes=[
            pltpu.SemaphoreType.DMA,
        ],
        compiler_params=pltpu.CompilerParams(vmem_limit_bytes=16 << 20),
        name="ray",
    )(fields, state)
    intensity = intensity.reshape(width, plan.lanes, W)
    return new_state, jnp.transpose(intensity, (2, 0, 1))


def solution(mesh):
    tiles, slabs = mesh.shape["tile"], mesh.shape["depth"]

    def body(density, momentum, magnetic, energy, shifts, levels):
        cells, width, cross = density.shape
        plan = Plan(tiles, slabs, cells, width, cross, levels.shape[0], 1)
        return per_device(plan, density, momentum, magnetic, energy, shifts, levels)

    return jax.shard_map(
        body,
        mesh=mesh,
        in_specs=(
            P("depth", "tile", None),
            P(None, "depth", "tile", None),
            P(None, "depth", "tile", None),
            P("depth", "tile", None),
            P(),
            P(),
        ),
        out_specs=(P(None, "depth", "tile", None), P(None, "tile", "depth")),
        check_vma=False,
    )
```

```python
import functools
import math

import jax
import jax.numpy as jnp
from jax import lax
from jax.experimental import pallas as pl
from jax.experimental.pallas import tpu as pltpu
from jax.sharding import PartitionSpec as P

W = 48
MOST = 8
GAMMA = 5.0 / 3.0
SECTION = 0.02
GRAVITY = 0.5
SIN_VIEW = 0.8660254037844386
COS_VIEW = 0.5
STRENGTH = 4.0
SPACING = 0.25
LOG2E = 1.4426950408889634
ROOT_LOG2E = math.sqrt(LOG2E)
F32 = jnp.float32
MESH = pl.DeviceIdType.MESH
PAD = 8


def column_shift(level):
    return (1732 * level + 1000) // 2000


def softplus(a):
    return jnp.maximum(a, 0.0) + jnp.log1p(jnp.exp(-jnp.abs(a)))


class Plan:
    def __init__(self, tiles, slabs, depth_cells, width, cross, positions, parts):
        self.tiles, self.slabs = tiles, slabs
        self.depth_cells, self.width, self.cross = depth_cells, width, cross
        self.positions = positions
        self.most = min(MOST, depth_cells)
        self.lanes = cross // slabs
        self.blocks = 128 // self.lanes
        self.items = 3 * self.most
        self.packed = -(-self.items // self.blocks)
        self.low = [column_shift(d * depth_cells) for d in range(slabs)]
        high = [column_shift((d + 1) * depth_cells - 1) for d in range(slabs)]
        self.rows = -(-(max(h - l for l, h in zip(self.low, high)) + width) // 8) * 8
        parts = min(parts, self.packed)
        cuts = [self.packed * i // parts for i in range(parts + 1)]
        self.groups = list(zip(cuts[:-1], cuts[1:]))
        self.spans = [(0, self.most)]
        if depth_cells > self.most:
            self.spans.append((self.most, depth_cells))
        self.core = width - 6
        self.sends = [(0, 6, 0, self.most), (6, 1, 0, self.most)]
        if depth_cells > self.most:
            self.sends.append((0, 7, self.most, depth_cells - self.most))
        self.pieces = []
        for d in range(slabs):
            mine = []
            for group, (start, stop) in enumerate(self.groups):
                slot_low = start * self.blocks // 3
                slot_high = min(self.most - 1, (stop * self.blocks - 1) // 3)
                low = column_shift(d * depth_cells + slot_low)
                high = column_shift(d * depth_cells + depth_cells - self.most + slot_high)
                for o in range(low // width, (high + width - 1) // width + 1):
                    for kind, left, right in ((0, 3, width - 3), (1, 0, 3), (1, width - 3, width)):
                        first = max(left, low - width * o)
                        last = min(right, high + width - width * o)
                        if last > first:
                            at = width * o + first - self.low[d]
                            row = first - (3 if kind == 0 else left and width - 8)
                            mine.append((o, group, row, last - first, at, kind))
            self.pieces.append(mine)
        self.count = max(len(p) for p in self.pieces)
        self.reach = sorted({p[0] for mine in self.pieces for p in mine if p[0] % tiles})


def slab_start(levels, lowest, positions):
    ahead = jnp.int32(0)
    for k in range(positions):
        ahead = ahead + jnp.where(levels[k] < lowest, 1, 0)
    return ahead


def level_order(plan, levels, d, order):
    cells, most, positions = plan.depth_cells, plan.most, plan.positions
    lowest = d * cells
    ahead = slab_start(levels, lowest, positions)
    held = slab_start(levels, lowest + cells, positions) - ahead
    spare = most - held
    used = [
        jnp.where(
            i < held, levels[jnp.minimum(ahead + i, positions - 1)] - lowest, 2 * cells
        )
        for i in range(most)
    ]

    def free(rank):
        level = rank
        for one in used:
            level = level + jnp.where(one <= level, 1, 0)
        return level

    full = jnp.where(spare > 0, free(spare - 1) + 1, 0)
    for j in range(most):
        later = levels[jnp.clip(ahead + j - spare, 0, positions - 1)] - lowest
        order[j] = jnp.clip(jnp.where(j < full, j, later), 0, cells - 1)
    for j in range(cells - most):
        order[most + j] = jnp.clip(free(spare + j), 0, cells - 1)
    first = [order[j] for j in range(most)]
    for level in range(cells):
        below, here = jnp.int32(0), jnp.int32(0)
        for one in first:
            below = below + jnp.where(one < level, 1, 0)
            here = here + jnp.where(one == level, 1, 0)
        slot = jnp.where(here > 0, below, most + level - below)
        order[cells + 3 * positions + level] = jnp.clip(slot, 0, cells - 1)


def ray_order(plan, levels, shifts, order):
    cells, most, positions = plan.depth_cells, plan.most, plan.positions
    slab = [levels[k] // cells for k in range(positions)]
    before = [jnp.int32(0)]
    for k in range(1, positions):
        before.append(jnp.where(slab[k] == slab[k - 1], before[-1] + 1, 0))
    held = [before[-1] + 1]
    for k in range(positions - 2, -1, -1):
        held.insert(0, jnp.where(slab[k] == slab[k + 1], held[0], before[k] + 1))
    for k in range(positions):
        spare = jnp.minimum(most - held[k], levels[k] - slab[k] * cells - before[k])
        at = cells + 3 * k
        start = shifts[k] - (1732 * (slab[k] * cells) + 1000) // 2000
        order[at] = jnp.clip(slab[k], 0, plan.slabs - 1)
        order[at + 1] = jnp.clip(before[k] + spare, 0, most - 1)
        order[at + 2] = jnp.clip(start, 0, plan.rows - plan.width)


def primitives(st, level):
    rho = st[0, level]
    mx, my, mz = st[1, level], st[2, level], st[3, level]
    bx, by, bz = st[4, level], st[5, level], st[6, level]
    en = st[7, level]
    inv = 1.0 / rho
    vx, vy, vz = mx * inv, my * inv, mz * inv
    half_sq = 0.5 * (bx * bx + by * by + bz * bz)
    kinetic = 0.5 * (mx * vx + my * vy + mz * vz)
    total = (GAMMA - 1.0) * (en - kinetic - half_sq) + half_sq
    vb = vx * bx + vy * by + vz * bz
    return rho, (mx, my, mz), (bx, by, bz), (vx, vy, vz), en, total, vb


def flux_along(axis, values):
    rho, m, b, v, en, total, vb = values
    out = [m[axis]]
    for i in range(3):
        term = m[i] * v[axis] - b[i] * b[axis]
        out.append(term + total if i == axis else term)
    for i in range(3):
        if i != axis:
            out.append(v[axis] * b[i] - b[axis] * v[i])
    out.append((en + total) * v[axis] - b[axis] * vb)
    return out


ROWS = ((0, 1, 2, 3, 5, 6, 7), (0, 1, 2, 3, 4, 6, 7), (0, 1, 2, 3, 4, 5, 7))
X_ROWS = (0, 1, 3, 5, 6, 7, 2)
SCALE = SECTION / 60.0


def stencil(f):
    return SCALE * (45.0 * (f[4] - f[2]) - 9.0 * (f[5] - f[1]) + (f[6] - f[0]))


def section_kernel(
    plan, levels_in, shifts_in, density, momentum, magnetic, energy, ns, fields,
    order, recv, levels, shifts, st, xf, yf, zf, part, pack, rim_pack, held, rim_held,
    in_sem, xs_sem, xr_sem, zs_sem, zr_sem, ds_sem, dr_sem, ls_sem, lr_sem,
    rs_sem,
):
    tiles, slabs, cells, width = plan.tiles, plan.slabs, plan.depth_cells, plan.width
    most = plan.most
    t = lax.axis_index("tile")
    d = lax.axis_index("depth")
    right = lax.rem(t + 1, tiles)
    left = lax.rem(t + tiles - 1, tiles)

    loads = [
        pltpu.make_async_copy(density, st.at[0], in_sem.at[0]),
        pltpu.make_async_copy(momentum, st.at[1:4], in_sem.at[1]),
        pltpu.make_async_copy(magnetic, st.at[4:7], in_sem.at[2]),
        pltpu.make_async_copy(energy, st.at[7], in_sem.at[3]),
    ]
    index_loads = [
        pltpu.make_async_copy(levels_in, levels, in_sem.at[4]),
        pltpu.make_async_copy(shifts_in, shifts, in_sem.at[5]),
    ]
    for load in index_loads + loads:
        load.start()

    barrier = pltpu.get_barrier_semaphore()

    def greet(tile, depth):
        pl.semaphore_signal(barrier, inc=1, device_id=(tile, depth), device_id_type=MESH)

    greet(right, d)
    greet(left, d)
    for i in range(1, slabs):
        greet(t, lax.rem(d + i, slabs))
    for o in plan.reach:
        greet(lax.rem(t + o, tiles), d)

    for load in index_loads:
        load.wait()
    level_order(plan, levels, d, order)
    for load in loads:
        load.wait()

    def along_x(slot, carry):
        values = flux_along(0, primitives(st, order[slot]))
        for c, row in enumerate(X_ROWS):
            xf[c, slot, PAD:PAD + width, :] = values[ROWS[0].index(row)]
        return carry

    def x_copy(side, span):
        src = PAD + width - 3 if side == 0 else PAD
        dst = PAD - 3 if side == 0 else PAD + width
        comp, comps, start, count = plan.sends[span]
        comps, slots = pl.ds(comp, comps), pl.ds(start, count)
        return pltpu.make_async_remote_copy(
            src_ref=xf.at[comps, slots, pl.ds(src, 3), :],
            dst_ref=xf.at[comps, slots, pl.ds(dst, 3), :],
            send_sem=xs_sem.at[side, span],
            recv_sem=xr_sem.at[side, span],
            device_id=(right if side == 0 else left, d),
            device_id_type=MESH,
        )

    def z_copy(side):
        src = cells if side == 0 else 3
        dst = 0 if side == 0 else cells + 3
        return pltpu.make_async_remote_copy(
            src_ref=zf.at[:, pl.ds(src, 3)],
            dst_ref=zf.at[:, pl.ds(dst, 3)],
            send_sem=zs_sem.at[side],
            recv_sem=zr_sem.at[side],
            device_id=(t, d + 1 if side == 0 else d - 1),
            device_id_type=MESH,
        )

    spans = len(plan.sends)

    def along_y(level, carry):
        values = primitives(st, level)
        rho, m, b, _, en, _, _ = values
        base = [
            rho, m[0], m[1], m[2] + (SECTION * GRAVITY) * rho, b[0], b[1], b[2],
            en + (SECTION * GRAVITY) * m[2],
        ]
        for row in range(8):
            part[row, level] = base[row]
        for c, f in enumerate(flux_along(1, values)):
            high = f.astype(jnp.bfloat16)
            yf[c, level, :, :plan.cross] = high
            yf[c, level, :, plan.cross:] = (f - high.astype(F32)).astype(jnp.bfloat16)
        return carry

    def cross():
        shape = (2 * plan.cross, plan.cross)
        ahead = lax.broadcasted_iota(jnp.int32, shape, 0) - lax.broadcasted_iota(
            jnp.int32, shape, 1
        )
        ahead = lax.rem(ahead + plan.cross, plan.cross)
        band = jnp.zeros(shape, F32)
        for i, weight in ((1, 45.0), (2, -9.0), (3, 1.0)):
            band = jnp.where(ahead == i, weight, band)
            band = jnp.where(ahead == plan.cross - i, -weight, band)
        band = band.astype(jnp.bfloat16)
        for c, row in enumerate(ROWS[1]):
            flat = yf[c].reshape(cells * width, 2 * plan.cross)
            slope = jnp.dot(flat, band, preferred_element_type=F32)
            part[row] = part[row] - SCALE * slope.reshape(cells, width, plan.cross)

    def all_y():
        lax.fori_loop(0, cells, along_y, 0)
        cross()

    def along_z(level):
        values = flux_along(2, primitives(st, level))
        for c in range(7):
            zf[c, level + 3] = values[c]

    def rim(i, carry):
        along_z(i)
        along_z(cells - 3 + i)
        return carry

    lax.fori_loop(0, 3, rim, 0)
    lax.fori_loop(*plan.spans[0], along_x, 0)
    pl.semaphore_wait(barrier, 2 + (slabs - 1) + len(plan.reach))

    @pl.when(d < slabs - 1)
    def _():
        z_copy(0).start()

    @pl.when(d > 0)
    def _():
        z_copy(1).start()

    x_copy(0, 0).start()
    x_copy(1, 0).start()
    for span in range(1, spans):
        if span == 1 and cells > most:
            lax.fori_loop(most, cells, along_x, 0)
        x_copy(0, span).start()
        x_copy(1, span).start()

    def inner(level, carry):
        along_z(level)
        return carry

    lax.fori_loop(3, cells - 3, inner, 0)

    all_y()

    @pl.when(d == 0)
    def _():
        for c in range(7):
            edge = zf[c, 3]
            for i in range(3):
                zf[c, i] = edge

    @pl.when(d > 0)
    def _():
        z_copy(0).wait_recv()

    @pl.when(d == slabs - 1)
    def _():
        for c in range(7):
            edge = zf[c, cells + 2]
            for i in range(3):
                zf[c, cells + 3 + i] = edge

    @pl.when(d < slabs - 1)
    def _():
        z_copy(1).wait_recv()

    def depth_part(level, carry):
        for c, row in enumerate(ROWS[2]):
            part[row, level] = part[row, level] - stencil([zf[c, level + i] for i in range(7)])
        return carry

    lax.fori_loop(0, cells, depth_part, 0)
    ray_order(plan, levels, shifts, order)

    x_row = {row: c for c, row in enumerate(X_ROWS)}

    def advance(row, level, slot):
        value = part[row, level]
        if row in x_row:
            value = value - stencil(
                [xf[x_row[row], slot, pl.ds(PAD - 3 + i, width), :] for i in range(7)]
            )
        return value

    def emit(new, out, height):
        block_of = lax.broadcasted_iota(jnp.int32, (height, 128), 1) // plan.lanes
        for slot in range(most):
            rho, mx, mz, bx, by, bz, en = new(slot)
            dens = 0.5 + softplus(rho)
            inv = 1.0 / dens
            speed = (COS_VIEW * mz + SIN_VIEW * mx) * inv
            source = softplus(en - 0.5 * (bx * bx + by * by + bz * bz)) * inv
            for f, value in enumerate((dens, speed, source)):
                item = 3 * slot + f
                row, block = item // plan.blocks, item % plan.blocks
                for target in range(slabs):
                    shift = ((block - target) * plan.lanes) % 128
                    moved = pltpu.roll(value, shift, 1) if shift else value
                    if block:
                        moved = jnp.where(block_of == block, moved, rows[target, row])
                    rows[target, row] = moved
                    if block == plan.blocks - 1 or item == plan.items - 1:
                        out[target, row] = rows.pop((target, row))

    rows = {}
    cores = 2 if slabs % 2 == 0 else 1

    def peer(step, sign):
        chip, core = d // cores, lax.rem(d, cores)
        far, flip = step // cores, step % cores
        chips = slabs // cores
        return lax.rem(chip + chips + sign * far, chips) * cores + (1 - core if flip else core)

    def depth_copy(step, kind):
        source, target = (rim_pack, rim_held) if kind else (pack, held)
        to = peer(step, 1)
        return pltpu.make_async_remote_copy(
            src_ref=source.at[to],
            dst_ref=target.at[d],
            send_sem=ds_sem.at[step, kind],
            recv_sem=dr_sem.at[step, kind],
            device_id=(t, to),
            device_id_type=MESH,
        )

    def line_copy(source, n, own=False):
        o, group, first, size, at, kind = plan.pieces[source][n]
        start, stop = plan.groups[group]
        if own:
            origin = rim_pack if kind else pack
        else:
            origin = rim_held if kind else held
        return pltpu.make_async_remote_copy(
            src_ref=origin.at[source, pl.ds(start, stop - start), pl.ds(first, size), :],
            dst_ref=recv.at[source, pl.ds(start, stop - start), pl.ds(at, size), :],
            send_sem=ls_sem.at[source, n],
            recv_sem=lr_sem.at[source, n],
            device_id=(lax.rem(t + tiles - o % tiles, tiles), d),
            device_id_type=MESH,
        )

    def rim_copy(source, n, target):
        o, group, first, size, at, _ = plan.pieces[source][n]
        start, stop = plan.groups[group]
        return pltpu.make_async_remote_copy(
            src_ref=rim_pack.at[target, pl.ds(start, stop - start), pl.ds(first, size), :],
            dst_ref=recv.at[source, pl.ds(start, stop - start), pl.ds(at, size), :],
            send_sem=rs_sem.at[n, target],
            recv_sem=lr_sem.at[source, n],
            device_id=(lax.rem(t + tiles - o % tiles, tiles), target),
            device_id_type=MESH,
        )

    def keep(source, n, own):
        _, group, first, size, at, kind = plan.pieces[source][n]
        start, stop = plan.groups[group]
        if own:
            origin = rim_pack if kind else pack
        else:
            origin = rim_held if kind else held
        for row in range(start, stop):
            recv[source, row, at:at + size, :] = origin[source, row, first:first + size, :]

    def forward(slab, kind, own=False):
        for source in range(slabs):

            @pl.when(slab == source)
            def _():
                for stays in (False, True):
                    for n, piece in reversed(list(enumerate(plan.pieces[source]))):
                        if piece[5] == kind and (piece[0] % tiles == 0) == stays:
                            if stays:
                                keep(source, n, own)
                            else:
                                line_copy(source, n, own).start()

    line_rows = (0, 1, 3, 4, 5, 6, 7)

    def core_state(slot):
        level = order[slot]
        out = []
        for row in line_rows:
            value = part[row, level, 3:width - 3, :]
            if row in x_row:
                value = value - stencil(
                    [xf[x_row[row], slot, pl.ds(PAD + i, plan.core), :] for i in range(7)]
                )
            out.append(value)
        return out

    emit(core_state, pack, plan.core)
    for step in range(1, slabs):
        depth_copy(step, 0).start()
    forward(d, 0, own=True)
    for step in range(1, slabs):
        depth_copy(step, 0).wait_recv()
        forward(peer(step, -1), 0)

    x_copy(0, 0).wait_recv()
    x_copy(1, 0).wait_recv()
    low_rows = lax.broadcasted_iota(jnp.int32, (8, 128), 0) < 3

    def rim_state(slot):
        new = [advance(row, order[slot], slot) for row in line_rows]
        return [jnp.where(low_rows, one[:8], one[width - 8:]) for one in new]

    emit(rim_state, rim_pack, 8)
    rims = [
        (source, n)
        for source in range(slabs)
        for n, piece in enumerate(plan.pieces[source])
        if piece[5] == 1
    ]
    for source in range(slabs):

        @pl.when(d == source)
        def _():
            for one, n in reversed(rims):
                if one == source:
                    for target in range(slabs):
                        if target == source and plan.pieces[source][n][0] % tiles == 0:
                            keep(source, n, True)
                        else:
                            rim_copy(source, n, target).start()


    def rest(level, carry):
        slot = order[cells + 3 * plan.positions + level]
        for row in range(8):
            ns[row, level] = advance(row, level, slot)
        return carry

    for span in range(1, spans):
        x_copy(0, span).wait_recv()
        x_copy(1, span).wait_recv()
    lax.fori_loop(0, cells, rest, 0)

    for span in range(spans):
        x_copy(0, span).wait_send()
        x_copy(1, span).wait_send()

    @pl.when(d < slabs - 1)
    def _():
        z_copy(0).wait_send()

    @pl.when(d > 0)
    def _():
        z_copy(1).wait_send()

    for step in range(1, slabs):
        depth_copy(step, 0).wait_send()
    for source in range(slabs):
        for n in range(len(plan.pieces[source])):
            if plan.pieces[source][n][0] % tiles and plan.pieces[source][n][5] == 0:
                line_copy(source, n).wait_send()

        @pl.when(d == source)
        def _():
            for one, n in rims:
                if one == source:
                    for target in range(slabs):
                        if not (target == source and plan.pieces[source][n][0] % tiles == 0):
                            rim_copy(source, n, target).wait_send()

    for source in range(slabs):
        for n in range(len(plan.pieces[source])):
            here = plan.pieces[source][n][0] % tiles == 0
            if plan.pieces[source][n][5] == 1 and here:
                pl.when(d != source)(rim_copy(source, n, source).wait_recv)
            elif plan.pieces[source][n][5] == 1:
                rim_copy(source, n, source).wait_recv()
            elif not here:
                line_copy(source, n).wait_recv()

    lane = lax.broadcasted_iota(jnp.int32, (width, 128), 1)
    within = lax.rem(lane, plan.lanes)
    wanted = lane // plan.lanes == lax.rem(
        lax.broadcasted_iota(jnp.int32, (width, 128), 0), plan.blocks
    )
    for k in range(plan.positions):
        at = cells + 3 * k
        slab, slot, start = order[at], order[at + 1], order[at + 2]
        for f in range(3):
            item = 3 * slot + f
            row, block = item // plan.blocks, lax.rem(item, plan.blocks)
            value = recv[slab, row, pl.ds(start, width), :]
            value = jnp.take_along_axis(value, within + block * plan.lanes, axis=1)
            value = jnp.where(wanted, value, 0.0)
            step = 1
            while step < plan.blocks:
                value = value + pltpu.roll(value, width - step, 0)
                step *= 2
            if f == 0:
                value = value * (-LOG2E * 2.0 / plan.positions)
            elif f == 1:
                value = value * ROOT_LOG2E
            fields[f, k] = value


def ray_kernel(plan, fields, hold, state_out, intensity, out_sem):
    width, blocks, positions = plan.width, plan.blocks, plan.positions
    out_copy = pltpu.make_async_copy(hold, state_out, out_sem)
    out_copy.start()

    groups = W // 8
    for part in range(width // blocks):
        waves = [
            (
                (8 * g + lax.broadcasted_iota(jnp.int32, (8, 128), 0)).astype(F32)
                - 0.5 * (W - 1)
            )
            * (SPACING * ROOT_LOG2E)
            for g in range(groups)
        ]

        def field(f, k):
            return jnp.broadcast_to(fields[f, k, part * blocks:part * blocks + 1, :], (8, 128))

        def step(k, carry):
            seen, total = carry
            thin, speed, source = field(0, k), field(1, k), field(2, k)
            strong = STRENGTH * thin
            seen_next, total_next = [], []
            for g in range(groups):
                gap = waves[g] - speed
                depth = thin + strong * jnp.exp2(-(gap * gap))
                after = seen[g] * jnp.exp2(depth)
                total_next.append(total[g] + source * (seen[g] - after))
                seen_next.append(after)
            return tuple(seen_next), tuple(total_next)

        ones = tuple(jnp.ones((8, 128), F32) for _ in range(groups))
        zeros = tuple(jnp.zeros((8, 128), F32) for _ in range(groups))
        seen, total = lax.fori_loop(0, positions, step, (ones, zeros), unroll=24)
        last = field(2, positions - 1)
        value = jnp.concatenate([total[g] + last * seen[g] for g in range(groups)], axis=0)
        intensity[part * 128:(part + 1) * 128, :] = value.T

    out_copy.wait()


def per_device(plan, density, momentum, magnetic, energy, shifts, levels):
    cells, width, cross = density.shape
    slabs = plan.slabs
    any_spec = pl.BlockSpec(memory_space=pl.ANY)
    vmem = pl.BlockSpec(memory_space=pltpu.VMEM)
    state_shape = (8, cells, width, cross)
    lines_shape = (slabs, plan.packed, plan.rows, 128)
    fields_shape = (3, plan.positions, width, 128)
    spans = len(plan.sends)
    state, fields = pl.pallas_call(
        functools.partial(section_kernel, plan),
        out_shape=(
            pltpu.VMEM(state_shape, F32),
            pltpu.VMEM(fields_shape, F32),
        ),
        in_specs=[pl.BlockSpec(memory_space=pltpu.HBM)] * 6,
        out_specs=(vmem, vmem),
        scratch_shapes=[
            pltpu.SMEM((2 * cells + 3 * plan.positions,), jnp.int32),
            pltpu.VMEM(lines_shape, F32),
            pltpu.SMEM((plan.positions,), jnp.int32),
            pltpu.SMEM((plan.positions,), jnp.int32),
            pltpu.VMEM(state_shape, F32),
            pltpu.VMEM((7, cells, width + 2 * PAD, cross), F32),
            pltpu.VMEM((7, cells, width, 2 * cross), jnp.bfloat16),
            pltpu.VMEM((7, cells + 6, width, cross), F32),
            pltpu.VMEM(state_shape, F32),
            pltpu.VMEM((slabs, plan.packed, plan.core, 128), F32),
            pltpu.VMEM((slabs, plan.packed, 8, 128), F32),
            pltpu.VMEM((slabs, plan.packed, plan.core, 128), F32),
            pltpu.VMEM((slabs, plan.packed, 8, 128), F32),
            pltpu.SemaphoreType.DMA((6,)),
            pltpu.SemaphoreType.DMA((2, spans)),
            pltpu.SemaphoreType.DMA((2, spans)),
            pltpu.SemaphoreType.DMA((2,)),
            pltpu.SemaphoreType.DMA((2,)),
            pltpu.SemaphoreType.DMA((slabs, 2)),
            pltpu.SemaphoreType.DMA((slabs, 2)),
            pltpu.SemaphoreType.DMA((slabs, plan.count)),
            pltpu.SemaphoreType.DMA((slabs, plan.count)),
            pltpu.SemaphoreType.DMA((plan.count, slabs)),
        ],
        compiler_params=pltpu.CompilerParams(
            collective_id=0, has_side_effects=True, vmem_limit_bytes=16 << 20
        ),
        name="section",
    )(*(
        pltpu.with_memory_space_constraint(x, pltpu.HBM)
        for x in (levels, shifts, density, momentum, magnetic, energy)
    ))
    fields = pltpu.with_memory_space_constraint(fields, pltpu.VMEM)
    state = pltpu.with_memory_space_constraint(state, pltpu.VMEM)
    new_state, intensity = pl.pallas_call(
        functools.partial(ray_kernel, plan),
        out_shape=(
            jax.ShapeDtypeStruct(state_shape, F32),
            jax.ShapeDtypeStruct((width * plan.lanes, W), F32),
        ),
        in_specs=[vmem, vmem],
        out_specs=(any_spec, vmem),
        scratch_shapes=[
            pltpu.SemaphoreType.DMA,
        ],
        compiler_params=pltpu.CompilerParams(vmem_limit_bytes=16 << 20),
        name="ray",
    )(fields, state)
    intensity = intensity.reshape(width, plan.lanes, W)
    return new_state, jnp.transpose(intensity, (2, 0, 1))


def solution(mesh):
    tiles, slabs = mesh.shape["tile"], mesh.shape["depth"]

    def body(density, momentum, magnetic, energy, shifts, levels):
        cells, width, cross = density.shape
        plan = Plan(tiles, slabs, cells, width, cross, levels.shape[0], 1)
        return per_device(plan, density, momentum, magnetic, energy, shifts, levels)

    return jax.shard_map(
        body,
        mesh=mesh,
        in_specs=(
            P("depth", "tile", None),
            P(None, "depth", "tile", None),
            P(None, "depth", "tile", None),
            P("depth", "tile", None),
            P(),
            P(),
        ),
        out_specs=(P(None, "depth", "tile", None), P(None, "tile", "depth")),
        check_vma=False,
    )
```
